32 devices in a mesh: tile: 8 (over z, y), rec: 4 (over x, core).
Axes of the slice: x: 2, y: 2, z: 4, core: 2. Of those that a mesh axis runs over, the one named last changes fastest.
Arguments:
- screens: bfloat16 [2, 384, 128, 128], P(None, 'tile', 'rec'), may hold values from -1.796875 to 1.796875
- tile_owner: int32 [2, 2, 1024, 1], replicated, may hold values from 0 to 7; in each aligned block of 128 rows (0 to 127, 128 to 255, ..., all dimensions but the last counted through in order) at most 24 rows name the same one
- tile_slot: int32 [2, 2, 1024], replicated, may hold values from 0 to 47
- commands_init: float32 [4096], P('rec'), may hold values from -1.2 to 1.2
- reconstructor: bfloat16 [32, 16, 128, 128], P('rec', 'tile'), may hold values from -1 to 1
- pattern: int32 [32, 16], P('rec', 'tile'), may hold values from 0 to 31
Outputs:
- lgs_slopes: float32 [2, 32, 128], P(None, 'tile', 'rec')
- science_residual: bfloat16 [2, 992, 128, 128], P(None, 'tile', 'rec')
- commands: float32 [4096], P('rec')
The draws below stay inside these ranges and needn't reach their ends.
Inputs may be any that keep to these rules, and one draw needn't show every extreme that they name: `tile_owner`: within the 128 consecutive entries of one index of tile for one frame and layer, each holder is named at most 24 times; in every frame and layer some such entries name one holder exactly 24 times.
All inputs are finite; a program needn't handle non-finite values.
Results may differ from the reference program's by a relative error of at most 0.011.
Values may be sent and summed in bfloat16 or wider, within the bound.
No kernel may reach another device: no remote copies, remote signals or barrier semaphores. Data moves between devices by JAX's collectives and lax.ppermute only.
A program may use at most 64 MiB of HBM per device.

```python
import math
import jax
import jax.numpy as jnp
import numpy as np
from jax import lax

TILE = 128
SUBPX = 16
SPOT = 32
SUB = 8
PT = 64
NC = 4096
BLOCK = 128
NBR = 32
LAYERS = 2
FRAMES = 2
TILES_DEV = 48
LG_DEV = 4
IT_DEV = 128
NT = 384
NBC = 32
NSC = 992
KB = 16
CAP = 24
N_TILE = 8


def plant(drawn, own_key, least, top_value):
    index_at = [jax.random.randint(jax.random.fold_in(own_key, axis), (), 0, length) for axis, length in enumerate(drawn.shape)]
    widest = drawn.shape.index(max(drawn.shape))
    neighbour = index_at[:widest] + [(index_at[widest] + 1) % drawn.shape[widest]] + index_at[widest + 1:]
    return drawn.at[tuple(index_at)].set(least).at[tuple(neighbour)].set(top_value)


def levels(key, shape, cuts, low, largest):
    gain, own = 1.0, jax.random.fold_in(key, 6)
    for axis_at, parts in cuts:
        heights = jnp.exp(jax.random.uniform(jax.random.fold_in(own, axis_at), (parts,), jnp.float32, low / len(cuts), largest / len(cuts)))
        gain = gain * jnp.repeat(heights, shape[axis_at] // parts).reshape([-1 if axis == axis_at else 1 for axis in range(len(shape))])
    return gain


def routed_block(own_key, own, number, rows, count, top, limit, slope):
    order = jax.random.permutation(own_key, count)
    crowded, common = load_shares(count, rows * top, limit, slope, True), load_shares(count, rows * top, limit, slope, False)
    places = jnp.arange(count)

    def named(sizes, rotation):
        used = int((sizes > 0).sum())
        fixed = max(1, used // 4)
        moved = fixed + (places - fixed + rotation * (used - fixed)) % max(1, count - fixed)
        return jnp.zeros((count,), jnp.int32).at[order[jnp.where(places < fixed, places, moved)]].set(jnp.asarray(sizes, jnp.int32))

    sizes = jnp.where(number % 4 == 0, named(crowded, number // 4), named(common, number - number // 4 - 1))
    mixed = jax.random.permutation(jax.random.fold_in(own, 3), count)
    giver, sink = mixed[0:count // 2 * 2:2], mixed[1:count // 2 * 2:2]
    margin = jnp.minimum(sizes[giver] - 1, limit - sizes[sink]) // 2
    margin = jnp.where((giver == order[0]) | (sink == order[0]) | (sizes[sink] == 0), 0, jnp.maximum(margin, 0))
    moved = jax.random.randint(jax.random.fold_in(own, 4), (count // 2,), 0, 1 << 20) % (margin + 1)
    sizes = sizes.at[giver].add(-moved).at[sink].add(moved)
    items = jnp.searchsorted(jnp.cumsum(sizes), jnp.arange(rows * top), side="right").astype(jnp.int32)
    table = items.reshape(top, rows).T
    table = table[jax.random.permutation(jax.random.fold_in(own, 1), rows)]
    rotation = jax.random.randint(jax.random.fold_in(own, 2), (rows, 1), 0, top)
    return jnp.take_along_axis(table, (jnp.arange(top)[None, :] + rotation) % top, axis=1)


def load_shares(number_of, total, most, lean, full):
    portions = [(1 << 20) // math.isqrt(rank ** lean) + 1 for rank in range(1, number_of + 1)]
    largest = most if full else min(most, max(-(-total // number_of), total * portions[0] // sum(portions)))
    least = 1 if total - largest >= number_of - 1 else 0
    given, rest = [largest] + [least] * (number_of - 1), total - largest - least * (number_of - 1)
    while rest > 0:
        movable = [i for i in range(1, number_of) if given[i] < largest] or [i for i in range(1, number_of) if given[i] < most]
        mass, remaining = sum([portions[i] for i in movable]), rest
        for i in movable:
            addition = min(most - given[i], max(1, remaining * portions[i] // mass), rest)
            given[i] = given[i] + addition
            rest = rest - addition
    return np.array(given)


def scatter_about(stream_key, extent, scale, reach, cuts=(), kind=jnp.bfloat16):
    factor_of = levels(stream_key, extent, cuts, -0.22, 0.18) if cuts else 1.0
    drawn = jax.random.normal(stream_key, extent, jnp.float32) * scale * factor_of
    return jnp.minimum(jnp.maximum(drawn, -reach), reach).astype(kind)


def setup_inputs(seed: int = 0) -> dict:
    splits = jax.random.split(jax.random.key(seed), 7)
    screens = scatter_about(splits[0], (LAYERS, NT, TILE, TILE), 0.3, 1.796875, ((1, 8), (2, 4)))
    tile_owner_keys = jax.random.split(jax.random.fold_in(splits[1], 1), FRAMES * LAYERS * (N_TILE * IT_DEV) // IT_DEV)
    tile_owner_turns = jax.random.permutation(jax.random.fold_in(splits[1], 3), FRAMES * LAYERS * (N_TILE * IT_DEV) // IT_DEV)
    tile_owner = jax.vmap(lambda own, number: routed_block(jax.random.fold_in(splits[1], 2), own, number, IT_DEV, N_TILE, 1, CAP, 2))(tile_owner_keys, tile_owner_turns).reshape((FRAMES, LAYERS, N_TILE * IT_DEV, 1))
    tile_slot = plant(jax.random.randint(splits[2], (FRAMES, LAYERS, N_TILE * IT_DEV), 0, TILES_DEV), jax.random.fold_in(splits[2], 1), 0, TILES_DEV - 1).astype(jnp.int32)
    commands_init = scatter_about(splits[3], (NC,), 0.2, 1.2, ((0, 4),), jnp.float32)
    reconstructor = jnp.clip(jax.random.uniform(splits[4], (NBR, KB, BLOCK, BLOCK), jnp.float32, -1.0, 1.0) * levels(splits[4], (NBR, KB, BLOCK, BLOCK), ((0, 4), (1, 8)), -0.4, 0.0), -1.0, 1.0).astype(jnp.bfloat16)
    pattern = plant(jax.random.randint(splits[5], (NBR, KB), 0, NBC), jax.random.fold_in(splits[5], 1), 0, NBC - 1).astype(jnp.int32)
    return {"screens": screens, "tile_owner": tile_owner, "tile_slot": tile_slot, "commands_init": commands_init, "reconstructor": reconstructor, "pattern": pattern}


loop_gain = 0.5


def influence(tile_px, sub_px, sub_count):
    pixel = jnp.arange(tile_px, dtype=jnp.float32)[:, None] + 0.5
    centre = (jnp.arange(sub_count, dtype=jnp.float32)[None, :] + 0.5) * sub_px
    return jnp.maximum(0.0, 1.0 - jnp.abs(pixel - centre) / sub_px)


def tables(spot_px, sub_px):
    freq = jnp.arange(spot_px, dtype=jnp.int32)[:, None]
    pixel = jnp.arange(sub_px, dtype=jnp.int32)[None, :]
    turns = ((freq * pixel) % spot_px).astype(jnp.float32) * (2.0 * math.pi / spot_px)
    cos_low = lax.optimization_barrier(jnp.cos(turns).astype(jnp.bfloat16))
    sin_low = lax.optimization_barrier(jnp.sin(turns).astype(jnp.bfloat16))
    return cos_low.astype(jnp.float32), sin_low.astype(jnp.float32)


def centred(spot_px):
    index = jnp.arange(spot_px, dtype=jnp.int32)
    return (((index + spot_px // 2) % spot_px) - spot_px // 2).astype(jnp.float32) / spot_px


def rounded(value):
    return lax.optimization_barrier(value.astype(jnp.bfloat16)).astype(jnp.float32)


def spot_slopes(residual):
    item_count, row_px, col_px = residual.shape
    sub_rows = row_px // SUBPX
    sub_cols = col_px // SUBPX
    cos_t, sin_t = tables(SPOT, SUBPX)
    pieces = residual.reshape(item_count, sub_rows, SUBPX, sub_cols, SUBPX)
    real_part = rounded(jnp.cos(pieces))
    imag_part = rounded(jnp.sin(pieces))
    hp = lax.Precision.HIGHEST
    g_re = rounded(jnp.einsum("iaubv,nv->iaubn", real_part, cos_t, precision=hp)
                   + jnp.einsum("iaubv,nv->iaubn", imag_part, sin_t, precision=hp))
    g_im = rounded(jnp.einsum("iaubv,nv->iaubn", imag_part, cos_t, precision=hp)
                   - jnp.einsum("iaubv,nv->iaubn", real_part, sin_t, precision=hp))
    h_re = (jnp.einsum("mu,iaubn->iabmn", cos_t, g_re, precision=hp)
            + jnp.einsum("mu,iaubn->iabmn", sin_t, g_im, precision=hp))
    h_im = (jnp.einsum("mu,iaubn->iabmn", cos_t, g_im, precision=hp)
            - jnp.einsum("mu,iaubn->iabmn", sin_t, g_re, precision=hp))
    spots = h_re * h_re + h_im * h_im
    coords = centred(SPOT)
    totals = jnp.sum(spots, axis=(3, 4))
    slope_x = jnp.sum(spots * coords[None, None, None, None, :], axis=(3, 4)) / totals
    slope_y = jnp.sum(spots * coords[None, None, None, :, None], axis=(3, 4)) / totals
    return jnp.stack([slope_x, slope_y], axis=-1).reshape(item_count, sub_rows * sub_cols * 2)


def reference(screens, tile_owner, tile_slot, commands_init, reconstructor, pattern):
    ids = (tile_owner[..., 0] * TILES_DEV + tile_slot).astype(jnp.int32)
    influence_all = influence(TILE, SUBPX, SUB)
    lgs_places = jnp.arange(NBC, dtype=jnp.int32) % PT
    sci_places = jnp.arange(NSC, dtype=jnp.int32) % PT
    commands = commands_init.astype(jnp.float32)
    slope_frames = []
    science_frames = []
    for frame in range(FRAMES):
        phase = jnp.take(screens[0], ids[frame, 0], axis=0).astype(jnp.float32)
        for layer_idx in range(1, LAYERS):
            phase = phase + jnp.take(screens[layer_idx], ids[frame, layer_idx], axis=0).astype(jnp.float32)
        phase = phase.reshape(N_TILE, IT_DEV, TILE, TILE)
        lgs_phase = phase[:, :LG_DEV].reshape(NBC, TILE, TILE)
        sci_phase = phase[:, LG_DEV:].reshape(NSC, TILE, TILE)
        mirror = commands.reshape(PT, SUB, SUB)
        shapes = jnp.einsum("xa,pab,yb->pxy", influence_all, mirror, influence_all,
                            precision=lax.Precision.HIGHEST)
        sci_res = sci_phase - jnp.take(shapes, sci_places, axis=0)
        lgs_res = lgs_phase - jnp.take(shapes, lgs_places, axis=0)
        science_frames.append(sci_res.astype(jnp.bfloat16))
        slopes = spot_slopes(lgs_res)
        slope_frames.append(slopes)
        slopes_b = slopes.astype(jnp.bfloat16)

        def block_row(inputs):
            blocks, columns = inputs
            chosen = jnp.take(slopes_b, columns, axis=0).astype(jnp.float32)
            return jnp.einsum("bcs,bs->c", blocks.astype(jnp.float32), chosen,
                              precision=lax.Precision.HIGHEST)

        update = lax.map(block_row, (reconstructor, pattern))
        commands = commands + loop_gain * update.reshape(-1)
    return jnp.stack(slope_frames, axis=0), jnp.stack(science_frames, axis=0), commands
```

```python
import functools
import math

import jax
import jax.numpy as jnp
import ml_dtypes
import numpy as np
from jax import lax
from jax.experimental import pallas as pl
from jax.experimental.pallas import tpu as pltpu
from jax.sharding import PartitionSpec as P

SUBPX = 16
SPOT = 32
SUB = 8
PT = 64
LG_DEV = 4
SC_DEV = 124
ITEMS = LG_DEV + SC_DEV
LANES = 128
CMD = SUB * SUB

loop_gain = 0.5


def influence(tile_px, sub_px, sub_count):
    pixel = jnp.arange(tile_px, dtype=jnp.float32)[:, None] + 0.5
    centre = (jnp.arange(sub_count, dtype=jnp.float32)[None, :] + 0.5) * sub_px
    return jnp.maximum(0.0, 1.0 - jnp.abs(pixel - centre) / sub_px)


def tables(spot_px, sub_px):
    freq = jnp.arange(spot_px, dtype=jnp.int32)[:, None]
    pixel = jnp.arange(sub_px, dtype=jnp.int32)[None, :]
    turns = (freq * pixel % spot_px).astype(jnp.float32) * (2.0 * math.pi / spot_px)
    return (jnp.cos(turns).astype(jnp.bfloat16), jnp.sin(turns).astype(jnp.bfloat16))


def centred(spot_px):
    index = jnp.arange(spot_px, dtype=jnp.int32)
    return ((index + spot_px // 2) % spot_px - spot_px // 2).astype(jnp.float32) / spot_px


def along_pixels(values, table):
    return jnp.einsum("iaubv,nv->iaubn", values, table, preferred_element_type=jnp.float32)


def along_rows(table, values):
    return jnp.einsum("mu,iaubn->iabmn", table, values, preferred_element_type=jnp.float32)


def spot_slopes(residual):
    item_count, row_px, col_px = residual.shape
    sub_rows = row_px // SUBPX
    sub_cols = col_px // SUBPX
    cos_t, sin_t = tables(SPOT, SUBPX)
    pieces = residual.reshape(item_count, sub_rows, SUBPX, sub_cols, SUBPX)
    real_part = jnp.cos(pieces).astype(jnp.bfloat16)
    imag_part = jnp.sin(pieces).astype(jnp.bfloat16)
    g_re = (along_pixels(real_part, cos_t) + along_pixels(imag_part, sin_t)).astype(jnp.bfloat16)
    g_im = (along_pixels(imag_part, cos_t) - along_pixels(real_part, sin_t)).astype(jnp.bfloat16)
    h_re = along_rows(cos_t, g_re) + along_rows(sin_t, g_im)
    h_im = along_rows(cos_t, g_im) - along_rows(sin_t, g_re)
    spots = h_re * h_re + h_im * h_im
    coords = centred(SPOT)
    totals = jnp.sum(spots, axis=(3, 4))
    slope_x = jnp.sum(spots * coords[None, None, None, None, :], axis=(3, 4)) / totals
    slope_y = jnp.sum(spots * coords[None, None, None, :, None], axis=(3, 4)) / totals
    return jnp.stack([slope_x, slope_y], axis=-1).reshape(item_count, sub_rows * sub_cols * 2)


def pack_tiles(screens, owners, slots, pairs, my_tile, capacity):
    packed = []
    places = jnp.arange(capacity, dtype=jnp.int32)
    for frame, layer_idx in pairs:
        owner_rows = owners[frame, layer_idx]
        slot_rows = slots[frame, layer_idx]
        mine = owner_rows == my_tile
        order = jnp.cumsum(mine.astype(jnp.int32), axis=1) - 1
        picked = mine[:, None, :] & (order[:, None, :] == places[None, :, None])
        wanted = jnp.sum(jnp.where(picked, slot_rows[:, None, :], 0), axis=2)
        packed.append(jnp.take(screens[layer_idx], wanted, axis=0))
    return jnp.stack(packed, axis=1)


def unpack_tiles(received, owners, pairs, my_tile, capacity):
    results = []
    item_count = owners.shape[3]
    later = jnp.arange(item_count, dtype=jnp.int32)
    earlier_mask = later[None, :] < later[:, None]
    for position in range(len(pairs)):
        frame, layer_idx = pairs[position]
        mine = lax.dynamic_index_in_dim(owners[frame, layer_idx], my_tile, 0, keepdims=False)
        same_owner = mine[:, None] == mine[None, :]
        order = jnp.sum((same_owner & earlier_mask).astype(jnp.int32), axis=1)
        flat_index = mine * capacity + order
        layer_tiles = received[:, position].reshape(-1, received.shape[3], received.shape[4])
        results.append(jnp.take(layer_tiles, flat_index, axis=0).astype(jnp.float32))
    return results


def by_request(screens, tile_owner, tile_slot, commands_init, reconstructor, pattern):
    layer_total, tiles_here, slab_rows, tile_px = screens.shape
    frame_total = tile_owner.shape[0]
    tile_count = lax.axis_size("tile")
    rec_count = lax.axis_size("rec")
    my_tile = lax.axis_index("tile")
    my_rec = lax.axis_index("rec")
    capacity = max(2, 3 * ITEMS // (2 * tile_count))
    owners = tile_owner[..., 0].reshape(frame_total, layer_total, tile_count, ITEMS)
    slots = tile_slot.reshape(frame_total, layer_total, tile_count, ITEMS)
    influence_all = influence(tile_px, SUBPX, SUB)
    influence_rows = lax.dynamic_slice_in_dim(influence_all, my_rec * slab_rows, slab_rows, 0)
    lgs_places = (my_tile * LG_DEV + jnp.arange(LG_DEV, dtype=jnp.int32)) % PT
    sci_places = (my_tile * SC_DEV + jnp.arange(SC_DEV, dtype=jnp.int32)) % PT
    item_places = jnp.concatenate([lgs_places, sci_places])
    state = commands_init
    slope_frames = []
    science_frames = []
    for frame in range(frame_total):
        pairs = [(frame, layer_idx) for layer_idx in range(layer_total)]
        sending = pack_tiles(screens, owners, slots, pairs, my_tile, capacity)
        received = lax.all_to_all(sending, "tile", split_axis=0, concat_axis=0, tiled=True)
        pieces = unpack_tiles(received, owners, pairs, my_tile, capacity)
        phase = functools.reduce(jnp.add, pieces)
        full_commands = lax.all_gather(state, "rec", axis=0, tiled=True)
        mirror = full_commands.reshape(PT, SUB, SUB)
        chosen = jnp.take(mirror, item_places, axis=0)
        shapes = jnp.einsum(
            "xa,iab,yb->ixy", influence_rows, chosen, influence_all, precision=lax.Precision.HIGHEST
        )
        residual = phase - shapes
        science_frames.append(residual[LG_DEV:].astype(jnp.bfloat16))
        slopes = spot_slopes(residual[:LG_DEV])
        slope_frames.append(slopes)
        slopes_b = slopes.astype(jnp.bfloat16)
        everyone = lax.all_gather(slopes_b[None], ("tile", "rec"), axis=0, tiled=True)
        everyone = everyone.reshape(tile_count, rec_count, LG_DEV, -1).transpose(0, 2, 1, 3)
        everyone = everyone.reshape(tile_count * LG_DEV, -1)
        needed = jnp.take(everyone, pattern, axis=0)
        partial_rows = jnp.einsum(
            "ibcs,ibs->ic", reconstructor, needed, preferred_element_type=jnp.float32
        ).reshape(-1)
        state = state + loop_gain * lax.psum(partial_rows, "tile")
    return (jnp.stack(slope_frames, axis=0), jnp.stack(science_frames, axis=0), state)


def vmem():
    return pl.BlockSpec(memory_space=pltpu.VMEM)


def smem():
    return pl.BlockSpec(memory_space=pltpu.SMEM)


def constant_tables(slab_rows):
    f32, bf16 = np.float32, ml_dtypes.bfloat16
    turns = (np.arange(SPOT)[:, None] * np.arange(SUBPX)[None, :] % SPOT).astype(f32)
    turns = turns * f32(2.0 * math.pi / SPOT)
    cos_t, sin_t = np.cos(turns).astype(bf16).astype(f32), np.sin(turns).astype(bf16).astype(f32)
    cols = LANES // SUBPX
    eye_c = np.eye(cols, dtype=f32)
    cos_v, sin_v = np.kron(eye_c, cos_t.T), np.kron(eye_c, sin_t.T)
    along_v = np.block([[cos_v, -sin_v], [sin_v, cos_v]])
    rows = LG_DEV * slab_rows // SUBPX
    eye_r = np.eye(rows, dtype=f32)
    cos_u, sin_u = np.kron(eye_r, cos_t), np.kron(eye_r, sin_t)
    along_u = np.block([[cos_u, sin_u], [-sin_u, cos_u]])
    index = np.arange(SPOT)
    coord = (((index + SPOT // 2) % SPOT) - SPOT // 2).astype(f32) / SPOT
    groups = LANES // (2 * cols)
    total_n = np.zeros((cols, SPOT, groups, cols, 2), f32)
    coord_n = np.zeros((cols, SPOT, groups, cols, 2), f32)
    for b in range(cols):
        total_n[b, :, :, b, :] = 1.0
        coord_n[b, :, :, b, 0] = coord[:, None]
    over_n = np.concatenate([t.reshape(cols * SPOT, LANES) for t in (total_n, coord_n)], axis=1)
    sub_rows = slab_rows // SUBPX
    total_m = np.zeros((sub_rows, LG_DEV, LG_DEV, sub_rows, SPOT), f32)
    coord_m = np.zeros((sub_rows, LG_DEV, LG_DEV, sub_rows, SPOT), f32)
    for a in range(sub_rows):
        for i in range(LG_DEV):
            total_m[a, i, i, a, :] = 1.0
            coord_m[a, i, i, a, :] = coord
    over_m = np.concatenate([t.reshape(rows, rows * SPOT) for t in (total_m, coord_m)], axis=0)
    pixel = np.arange(LANES, dtype=f32)[:, None] + f32(0.5)
    centre = (np.arange(SUB, dtype=f32)[None, :] + f32(0.5)) * SUBPX
    infl = np.maximum(f32(0.0), f32(1.0) - np.abs(pixel - centre) / f32(SUBPX))
    per_row = LANES // CMD
    spread = np.tile(infl.T, (per_row * SUB, 1))
    keep = np.kron(np.eye(per_row * SUB, dtype=f32), np.ones((1, SUB), f32))
    return dict(
        along_v=along_v.astype(bf16),
        along_u=along_u.astype(bf16),
        over_n=over_n.astype(bf16),
        over_m=over_m.astype(bf16),
        spread=spread,
        keep=keep,
    )


def split_dot(exact, wide, left):
    high = wide.astype(jnp.bfloat16)
    low = (wide - high.astype(jnp.float32)).astype(jnp.bfloat16)
    dot = functools.partial(jnp.dot, preferred_element_type=jnp.float32)
    if left:
        return dot(exact, high) + dot(exact, low)
    return dot(high, exact) + dot(low, exact)


def sincos(x):
    turns = jnp.floor(x * np.float32(2.0 / math.pi) + 0.5)
    r = x - turns * np.float32(1.5703125)
    r = r - turns * np.float32(4.837512969970703125e-4)
    r = r - turns * np.float32(7.54978995489188216e-8)
    z = r * r
    s = ((np.float32(-1.9515295891e-4) * z + np.float32(8.3321608736e-3)) * z - np.float32(1.6666654611e-1)) * z * r + r
    c = ((np.float32(2.443315711809948e-5) * z - np.float32(1.388731625493765e-3)) * z + np.float32(4.166664568298827e-2)) * z * z - np.float32(0.5) * z + 1.0
    q = turns.astype(jnp.int32) & 3
    odd = (q & 1) == 1
    sine = jnp.where(odd, c, s)
    cosine = jnp.where(odd, s, c)
    sine = jnp.where(q >= 2, -sine, sine)
    cosine = jnp.where((q == 1) | (q == 2), -cosine, cosine)
    return sine, cosine


def row_weights(my_rec, slab_rows):
    groups = []
    for k in range(slab_rows // 8):
        g = my_rec * (slab_rows // 8) + k
        first = (g + 1) // 2 - 1
        x = (g * 8 + lax.broadcasted_iota(jnp.int32, (8, LANES), 0)).astype(jnp.float32) + 0.5
        pair = []
        for a in (first, first + 1):
            inside = (a >= 0) & (a < SUB)
            centre = (a.astype(jnp.float32) + 0.5) * SUBPX
            w = jnp.maximum(0.0, 1.0 - jnp.abs(x - centre) / SUBPX)
            pair.append((jnp.clip(a, 0, SUB - 1), jnp.where(inside, w, 0.0)))
        groups.append(pair)
    return groups


def column_profiles(c_rows, keep, spread):
    picked = [jnp.broadcast_to(c_rows[i : i + 1], keep.shape) * keep for i in range(c_rows.shape[0])]
    return jnp.dot(
        jnp.concatenate(picked, axis=0), spread, preferred_element_type=jnp.float32, precision=lax.Precision.HIGHEST
    )


def pick_kernel(slots, screens, out):
    tile_count, layers = out.shape[0], out.shape[1]
    total = slots.shape[0] // layers
    for t in range(tile_count):
        for l in range(layers):
            for i in range(LG_DEV):
                out[t, l, i] = screens[l, slots[l * total + t * ITEMS + i]]


def slope_kernel(first, owners, received, c_base, *refs):
    if first:
        along_v, along_u, over_n, over_m, keep, spread, payload, slopes, prof = refs
    else:
        updates, along_v, along_u, over_n, over_m, keep, spread, payload, slopes, c_out, prof = refs
    slab_rows = received.shape[3]
    my_tile, my_rec = lax.axis_index("tile"), lax.axis_index("rec")
    per_row = LANES // CMD
    need = LG_DEV // per_row
    row_count = PT // per_row
    base = lax.rem(my_tile * need, row_count)
    if first:
        c_rows = c_base[pl.ds(base, need), :]
    else:
        c_new = c_base[...] + loop_gain * jnp.sum(updates[...], axis=0).reshape(c_base.shape)
        c_out[...] = c_new
        c_rows = c_out[pl.ds(base, need), :]
    prof[...] = column_profiles(c_rows, keep[...], spread[...])
    weights = row_weights(my_rec, slab_rows)
    layers = received.shape[1]
    total = owners.shape[0] // layers
    rows = []
    for i in range(LG_DEV):
        phase = None
        for l in range(layers):
            tile = received[owners[l * total + my_tile * ITEMS + i], l, i].astype(jnp.float32)
            phase = tile if phase is None else phase + tile
        for k, ((a0, w0), (a1, w1)) in enumerate(weights):
            shape = w0 * prof[pl.ds(i * SUB + a0, 1), :] + w1 * prof[pl.ds(i * SUB + a1, 1), :]
            rows.append(phase[k * 8 : (k + 1) * 8] - shape)
    residual = jnp.concatenate(rows, axis=0)
    sine, cosine = sincos(residual)
    e = jnp.concatenate([cosine.astype(jnp.bfloat16), sine.astype(jnp.bfloat16)], axis=1)
    g = jnp.dot(e, along_v[...], preferred_element_type=jnp.float32).astype(jnp.bfloat16)
    half = g.shape[1] // 2
    g = jnp.concatenate([g[:, :half], g[:, half:]], axis=0)
    h = jnp.dot(along_u[...], g, preferred_element_type=jnp.float32)
    n = h.shape[0] // 2
    h_re, h_im = h[:n], h[n:]
    spot = h_re * h_re + h_im * h_im
    sums = split_dot(over_m[...], split_dot(over_n[...], spot, False), True)
    m = sums.shape[0] // 2
    lane = lax.broadcasted_iota(jnp.int32, (m, LANES), 1)
    row = lax.broadcasted_iota(jnp.int32, (m, LANES), 0)
    top = sums[:m, LANES:] + jnp.where(lane % 2 == 1, sums[m:, :LANES], 0.0)
    ratio = top / sums[:m, :LANES]
    sub_rows = slab_rows // SUBPX
    ratio = jnp.where(lane // SUBPX == my_rec * sub_rows + row // LG_DEV, ratio, 0.0)
    own = ratio[:LG_DEV]
    for a in range(1, sub_rows):
        own = own + ratio[a * LG_DEV : (a + 1) * LG_DEV]
    slopes[...] = own
    payload[...] = jnp.broadcast_to(own.astype(jnp.bfloat16).astype(jnp.float32)[None], payload.shape)


def update_kernel(pattern, received, blocks, out, slopes):
    slopes[...] = jnp.sum(received[...], axis=1).reshape(slopes.shape)
    rows = []
    for i in range(blocks.shape[0]):
        total = None
        for b in range(blocks.shape[1]):
            vector = slopes[pl.ds(pattern[i, b], 1), :].astype(jnp.bfloat16)
            part = lax.dot_general(
                vector, blocks[i, b], (((1,), (1,)), ((), ())), preferred_element_type=jnp.float32
            )
            total = part if total is None else total + part
        rows.append(total)
    out[...] = jnp.broadcast_to(jnp.concatenate(rows, axis=0)[None], out.shape)


def science_kernel(first_ids, second_ids, c_first, c_second, keep, spread, *refs):
    *pieces, out, store, prof, sem = refs
    slab_rows = out.shape[2]
    my_tile, my_rec = lax.axis_index("tile"), lax.axis_index("rec")
    copies, at = [], 0
    for i, piece in enumerate(pieces):
        copies.append(pltpu.make_async_copy(piece, store.at[pl.ds(at, piece.shape[0])], sem.at[i]))
        at += piece.shape[0]
    for copy in copies:
        copy.start()
    weights = row_weights(my_rec, slab_rows)
    profile_rows = PT * SUB
    for f, c in enumerate((c_first, c_second)):
        prof[pl.ds(f * profile_rows, profile_rows)] = column_profiles(c[...], keep[...], spread[...])
    for copy in copies:
        copy.wait()
    start = lax.rem(my_tile * SC_DEV, PT)
    for f, ids in enumerate((first_ids, second_ids)):

        @pl.loop(0, PT)
        def _(q):
            p = lax.rem(start + q, PT)
            row = f * profile_rows + p * SUB
            shapes = [
                w0 * prof[pl.ds(row + a0, 1), :] + w1 * prof[pl.ds(row + a1, 1), :]
                for (a0, w0), (a1, w1) in weights
            ]
            shape = jnp.concatenate(shapes, axis=0)

            def item(k):
                phase = store[ids[k]].astype(jnp.float32) + store[ids[SC_DEV + k]].astype(jnp.float32)
                out[f, k] = (phase - shape).astype(jnp.bfloat16)

            item(q)

            @pl.when(q + PT < SC_DEV)
            def _():
                item(q + PT)


def by_ring(screens, tile_owner, tile_slot, commands_init, reconstructor, pattern):
    layers, tiles_here, slab_rows, tile_px = screens.shape
    frames = tile_owner.shape[0]
    n = lax.axis_size("tile")
    rec_count = lax.axis_size("rec")
    everyone = n * rec_count
    my_tile, my_rec = lax.axis_index("tile"), lax.axis_index("rec")
    table = {k: jnp.asarray(v) for k, v in constant_tables(slab_rows).items()}
    block_rows = reconstructor.shape[0]
    f32 = jnp.float32

    ring = list(range(0, n, 2)) + list(range(n - 1, 0, -2))
    forward = [(ring[k], ring[(k + 1) % n]) for k in range(n)]
    backward = [(b, a) for a, b in forward]

    def place(tile):
        return jnp.where(tile % 2 == 0, tile // 2, n - 1 - tile // 2)

    slots = tile_slot.reshape(frames, layers * n * ITEMS)
    owners = tile_owner.reshape(frames, layers * n * ITEMS)

    def guide_tiles(frame):
        picked = pl.pallas_call(
            pick_kernel,
            out_shape=jax.ShapeDtypeStruct((n, layers, LG_DEV, slab_rows, tile_px), screens.dtype),
            in_specs=[smem(), vmem()],
            out_specs=vmem(),
        )(slots[frame], screens)
        return lax.all_to_all(picked, "tile", split_axis=0, concat_axis=0, tiled=True)

    def slopes_of(frame, received, c_base, updates):
        first = updates is None
        outs = [
            jax.ShapeDtypeStruct((everyone, LG_DEV, LANES), f32),
            jax.ShapeDtypeStruct((LG_DEV, LANES), f32),
        ]
        if not first:
            outs.append(jax.ShapeDtypeStruct(c_base.shape, f32))
        args = [received, c_base] + ([] if first else [updates])
        args += [table[k] for k in ("along_v", "along_u", "over_n", "over_m", "keep", "spread")]
        result = pl.pallas_call(
            functools.partial(slope_kernel, first),
            out_shape=outs,
            in_specs=[smem()] + [vmem()] * len(args),
            out_specs=[vmem()] * len(outs),
            scratch_shapes=[pltpu.VMEM((LG_DEV * SUB, LANES), f32)],
        )(owners[frame], *args)
        payload, own = result[0], result[1]
        own = lax.dynamic_slice_in_dim(own, my_rec * (slab_rows // SUBPX * SUB * 2), slab_rows // SUBPX * SUB * 2, 1)
        return payload, own, (c_base if first else result[2])

    def updates_of(payload, copies):
        received = lax.all_to_all(payload, ("tile", "rec"), split_axis=0, concat_axis=0, tiled=True)
        received = received.reshape(n, rec_count, LG_DEV, LANES)
        return pl.pallas_call(
            update_kernel,
            out_shape=jax.ShapeDtypeStruct((copies, block_rows, LANES), f32),
            in_specs=[smem(), vmem(), vmem()],
            out_specs=vmem(),
            scratch_shapes=[pltpu.VMEM((n * LG_DEV, LANES), f32)],
        )(pattern, received, reconstructor)

    received = [guide_tiles(f) for f in range(frames)]
    c0 = lax.all_gather(commands_init.reshape(-1, LANES), "rec", axis=0, tiled=True)
    ahead, behind = [screens], [screens]
    for _ in range(n // 2 - 1):
        ahead.append(lax.ppermute(ahead[-1], "tile", forward))
        behind.append(lax.ppermute(behind[-1], "tile", backward))
    far_first = lax.ppermute(ahead[-1][0], "tile", forward)
    far_second = lax.ppermute(behind[-1][1], "tile", backward)

    payload, slopes_first, _ = slopes_of(0, received[0], c0, None)
    updates = updates_of(payload, everyone)
    updates = lax.all_to_all(updates, ("tile", "rec"), split_axis=0, concat_axis=0, tiled=True)
    updates = updates.reshape(n, rec_count, block_rows, LANES)
    payload, slopes_second, c1 = slopes_of(1, received[1], c0, updates)
    updates = updates_of(payload, n)
    updates = lax.all_to_all(updates, "tile", split_axis=0, concat_axis=0, tiled=True)
    mine = lax.dynamic_slice_in_dim(c1, my_rec * block_rows, block_rows, 0)
    c2 = mine + loop_gain * jnp.sum(updates, axis=0)

    pieces = [x.reshape(layers * tiles_here, slab_rows, tile_px) for x in ahead]
    pieces += [far_first, far_second]
    pieces += [x.reshape(layers * tiles_here, slab_rows, tile_px) for x in reversed(behind[1:])]
    back = (place(my_tile) - place(tile_owner[..., 0].reshape(frames, layers, n, ITEMS))) % n
    layer = jnp.arange(layers, dtype=jnp.int32)[None, :, None, None]
    where = (back * layers + layer) * tiles_here + tile_slot.reshape(frames, layers, n, ITEMS)
    where = lax.dynamic_index_in_dim(where, my_tile, 2, keepdims=False)[:, :, LG_DEV:]
    where = where.reshape(frames, layers * SC_DEV)
    science = pl.pallas_call(
        science_kernel,
        out_shape=jax.ShapeDtypeStruct((frames, SC_DEV, slab_rows, tile_px), jnp.bfloat16),
        in_specs=[smem()] * 2 + [vmem()] * 4 + [pl.BlockSpec(memory_space=pl.ANY)] * len(pieces),
        out_specs=vmem(),
        scratch_shapes=[
            pltpu.VMEM((n * layers * tiles_here, slab_rows, tile_px), screens.dtype),
            pltpu.VMEM((frames * PT * SUB, LANES), f32),
            pltpu.SemaphoreType.DMA((len(pieces),)),
        ],
        compiler_params=pltpu.CompilerParams(vmem_limit_bytes=32 << 20),
    )(where[0], where[1], c0, c1, table["keep"], table["spread"], *pieces)
    return jnp.stack([slopes_first, slopes_second], axis=0), science, c2.reshape(-1)


def per_device(screens, tile_owner, *rest):
    layers, tiles_here, _, _ = screens.shape
    frames, n = tile_owner.shape[0], lax.axis_size("tile")
    capacity = max(2, 3 * ITEMS // (2 * n))
    few = tiles_here <= frames * capacity and n % 2 == 0 and frames == 2 and layers == 2
    return (by_ring if few else by_request)(screens, tile_owner, *rest)


def solution(mesh):
    placed = (
        P(None, "tile", "rec", None),
        P(),
        P(),
        P("rec"),
        P("rec", "tile", None, None),
        P("rec", "tile"),
    )
    return jax.shard_map(
        per_device,
        mesh=mesh,
        in_specs=placed,
        out_specs=(P(None, "tile", "rec"), P(None, "tile", "rec", None), P("rec")),
        check_vma=False,
    )
```

```python
import functools
import math

import jax
import jax.numpy as jnp
import ml_dtypes
import numpy as np
from jax import lax
from jax.experimental import pallas as pl
from jax.experimental.pallas import tpu as pltpu
from jax.sharding import PartitionSpec as P

SUBPX = 16
SPOT = 32
SUB = 8
PT = 64
LG_DEV = 4
SC_DEV = 124
ITEMS = LG_DEV + SC_DEV
LANES = 128
CMD = SUB * SUB

loop_gain = 0.5


def influence(tile_px, sub_px, sub_count):
    pixel = jnp.arange(tile_px, dtype=jnp.float32)[:, None] + 0.5
    centre = (jnp.arange(sub_count, dtype=jnp.float32)[None, :] + 0.5) * sub_px
    return jnp.maximum(0.0, 1.0 - jnp.abs(pixel - centre) / sub_px)


def tables(spot_px, sub_px):
    freq = jnp.arange(spot_px, dtype=jnp.int32)[:, None]
    pixel = jnp.arange(sub_px, dtype=jnp.int32)[None, :]
    turns = (freq * pixel % spot_px).astype(jnp.float32) * (2.0 * math.pi / spot_px)
    return (jnp.cos(turns).astype(jnp.bfloat16), jnp.sin(turns).astype(jnp.bfloat16))


def centred(spot_px):
    index = jnp.arange(spot_px, dtype=jnp.int32)
    return ((index + spot_px // 2) % spot_px - spot_px // 2).astype(jnp.float32) / spot_px


def along_pixels(values, table):
    return jnp.einsum("iaubv,nv->iaubn", values, table, preferred_element_type=jnp.float32)


def along_rows(table, values):
    return jnp.einsum("mu,iaubn->iabmn", table, values, preferred_element_type=jnp.float32)


def spot_slopes(residual):
    item_count, row_px, col_px = residual.shape
    sub_rows = row_px // SUBPX
    sub_cols = col_px // SUBPX
    cos_t, sin_t = tables(SPOT, SUBPX)
    pieces = residual.reshape(item_count, sub_rows, SUBPX, sub_cols, SUBPX)
    real_part = jnp.cos(pieces).astype(jnp.bfloat16)
    imag_part = jnp.sin(pieces).astype(jnp.bfloat16)
    g_re = (along_pixels(real_part, cos_t) + along_pixels(imag_part, sin_t)).astype(jnp.bfloat16)
    g_im = (along_pixels(imag_part, cos_t) - along_pixels(real_part, sin_t)).astype(jnp.bfloat16)
    h_re = along_rows(cos_t, g_re) + along_rows(sin_t, g_im)
    h_im = along_rows(cos_t, g_im) - along_rows(sin_t, g_re)
    spots = h_re * h_re + h_im * h_im
    coords = centred(SPOT)
    totals = jnp.sum(spots, axis=(3, 4))
    slope_x = jnp.sum(spots * coords[None, None, None, None, :], axis=(3, 4)) / totals
    slope_y = jnp.sum(spots * coords[None, None, None, :, None], axis=(3, 4)) / totals
    return jnp.stack([slope_x, slope_y], axis=-1).reshape(item_count, sub_rows * sub_cols * 2)


def pack_tiles(screens, owners, slots, pairs, my_tile, capacity):
    packed = []
    places = jnp.arange(capacity, dtype=jnp.int32)
    for frame, layer_idx in pairs:
        owner_rows = owners[frame, layer_idx]
        slot_rows = slots[frame, layer_idx]
        mine = owner_rows == my_tile
        order = jnp.cumsum(mine.astype(jnp.int32), axis=1) - 1
        picked = mine[:, None, :] & (order[:, None, :] == places[None, :, None])
        wanted = jnp.sum(jnp.where(picked, slot_rows[:, None, :], 0), axis=2)
        packed.append(jnp.take(screens[layer_idx], wanted, axis=0))
    return jnp.stack(packed, axis=1)


def unpack_tiles(received, owners, pairs, my_tile, capacity):
    results = []
    item_count = owners.shape[3]
    later = jnp.arange(item_count, dtype=jnp.int32)
    earlier_mask = later[None, :] < later[:, None]
    for position in range(len(pairs)):
        frame, layer_idx = pairs[position]
        mine = lax.dynamic_index_in_dim(owners[frame, layer_idx], my_tile, 0, keepdims=False)
        same_owner = mine[:, None] == mine[None, :]
        order = jnp.sum((same_owner & earlier_mask).astype(jnp.int32), axis=1)
        flat_index = mine * capacity + order
        layer_tiles = received[:, position].reshape(-1, received.shape[3], received.shape[4])
        results.append(jnp.take(layer_tiles, flat_index, axis=0).astype(jnp.float32))
    return results


def by_request(screens, tile_owner, tile_slot, commands_init, reconstructor, pattern):
    layer_total, tiles_here, slab_rows, tile_px = screens.shape
    frame_total = tile_owner.shape[0]
    tile_count = lax.axis_size("tile")
    rec_count = lax.axis_size("rec")
    my_tile = lax.axis_index("tile")
    my_rec = lax.axis_index("rec")
    capacity = max(2, 3 * ITEMS // (2 * tile_count))
    owners = tile_owner[..., 0].reshape(frame_total, layer_total, tile_count, ITEMS)
    slots = tile_slot.reshape(frame_total, layer_total, tile_count, ITEMS)
    influence_all = influence(tile_px, SUBPX, SUB)
    influence_rows = lax.dynamic_slice_in_dim(influence_all, my_rec * slab_rows, slab_rows, 0)
    lgs_places = (my_tile * LG_DEV + jnp.arange(LG_DEV, dtype=jnp.int32)) % PT
    sci_places = (my_tile * SC_DEV + jnp.arange(SC_DEV, dtype=jnp.int32)) % PT
    item_places = jnp.concatenate([lgs_places, sci_places])
    state = commands_init
    slope_frames = []
    science_frames = []
    for frame in range(frame_total):
        pairs = [(frame, layer_idx) for layer_idx in range(layer_total)]
        sending = pack_tiles(screens, owners, slots, pairs, my_tile, capacity)
        received = lax.all_to_all(sending, "tile", split_axis=0, concat_axis=0, tiled=True)
        pieces = unpack_tiles(received, owners, pairs, my_tile, capacity)
        phase = functools.reduce(jnp.add, pieces)
        full_commands = lax.all_gather(state, "rec", axis=0, tiled=True)
        mirror = full_commands.reshape(PT, SUB, SUB)
        chosen = jnp.take(mirror, item_places, axis=0)
        shapes = jnp.einsum(
            "xa,iab,yb->ixy", influence_rows, chosen, influence_all, precision=lax.Precision.HIGHEST
        )
        residual = phase - shapes
        science_frames.append(residual[LG_DEV:].astype(jnp.bfloat16))
        slopes = spot_slopes(residual[:LG_DEV])
        slope_frames.append(slopes)
        slopes_b = slopes.astype(jnp.bfloat16)
        everyone = lax.all_gather(slopes_b[None], ("tile", "rec"), axis=0, tiled=True)
        everyone = everyone.reshape(tile_count, rec_count, LG_DEV, -1).transpose(0, 2, 1, 3)
        everyone = everyone.reshape(tile_count * LG_DEV, -1)
        needed = jnp.take(everyone, pattern, axis=0)
        partial_rows = jnp.einsum(
            "ibcs,ibs->ic", reconstructor, needed, preferred_element_type=jnp.float32
        ).reshape(-1)
        state = state + loop_gain * lax.psum(partial_rows, "tile")
    return (jnp.stack(slope_frames, axis=0), jnp.stack(science_frames, axis=0), state)


def microseconds(t):
    return pl.CostEstimate(flops=0, bytes_accessed=int(t * 3.69e6), transcendentals=0)


def vmem():
    return pl.BlockSpec(memory_space=pltpu.VMEM)


def smem():
    return pl.BlockSpec(memory_space=pltpu.SMEM)


def constant_tables(slab_rows):
    f32, bf16 = np.float32, ml_dtypes.bfloat16
    turns = (np.arange(SPOT)[:, None] * np.arange(SUBPX)[None, :] % SPOT).astype(f32)
    turns = turns * f32(2.0 * math.pi / SPOT)
    cos_t, sin_t = np.cos(turns).astype(bf16).astype(f32), np.sin(turns).astype(bf16).astype(f32)
    cols = LANES // SUBPX
    eye_c = np.eye(cols, dtype=f32)
    cos_v, sin_v = np.kron(eye_c, cos_t.T), np.kron(eye_c, sin_t.T)
    along_v = np.block([[cos_v, -sin_v], [sin_v, cos_v]])
    rows = LG_DEV * slab_rows // SUBPX
    eye_r = np.eye(rows, dtype=f32)
    cos_u, sin_u = np.kron(eye_r, cos_t), np.kron(eye_r, sin_t)
    along_u = np.block([[cos_u, sin_u], [-sin_u, cos_u]])
    index = np.arange(SPOT)
    coord = (((index + SPOT // 2) % SPOT) - SPOT // 2).astype(f32) / SPOT
    groups = LANES // (2 * cols)
    total_n = np.zeros((cols, SPOT, groups, cols, 2), f32)
    coord_n = np.zeros((cols, SPOT, groups, cols, 2), f32)
    for b in range(cols):
        total_n[b, :, :, b, :] = 1.0
        coord_n[b, :, :, b, 0] = coord[:, None]
    over_n = np.concatenate([t.reshape(cols * SPOT, LANES) for t in (total_n, coord_n)], axis=1)
    sub_rows = slab_rows // SUBPX
    total_m = np.zeros((sub_rows, LG_DEV, LG_DEV, sub_rows, SPOT), f32)
    coord_m = np.zeros((sub_rows, LG_DEV, LG_DEV, sub_rows, SPOT), f32)
    for a in range(sub_rows):
        for i in range(LG_DEV):
            total_m[a, i, i, a, :] = 1.0
            coord_m[a, i, i, a, :] = coord
    over_m = np.concatenate([t.reshape(rows, rows * SPOT) for t in (total_m, coord_m)], axis=0)
    pixel = np.arange(LANES, dtype=f32)[:, None] + f32(0.5)
    centre = (np.arange(SUB, dtype=f32)[None, :] + f32(0.5)) * SUBPX
    infl = np.maximum(f32(0.0), f32(1.0) - np.abs(pixel - centre) / f32(SUBPX))
    per_row = LANES // CMD
    spread = np.tile(infl.T, (per_row * SUB, 1))
    keep = np.kron(np.eye(per_row * SUB, dtype=f32), np.ones((1, SUB), f32))
    half = along_v.shape[1] // 2
    exact = [along_v[:, :half], along_v[:, half:], along_u, over_n, over_m]
    return dict(exact=np.concatenate(exact, axis=0).astype(bf16), mirror=np.concatenate([keep, spread], axis=0))


def unpack_tables(exact, slab_rows):
    e_cols = 2 * LANES
    spots = LG_DEV * slab_rows // SUBPX * SPOT
    edges = [0, e_cols, 2 * e_cols, 2 * e_cols + 2 * spots, 3 * e_cols + 2 * spots, exact.shape[0]]
    v_re, v_im, u, over_n, over_m = [exact.at[pl.ds(a, b - a)] for a, b in zip(edges, edges[1:])]
    return v_re, v_im, u, over_n, over_m


def split_dot(exact, wide, left):
    high = wide.astype(jnp.bfloat16)
    low = (wide - high.astype(jnp.float32)).astype(jnp.bfloat16)
    dot = functools.partial(jnp.dot, preferred_element_type=jnp.float32)
    if left:
        return dot(exact, high) + dot(exact, low)
    return dot(high, exact) + dot(low, exact)


def sincos(x):
    turns = jnp.floor(x * np.float32(2.0 / math.pi) + 0.5)
    r = x - turns * np.float32(1.5703125)
    r = r - turns * np.float32(4.837512969970703125e-4)
    r = r - turns * np.float32(7.54978995489188216e-8)
    z = r * r
    s = ((np.float32(-1.9515295891e-4) * z + np.float32(8.3321608736e-3)) * z - np.float32(1.6666654611e-1)) * z * r + r
    c = ((np.float32(2.443315711809948e-5) * z - np.float32(1.388731625493765e-3)) * z + np.float32(4.166664568298827e-2)) * z * z - np.float32(0.5) * z + 1.0
    q = turns.astype(jnp.int32) & 3
    odd = (q & 1) == 1
    sine = jnp.where(odd, c, s)
    cosine = jnp.where(odd, s, c)
    sine = jnp.where(q >= 2, -sine, sine)
    cosine = jnp.where((q == 1) | (q == 2), -cosine, cosine)
    return sine, cosine


def row_weights(my_rec, slab_rows):
    groups = []
    for k in range(slab_rows // 8):
        g = my_rec * (slab_rows // 8) + k
        first = (g + 1) // 2 - 1
        x = (g * 8 + lax.broadcasted_iota(jnp.int32, (8, LANES), 0)).astype(jnp.float32) + 0.5
        pair = []
        for a in (first, first + 1):
            inside = (a >= 0) & (a < SUB)
            centre = (a.astype(jnp.float32) + 0.5) * SUBPX
            w = jnp.maximum(0.0, 1.0 - jnp.abs(x - centre) / SUBPX)
            pair.append((jnp.clip(a, 0, SUB - 1), jnp.where(inside, w, 0.0)))
        groups.append(pair)
    return groups


def column_profiles(c_rows, mirror):
    at = LANES // CMD * SUB
    keep, spread = mirror[:at], mirror[at:]
    picked = [jnp.broadcast_to(c_rows[i : i + 1], keep.shape) * keep for i in range(c_rows.shape[0])]
    return jnp.dot(
        jnp.concatenate(picked, axis=0), spread, preferred_element_type=jnp.float32, precision=lax.Precision.HIGHEST
    )


def stages(n):
    return [1 << k for k in range(n.bit_length() - 1)]


def destination(me, bits, k):
    return (k << bits) | (me & ((1 << bits) - 1))


def offer_kernel(frame, slots, screens, out):
    partner = lax.axis_index("tile") ^ 1
    count, layers = out.shape[0], out.shape[1]
    for k in range(count):
        d = destination(partner, 1, k)
        for l in range(layers):
            for i in range(LG_DEV):
                out[k, l, i] = screens[l, slots[frame, l, d * ITEMS + i]]


def merge_kernel(frame, bits, owners, slots, mine, received, send, keep):
    me = lax.axis_index("tile")
    count, layers = send.shape[0], send.shape[1]
    other = 1 << (bits - 1)
    for out, side in ((keep, me), (send, me ^ (1 << bits))):
        for k in range(count):
            d = destination(side, bits + 1, k)
            j = d >> bits
            for l in range(layers):
                for i in range(LG_DEV):
                    g = d * ITEMS + i
                    theirs = ((owners[frame, l, g] ^ me) & other) != 0
                    ours = mine[l, slots[frame, l, g]] if bits == 1 else mine[j, l, i]
                    out[k, l, i] = jnp.where(theirs, received[j, l, i], ours)


def last_merge(frame, owners, kept, received):
    me = lax.axis_index("tile")
    layers = owners.shape[1]
    other = lax.axis_size("tile") // 2
    tiles = []
    for i in range(LG_DEV):
        row = []
        for l in range(layers):
            theirs = ((owners[frame, l, me * ITEMS + i] ^ me) & other) != 0
            row.append(jnp.where(theirs, received[0, l, i], kept[0, l, i]))
        tiles.append(row)
    return tiles


def slopes_from(tiles, prof, table, payload, slopes):
    slab_rows = tiles[0][0].shape[0]
    v_re, v_im, along_u, over_n, over_m = unpack_tables(table, slab_rows)
    my_rec = lax.axis_index("rec")
    weights = row_weights(my_rec, slab_rows)
    rows = []
    for i in range(LG_DEV):
        phase = functools.reduce(jnp.add, [tile.astype(jnp.float32) for tile in tiles[i]])
        for k, ((a0, w0), (a1, w1)) in enumerate(weights):
            shape = w0 * prof[pl.ds(i * SUB + a0, 1), :] + w1 * prof[pl.ds(i * SUB + a1, 1), :]
            rows.append(phase[k * 8 : (k + 1) * 8] - shape)
    residual = jnp.concatenate(rows, axis=0)
    sine, cosine = sincos(residual)
    e = jnp.concatenate([cosine.astype(jnp.bfloat16), sine.astype(jnp.bfloat16)], axis=1)
    g = [jnp.dot(e, v[...], preferred_element_type=jnp.float32).astype(jnp.bfloat16) for v in (v_re, v_im)]
    g = jnp.concatenate(g, axis=0)
    h = jnp.dot(along_u[...], g, preferred_element_type=jnp.float32)
    n = h.shape[0] // 2
    h_re, h_im = h[:n], h[n:]
    spot = h_re * h_re + h_im * h_im
    sums = split_dot(over_m[...], split_dot(over_n[...], spot, False), True)
    m = sums.shape[0] // 2
    lane = lax.broadcasted_iota(jnp.int32, (m, LANES), 1)
    row = lax.broadcasted_iota(jnp.int32, (m, LANES), 0)
    top = sums[:m, LANES:] + jnp.where(lane % 2 == 1, sums[m:, :LANES], 0.0)
    ratio = top / sums[:m, :LANES]
    sub_rows = slab_rows // SUBPX
    ratio = jnp.where(lane // SUBPX == my_rec * sub_rows + row // LG_DEV, ratio, 0.0)
    own = ratio[:LG_DEV]
    for a in range(1, sub_rows):
        own = own + ratio[a * LG_DEV : (a + 1) * LG_DEV]
    slopes[...] = own
    payload[...] = jnp.broadcast_to(own.astype(jnp.bfloat16).astype(jnp.float32)[None], payload.shape)


def own_rows(my_tile):
    per_row = LANES // CMD
    need = LG_DEV // per_row
    return lax.rem(my_tile * need, PT // per_row), need


def first_slopes(owners, kept, received, mirror, table, *refs):
    *c_parts, payload, slopes, c, prof = refs
    my_tile, my_rec = lax.axis_index("tile"), lax.axis_index("rec")
    for k, part in enumerate(c_parts):
        c[pl.ds((my_rec ^ k) * part.shape[0], part.shape[0]), :] = part[...]
    base, need = own_rows(my_tile)
    prof[...] = column_profiles(c[pl.ds(base, need), :], mirror)
    tiles = last_merge(0, owners, kept, received)
    slopes_from(tiles, prof, table, payload, slopes)


def ring_place(n, tile):
    return jnp.where(lax.rem(tile, 2) == 0, tile // 2, n - 1 - tile // 2)


def second_slopes(owners, kept, received, c_base, updates, mirror, table, payload, slopes, c_out, prof):
    my_tile = lax.axis_index("tile")
    c_out[...] = c_base[...] + loop_gain * jnp.sum(updates[...], axis=0).reshape(c_base.shape)
    base, need = own_rows(my_tile)
    prof[...] = column_profiles(c_out[pl.ds(base, need), :], mirror)
    tiles = last_merge(1, owners, kept, received)
    slopes_from(tiles, prof, table, payload, slopes)


def update_kernel(pattern, received, blocks, out, slopes):
    slopes[...] = jnp.sum(received[...], axis=1).reshape(slopes.shape)
    rows = []
    for i in range(blocks.shape[0]):
        total = None
        for b in range(blocks.shape[1]):
            vector = slopes[pl.ds(pattern[b, i], 1), :].astype(jnp.bfloat16)
            part = lax.dot_general(
                vector, blocks[i, b], (((1,), (1,)), ((), ())), preferred_element_type=jnp.float32
            )
            total = part if total is None else total + part
        rows.append(total)
    out[...] = jnp.broadcast_to(jnp.concatenate(rows, axis=0)[None], out.shape)


def science_kernel(n, tiles_here, owners, slots, c_first, c_second, mirror, *refs):
    gathered, out, store, prof, starts, sem = refs
    layers = owners.shape[1]
    slab_rows = out.shape[2]
    my_tile, my_rec = lax.axis_index("tile"), lax.axis_index("rec")
    copy = pltpu.make_async_copy(gathered, store, sem)
    copy.start()
    for o in range(n):
        starts[o] = ring_place(n, jnp.int32(o)) * layers * tiles_here
    weights = row_weights(my_rec, slab_rows)
    profile_rows = PT * SUB
    for f, c in enumerate((c_first, c_second)):
        prof[pl.ds(f * profile_rows, profile_rows)] = column_profiles(c[...], mirror)
    copy.wait()
    start = lax.rem(my_tile * SC_DEV, PT)
    for f in range(out.shape[0]):

        def one(q, both):
            row = f * profile_rows + lax.rem(start + q, PT) * SUB
            shapes = [
                w0 * prof[pl.ds(row + a0, 1), :] + w1 * prof[pl.ds(row + a1, 1), :]
                for (a0, w0), (a1, w1) in weights
            ]
            shape = jnp.concatenate(shapes, axis=0)
            for k in (q, q + PT)[: 1 + both]:
                g = my_tile * ITEMS + LG_DEV + k
                phase = None
                for l in range(layers):
                    tile = store[starts[owners[f, l, g]] + l * tiles_here + slots[f, l, g]].astype(jnp.float32)
                    phase = tile if phase is None else phase + tile
                out[f, k] = (phase - shape).astype(jnp.bfloat16)

        twice = SC_DEV - PT
        together = 4

        @pl.loop(0, twice // together)
        def _(q):
            for j in range(together):
                one(q * together + j, True)

        for q in range(twice // together * together, PT):
            one(q, q < twice)


def by_ring(screens, tile_owner, tile_slot, commands_init, reconstructor, pattern):
    layers, tiles_here, slab_rows, tile_px = screens.shape
    frames = tile_owner.shape[0]
    n = lax.axis_size("tile")
    rec_count = lax.axis_size("rec")
    everyone = n * rec_count
    my_tile, my_rec = lax.axis_index("tile"), lax.axis_index("rec")
    table = {k: jnp.asarray(v) for k, v in constant_tables(slab_rows).items()}
    block_rows = reconstructor.shape[0]
    f32 = jnp.float32
    limit = pltpu.CompilerParams(vmem_limit_bytes=24 << 20)

    ring = list(range(0, n, 2)) + list(range(n - 1, 0, -2))

    owners = tile_owner[..., 0]
    tables_in = [table["mirror"], table["exact"]]
    payload_out = [
        jax.ShapeDtypeStruct((everyone, LG_DEV, LANES), f32),
        jax.ShapeDtypeStruct((LG_DEV, LANES), f32),
    ]

    def exchange(payload):
        return lax.all_to_all(payload, ("tile", "rec"), split_axis=0, concat_axis=0, tiled=True)

    def updates_of(received, copies):
        received = received.reshape(n, rec_count, LG_DEV, LANES)
        return pl.pallas_call(
            update_kernel,
            out_shape=jax.ShapeDtypeStruct((copies, block_rows, LANES), f32),
            in_specs=[smem(), vmem(), vmem()],
            out_specs=vmem(),
            scratch_shapes=[pltpu.VMEM((n * LG_DEV, LANES), f32)],
            compiler_params=limit,
            cost_estimate=microseconds(2),
        )(pattern.T, received, reconstructor)

    wide = (layers, LG_DEV, slab_rows, tile_px)

    def tiles_of(*counts):
        shapes = [jax.ShapeDtypeStruct((c,) + wide, screens.dtype) for c in counts]
        return dict(out_shape=shapes, out_specs=[vmem()] * len(shapes))

    def swap(x, bit):
        return lax.ppermute(x, "tile", [(t, t ^ bit) for t in range(n)])

    def offer(frame, mine):
        (out,) = pl.pallas_call(
            functools.partial(offer_kernel, frame), in_specs=[smem(), vmem()], compiler_params=limit, **tiles_of(n // 2)
        )(tile_slot, mine)
        return out

    def merge(frame, bits, mine, received):
        count = n >> (bits + 1)
        return pl.pallas_call(
            functools.partial(merge_kernel, frame, bits),
            in_specs=[smem()] * 2 + [vmem()] * 2,
            compiler_params=limit,
            **tiles_of(count, count),
        )(owners, tile_slot, mine, received)

    def later(value, after):
        return lax.optimization_barrier((value, after))[0]

    def own_lanes(slopes):
        width = slab_rows // SUBPX * SUB * 2
        return lax.dynamic_slice_in_dim(slopes, my_rec * width, width, 1)

    last = n.bit_length() - 1
    sent = [offer(0, screens)]
    gathered_after = sent[0]
    second = offer(1, later(screens, sent[0]))
    kept, got = screens, swap(sent[0], 1)
    for bits in range(1, last):
        send, kept = merge(0, bits, kept, got)
        got = swap(send, 1 << bits)
    kept_second, got_second = later(screens, send), swap(second, 1)
    for bits in range(1, last):
        send, kept_second = merge(1, bits, kept_second, got_second)
        got_second = swap(send, 1 << bits)
        if bits == 1:
            kept = later(kept, send)
    guide = [(kept, got), (kept_second, got_second)]
    c_own = commands_init.reshape(-1, LANES)
    c_parts = [c_own] + [
        lax.ppermute(c_own, "rec", [(r, r ^ k) for r in range(rec_count)]) for k in range(1, rec_count)
    ]

    gathered = lax.all_gather(later(screens, gathered_after), "tile", axis_index_groups=[ring])
    gathered = gathered.reshape(n * layers * tiles_here, slab_rows, tile_px)

    payload, slopes_first, c0 = pl.pallas_call(
        first_slopes,
        out_shape=payload_out + [jax.ShapeDtypeStruct((rec_count * block_rows, LANES), f32)],
        in_specs=[smem()] + [vmem()] * (2 + rec_count + len(tables_in)),
        out_specs=[vmem()] * 3,
        scratch_shapes=[pltpu.VMEM((LG_DEV * SUB, LANES), f32)],
        compiler_params=limit,
        cost_estimate=microseconds(3),
    )(owners, *guide[0], *tables_in, *c_parts)
    slopes_first = own_lanes(slopes_first)
    updates = updates_of(later(exchange(payload), send), everyone)
    updates = lax.all_to_all(updates, ("tile", "rec"), split_axis=0, concat_axis=0, tiled=True)
    updates = updates.reshape(n, rec_count, block_rows, LANES)

    payload, slopes_second, c1 = pl.pallas_call(
        second_slopes,
        out_shape=payload_out + [jax.ShapeDtypeStruct(c0.shape, f32)],
        in_specs=[smem()] + [vmem()] * (4 + len(tables_in)),
        out_specs=[vmem()] * 3,
        scratch_shapes=[pltpu.VMEM((LG_DEV * SUB, LANES), f32)],
        compiler_params=limit,
        cost_estimate=microseconds(3),
    )(owners, *guide[1], c0, updates, *tables_in)
    updates = updates_of(exchange(payload), n)
    updates = lax.all_to_all(updates, "tile", split_axis=0, concat_axis=0, tiled=True)
    science = pl.pallas_call(
        functools.partial(science_kernel, n, tiles_here),
        out_shape=jax.ShapeDtypeStruct((frames, SC_DEV, slab_rows, tile_px), jnp.bfloat16),
        in_specs=[smem()] * 2 + [vmem()] * 3 + [pl.BlockSpec(memory_space=pl.ANY)],
        out_specs=vmem(),
        scratch_shapes=[
            pltpu.VMEM((n * layers * tiles_here, slab_rows, tile_px), screens.dtype),
            pltpu.VMEM((frames * PT * SUB, LANES), f32),
            pltpu.SMEM((n,), jnp.int32),
            pltpu.SemaphoreType.DMA,
        ],
        compiler_params=pltpu.CompilerParams(vmem_limit_bytes=60 << 20),
        cost_estimate=pl.CostEstimate(
            flops=8 * frames * SC_DEV * slab_rows * tile_px,
            bytes_accessed=2 * (n * layers * tiles_here + frames * SC_DEV) * slab_rows * tile_px,
            transcendentals=0,
        ),
    )(owners, tile_slot, c0, c1, table["mirror"], gathered)
    updates = later(updates, science)
    mine = lax.dynamic_slice_in_dim(c1, my_rec * block_rows, block_rows, 0)
    c2 = mine + loop_gain * jnp.sum(updates, axis=0)
    return jnp.stack([slopes_first, own_lanes(slopes_second)], axis=0), science, c2.reshape(-1)


def per_device(screens, tile_owner, *rest):
    layers, tiles_here, _, _ = screens.shape
    frames, n = tile_owner.shape[0], lax.axis_size("tile")
    capacity = max(2, 3 * ITEMS // (2 * n))
    few = tiles_here <= frames * capacity and n & (n - 1) == 0 and frames == 2 and layers == 2
    return (by_ring if few else by_request)(screens, tile_owner, *rest)


def solution(mesh):
    placed = (
        P(None, "tile", "rec", None),
        P(),
        P(),
        P("rec"),
        P("rec", "tile", None, None),
        P("rec", "tile"),
    )
    return jax.shard_map(
        per_device,
        mesh=mesh,
        in_specs=placed,
        out_specs=(P(None, "tile", "rec"), P(None, "tile", "rec", None), P("rec")),
        check_vma=False,
    )
```

```python
import functools
import math

import jax
import jax.numpy as jnp
import ml_dtypes
import numpy as np
from jax import lax
from jax.experimental import pallas as pl
from jax.experimental.pallas import tpu as pltpu
from jax.sharding import PartitionSpec as P

SUBPX = 16
SPOT = 32
SUB = 8
PT = 64
LG_DEV = 4
SC_DEV = 124
ITEMS = LG_DEV + SC_DEV
LANES = 128
CMD = SUB * SUB

loop_gain = 0.5


def influence(tile_px, sub_px, sub_count):
    pixel = jnp.arange(tile_px, dtype=jnp.float32)[:, None] + 0.5
    centre = (jnp.arange(sub_count, dtype=jnp.float32)[None, :] + 0.5) * sub_px
    return jnp.maximum(0.0, 1.0 - jnp.abs(pixel - centre) / sub_px)


def tables(spot_px, sub_px):
    freq = jnp.arange(spot_px, dtype=jnp.int32)[:, None]
    pixel = jnp.arange(sub_px, dtype=jnp.int32)[None, :]
    turns = (freq * pixel % spot_px).astype(jnp.float32) * (2.0 * math.pi / spot_px)
    return (jnp.cos(turns).astype(jnp.bfloat16), jnp.sin(turns).astype(jnp.bfloat16))


def centred(spot_px):
    index = jnp.arange(spot_px, dtype=jnp.int32)
    return ((index + spot_px // 2) % spot_px - spot_px // 2).astype(jnp.float32) / spot_px


def along_pixels(values, table):
    return jnp.einsum("iaubv,nv->iaubn", values, table, preferred_element_type=jnp.float32)


def along_rows(table, values):
    return jnp.einsum("mu,iaubn->iabmn", table, values, preferred_element_type=jnp.float32)


def spot_slopes(residual):
    item_count, row_px, col_px = residual.shape
    sub_rows = row_px // SUBPX
    sub_cols = col_px // SUBPX
    cos_t, sin_t = tables(SPOT, SUBPX)
    pieces = residual.reshape(item_count, sub_rows, SUBPX, sub_cols, SUBPX)
    real_part = jnp.cos(pieces).astype(jnp.bfloat16)
    imag_part = jnp.sin(pieces).astype(jnp.bfloat16)
    g_re = (along_pixels(real_part, cos_t) + along_pixels(imag_part, sin_t)).astype(jnp.bfloat16)
    g_im = (along_pixels(imag_part, cos_t) - along_pixels(real_part, sin_t)).astype(jnp.bfloat16)
    h_re = along_rows(cos_t, g_re) + along_rows(sin_t, g_im)
    h_im = along_rows(cos_t, g_im) - along_rows(sin_t, g_re)
    spots = h_re * h_re + h_im * h_im
    coords = centred(SPOT)
    totals = jnp.sum(spots, axis=(3, 4))
    slope_x = jnp.sum(spots * coords[None, None, None, None, :], axis=(3, 4)) / totals
    slope_y = jnp.sum(spots * coords[None, None, None, :, None], axis=(3, 4)) / totals
    return jnp.stack([slope_x, slope_y], axis=-1).reshape(item_count, sub_rows * sub_cols * 2)


def pack_tiles(screens, owners, slots, pairs, my_tile, capacity):
    packed = []
    places = jnp.arange(capacity, dtype=jnp.int32)
    for frame, layer_idx in pairs:
        owner_rows = owners[frame, layer_idx]
        slot_rows = slots[frame, layer_idx]
        mine = owner_rows == my_tile
        order = jnp.cumsum(mine.astype(jnp.int32), axis=1) - 1
        picked = mine[:, None, :] & (order[:, None, :] == places[None, :, None])
        wanted = jnp.sum(jnp.where(picked, slot_rows[:, None, :], 0), axis=2)
        packed.append(jnp.take(screens[layer_idx], wanted, axis=0))
    return jnp.stack(packed, axis=1)


def unpack_tiles(received, owners, pairs, my_tile, capacity):
    results = []
    item_count = owners.shape[3]
    later = jnp.arange(item_count, dtype=jnp.int32)
    earlier_mask = later[None, :] < later[:, None]
    for position in range(len(pairs)):
        frame, layer_idx = pairs[position]
        mine = lax.dynamic_index_in_dim(owners[frame, layer_idx], my_tile, 0, keepdims=False)
        same_owner = mine[:, None] == mine[None, :]
        order = jnp.sum((same_owner & earlier_mask).astype(jnp.int32), axis=1)
        flat_index = mine * capacity + order
        layer_tiles = received[:, position].reshape(-1, received.shape[3], received.shape[4])
        results.append(jnp.take(layer_tiles, flat_index, axis=0).astype(jnp.float32))
    return results


def by_request(screens, tile_owner, tile_slot, commands_init, reconstructor, pattern):
    layer_total, tiles_here, slab_rows, tile_px = screens.shape
    frame_total = tile_owner.shape[0]
    tile_count = lax.axis_size("tile")
    rec_count = lax.axis_size("rec")
    my_tile = lax.axis_index("tile")
    my_rec = lax.axis_index("rec")
    capacity = max(2, 3 * ITEMS // (2 * tile_count))
    owners = tile_owner[..., 0].reshape(frame_total, layer_total, tile_count, ITEMS)
    slots = tile_slot.reshape(frame_total, layer_total, tile_count, ITEMS)
    influence_all = influence(tile_px, SUBPX, SUB)
    influence_rows = lax.dynamic_slice_in_dim(influence_all, my_rec * slab_rows, slab_rows, 0)
    lgs_places = (my_tile * LG_DEV + jnp.arange(LG_DEV, dtype=jnp.int32)) % PT
    sci_places = (my_tile * SC_DEV + jnp.arange(SC_DEV, dtype=jnp.int32)) % PT
    item_places = jnp.concatenate([lgs_places, sci_places])
    state = commands_init
    slope_frames = []
    science_frames = []
    for frame in range(frame_total):
        pairs = [(frame, layer_idx) for layer_idx in range(layer_total)]
        sending = pack_tiles(screens, owners, slots, pairs, my_tile, capacity)
        received = lax.all_to_all(sending, "tile", split_axis=0, concat_axis=0, tiled=True)
        pieces = unpack_tiles(received, owners, pairs, my_tile, capacity)
        phase = functools.reduce(jnp.add, pieces)
        full_commands = lax.all_gather(state, "rec", axis=0, tiled=True)
        mirror = full_commands.reshape(PT, SUB, SUB)
        chosen = jnp.take(mirror, item_places, axis=0)
        shapes = jnp.einsum(
            "xa,iab,yb->ixy", influence_rows, chosen, influence_all, precision=lax.Precision.HIGHEST
        )
        residual = phase - shapes
        science_frames.append(residual[LG_DEV:].astype(jnp.bfloat16))
        slopes = spot_slopes(residual[:LG_DEV])
        slope_frames.append(slopes)
        slopes_b = slopes.astype(jnp.bfloat16)
        everyone = lax.all_gather(slopes_b[None], ("tile", "rec"), axis=0, tiled=True)
        everyone = everyone.reshape(tile_count, rec_count, LG_DEV, -1).transpose(0, 2, 1, 3)
        everyone = everyone.reshape(tile_count * LG_DEV, -1)
        needed = jnp.take(everyone, pattern, axis=0)
        partial_rows = jnp.einsum(
            "ibcs,ibs->ic", reconstructor, needed, preferred_element_type=jnp.float32
        ).reshape(-1)
        state = state + loop_gain * lax.psum(partial_rows, "tile")
    return (jnp.stack(slope_frames, axis=0), jnp.stack(science_frames, axis=0), state)


def microseconds(t):
    return pl.CostEstimate(flops=0, bytes_accessed=int(t * 3.69e6), transcendentals=0)


def vmem():
    return pl.BlockSpec(memory_space=pltpu.VMEM)


def smem():
    return pl.BlockSpec(memory_space=pltpu.SMEM)


def constant_tables(slab_rows):
    f32, bf16 = np.float32, ml_dtypes.bfloat16
    turns = (np.arange(SPOT)[:, None] * np.arange(SUBPX)[None, :] % SPOT).astype(f32)
    turns = turns * f32(2.0 * math.pi / SPOT)
    cos_t, sin_t = np.cos(turns).astype(bf16).astype(f32), np.sin(turns).astype(bf16).astype(f32)
    cols = LANES // SUBPX
    eye_c = np.eye(cols, dtype=f32)
    cos_v, sin_v = np.kron(eye_c, cos_t.T), np.kron(eye_c, sin_t.T)
    along_v = np.block([[cos_v, -sin_v], [sin_v, cos_v]])
    rows = LG_DEV * slab_rows // SUBPX
    eye_r = np.eye(rows, dtype=f32)
    cos_u, sin_u = np.kron(eye_r, cos_t), np.kron(eye_r, sin_t)
    along_u = np.block([[cos_u, sin_u], [-sin_u, cos_u]])
    index = np.arange(SPOT)
    coord = (((index + SPOT // 2) % SPOT) - SPOT // 2).astype(f32) / SPOT
    groups = LANES // (2 * cols)
    total_n = np.zeros((cols, SPOT, groups, cols, 2), f32)
    coord_n = np.zeros((cols, SPOT, groups, cols, 2), f32)
    for b in range(cols):
        total_n[b, :, :, b, :] = 1.0
        coord_n[b, :, :, b, 0] = coord[:, None]
    over_n = np.concatenate([t.reshape(cols * SPOT, LANES) for t in (total_n, coord_n)], axis=1)
    sub_rows = slab_rows // SUBPX
    total_m = np.zeros((sub_rows, LG_DEV, LG_DEV, sub_rows, SPOT), f32)
    coord_m = np.zeros((sub_rows, LG_DEV, LG_DEV, sub_rows, SPOT), f32)
    for a in range(sub_rows):
        for i in range(LG_DEV):
            total_m[a, i, i, a, :] = 1.0
            coord_m[a, i, i, a, :] = coord
    over_m = np.concatenate([t.reshape(rows, rows * SPOT) for t in (total_m, coord_m)], axis=0)
    pixel = np.arange(LANES, dtype=f32)[:, None] + f32(0.5)
    centre = (np.arange(SUB, dtype=f32)[None, :] + f32(0.5)) * SUBPX
    infl = np.maximum(f32(0.0), f32(1.0) - np.abs(pixel - centre) / f32(SUBPX))
    per_row = LANES // CMD
    spread = np.tile(infl.T, (per_row * SUB, 1))
    keep = np.kron(np.eye(per_row * SUB, dtype=f32), np.ones((1, SUB), f32))
    half = along_v.shape[1] // 2
    exact = [along_v[:, :half], along_v[:, half:], along_u, over_n, over_m]
    return dict(exact=np.concatenate(exact, axis=0).astype(bf16), mirror=np.concatenate([keep, spread], axis=0))


def unpack_tables(exact, slab_rows):
    e_cols = 2 * LANES
    spots = LG_DEV * slab_rows // SUBPX * SPOT
    edges = [0, e_cols, 2 * e_cols, 2 * e_cols + 2 * spots, 3 * e_cols + 2 * spots, exact.shape[0]]
    v_re, v_im, u, over_n, over_m = [exact.at[pl.ds(a, b - a)] for a, b in zip(edges, edges[1:])]
    return v_re, v_im, u, over_n, over_m


def split_dot(exact, wide, left):
    high = wide.astype(jnp.bfloat16)
    low = (wide - high.astype(jnp.float32)).astype(jnp.bfloat16)
    dot = functools.partial(jnp.dot, preferred_element_type=jnp.float32)
    if left:
        return dot(exact, high) + dot(exact, low)
    return dot(high, exact) + dot(low, exact)


def sincos(x):
    turns = jnp.floor(x * np.float32(2.0 / math.pi) + 0.5)
    r = x - turns * np.float32(1.5703125)
    r = r - turns * np.float32(4.837512969970703125e-4)
    r = r - turns * np.float32(7.54978995489188216e-8)
    z = r * r
    s = ((np.float32(-1.9515295891e-4) * z + np.float32(8.3321608736e-3)) * z - np.float32(1.6666654611e-1)) * z * r + r
    c = ((np.float32(2.443315711809948e-5) * z - np.float32(1.388731625493765e-3)) * z + np.float32(4.166664568298827e-2)) * z * z - np.float32(0.5) * z + 1.0
    q = turns.astype(jnp.int32) & 3
    odd = (q & 1) == 1
    sine = jnp.where(odd, c, s)
    cosine = jnp.where(odd, s, c)
    sine = jnp.where(q >= 2, -sine, sine)
    cosine = jnp.where((q == 1) | (q == 2), -cosine, cosine)
    return sine, cosine


def row_weights(my_rec, slab_rows):
    groups = []
    for k in range(slab_rows // 8):
        g = my_rec * (slab_rows // 8) + k
        first = (g + 1) // 2 - 1
        x = (g * 8 + lax.broadcasted_iota(jnp.int32, (8, LANES), 0)).astype(jnp.float32) + 0.5
        pair = []
        for a in (first, first + 1):
            inside = (a >= 0) & (a < SUB)
            centre = (a.astype(jnp.float32) + 0.5) * SUBPX
            w = jnp.maximum(0.0, 1.0 - jnp.abs(x - centre) / SUBPX)
            pair.append((jnp.clip(a, 0, SUB - 1), jnp.where(inside, w, 0.0)))
        groups.append(pair)
    return groups


def column_profiles(c_rows, mirror):
    at = LANES // CMD * SUB
    keep, spread = mirror[:at], mirror[at:]
    picked = [jnp.broadcast_to(c_rows[i : i + 1], keep.shape) * keep for i in range(c_rows.shape[0])]
    return jnp.dot(
        jnp.concatenate(picked, axis=0), spread, preferred_element_type=jnp.float32, precision=lax.Precision.HIGHEST
    )


def stages(n):
    return [1 << k for k in range(n.bit_length() - 1)]


def destination(me, bits, k):
    return (k << bits) | (me & ((1 << bits) - 1))


def offer_kernel(frame, slots, screens, out):
    partner = lax.axis_index("tile") ^ 1
    for k in range(out.shape[0]):
        d = destination(partner, 1, k)
        for l in range(out.shape[1]):
            for i in range(LG_DEV):
                out[k, l, i] = screens[l, slots[frame, l, d * ITEMS + i]]


def merge_kernel(frame, bits, owners, slots, mine, received, send, keep, *flags):
    me = lax.axis_index("tile")
    count, layers = send.shape[0], send.shape[1]
    other = 1 << (bits - 1)
    for out, side in ((keep, me), (send, me ^ (1 << bits))):
        for k in range(count):
            d = destination(side, bits + 1, k)
            j = d >> bits
            for l in range(layers):
                for i in range(LG_DEV):
                    g = d * ITEMS + i
                    theirs = ((owners[frame, l, g] ^ me) & other) != 0
                    ours = mine[l, slots[frame, l, g]] if bits == 1 else mine[j, l, i]
                    out[k, l, i] = jnp.where(theirs, received[j, l, i], ours)
    for flag in flags:
        for l in range(layers):
            for i in range(LG_DEV):
                theirs = ((owners[frame, l, me * ITEMS + i] ^ me) >> bits) & 1
                flag[pl.ds(i * layers + l, 1), :] = jnp.full((1, LANES), theirs).astype(jnp.float32)


def last_merge(kept, received, flags):
    layers = kept.shape[1]

    def tile(i, l):
        theirs = flags[pl.ds(i * layers + l, 1), :] > 0.5
        return jnp.where(theirs, received[0, l, i].astype(jnp.float32), kept[0, l, i].astype(jnp.float32))

    return [[tile(i, l) for l in range(layers)] for i in range(LG_DEV)]


def slopes_from(tiles, prof, table, payload, slopes):
    slab_rows = tiles[0][0].shape[0]
    v_re, v_im, along_u, over_n, over_m = unpack_tables(table, slab_rows)
    my_rec = lax.axis_index("rec")
    weights = row_weights(my_rec, slab_rows)
    rows = []
    for i in range(LG_DEV):
        phase = functools.reduce(jnp.add, [tile.astype(jnp.float32) for tile in tiles[i]])
        for k, ((a0, w0), (a1, w1)) in enumerate(weights):
            shape = w0 * prof[pl.ds(i * SUB + a0, 1), :] + w1 * prof[pl.ds(i * SUB + a1, 1), :]
            rows.append(phase[k * 8 : (k + 1) * 8] - shape)
    residual = jnp.concatenate(rows, axis=0)
    sine, cosine = sincos(residual)
    e = jnp.concatenate([cosine.astype(jnp.bfloat16), sine.astype(jnp.bfloat16)], axis=1)
    g = [jnp.dot(e, v[...], preferred_element_type=jnp.float32).astype(jnp.bfloat16) for v in (v_re, v_im)]
    g = jnp.concatenate(g, axis=0)
    h = jnp.dot(along_u[...], g, preferred_element_type=jnp.float32)
    n = h.shape[0] // 2
    h_re, h_im = h[:n], h[n:]
    spot = h_re * h_re + h_im * h_im
    sums = split_dot(over_m[...], split_dot(over_n[...], spot, False), True)
    m = sums.shape[0] // 2
    lane = lax.broadcasted_iota(jnp.int32, (m, LANES), 1)
    row = lax.broadcasted_iota(jnp.int32, (m, LANES), 0)
    top = sums[:m, LANES:] + jnp.where(lane % 2 == 1, sums[m:, :LANES], 0.0)
    ratio = top / sums[:m, :LANES]
    sub_rows = slab_rows // SUBPX
    ratio = jnp.where(lane // SUBPX == my_rec * sub_rows + row // LG_DEV, ratio, 0.0)
    own = ratio[:LG_DEV]
    for a in range(1, sub_rows):
        own = own + ratio[a * LG_DEV : (a + 1) * LG_DEV]
    slopes[...] = own
    payload[...] = jnp.broadcast_to(own.astype(jnp.bfloat16).astype(jnp.float32)[None], payload.shape)


def own_rows(my_tile):
    per_row = LANES // CMD
    need = LG_DEV // per_row
    return lax.rem(my_tile * need, PT // per_row), need


def first_slopes(kept, received, flags, mirror, table, *refs):
    *c_parts, payload, slopes, c, prof = refs
    my_tile, my_rec = lax.axis_index("tile"), lax.axis_index("rec")
    for k, part in enumerate(c_parts):
        c[pl.ds((my_rec ^ k) * part.shape[0], part.shape[0]), :] = part[...]
    base, need = own_rows(my_tile)
    prof[...] = column_profiles(c[pl.ds(base, need), :], mirror)
    tiles = last_merge(kept, received, flags)
    slopes_from(tiles, prof, table, payload, slopes)


def second_slopes(kept, received, flags, c_base, updates, mirror, table, payload, slopes, c_out, c_own, prof):
    my_tile = lax.axis_index("tile")
    c_out[...] = c_base[...] + loop_gain * jnp.sum(updates[...], axis=0).reshape(c_base.shape)
    c_own[...] = c_out[pl.ds(lax.axis_index("rec") * c_own.shape[0], c_own.shape[0]), :]
    base, need = own_rows(my_tile)
    prof[...] = column_profiles(c_out[pl.ds(base, need), :], mirror)
    tiles = last_merge(kept, received, flags)
    slopes_from(tiles, prof, table, payload, slopes)


def update_kernel(pattern, received, blocks, out, slopes):
    slopes[...] = jnp.sum(received[...], axis=1).reshape(slopes.shape)
    rows = []
    for i in range(blocks.shape[0]):
        total = None
        for b in range(blocks.shape[1]):
            vector = slopes[pl.ds(pattern[b, i], 1), :].astype(jnp.bfloat16)
            part = lax.dot_general(
                vector, blocks[i, b], (((1,), (1,)), ((), ())), preferred_element_type=jnp.float32
            )
            total = part if total is None else total + part
        rows.append(total)
    out[...] = jnp.broadcast_to(jnp.concatenate(rows, axis=0)[None], out.shape)


def science_kernel(places, c_first, c_second, mirror, gathered, out, store, prof, sem):
    slab_rows = out.shape[2]
    my_tile, my_rec = lax.axis_index("tile"), lax.axis_index("rec")
    parts = sem.shape[0]
    size = store.shape[0] // parts
    copies = [
        pltpu.make_async_copy(gathered.at[pl.ds(i * size, size)], store.at[pl.ds(i * size, size)], sem.at[i])
        for i in range(parts)
    ]
    for copy in copies:
        copy.start()
    weights = row_weights(my_rec, slab_rows)
    profile_rows = PT * SUB
    for f, c in enumerate((c_first, c_second)):
        prof[pl.ds(f * profile_rows, profile_rows)] = column_profiles(c[...], mirror)
    for copy in copies:
        copy.wait()
    layers = places.shape[0] // (out.shape[0] * SC_DEV)
    start = lax.rem(my_tile * SC_DEV, PT)
    for f in range(out.shape[0]):

        def one(q, both):
            row = f * profile_rows + lax.rem(start + q, PT) * SUB
            shapes = [
                w0 * prof[pl.ds(row + a0, 1), :] + w1 * prof[pl.ds(row + a1, 1), :]
                for (a0, w0), (a1, w1) in weights
            ]
            shape = jnp.concatenate(shapes, axis=0)
            for k in (q, q + PT)[: 1 + both]:
                phase = None
                for l in range(layers):
                    tile = store[places[(f * layers + l) * SC_DEV + k]].astype(jnp.float32)
                    phase = tile if phase is None else phase + tile
                out[f, k] = (phase - shape).astype(jnp.bfloat16)

        twice = SC_DEV - PT
        together = 4

        @pl.loop(0, twice // together)
        def _(q):
            for j in range(together):
                one(q * together + j, True)

        for q in range(twice // together * together, PT):
            one(q, q < twice)


def by_ring(screens, tile_owner, tile_slot, commands_init, reconstructor, pattern):
    layers, tiles_here, slab_rows, tile_px = screens.shape
    frames = tile_owner.shape[0]
    n = lax.axis_size("tile")
    rec_count = lax.axis_size("rec")
    everyone = n * rec_count
    my_tile, my_rec = lax.axis_index("tile"), lax.axis_index("rec")
    table = {k: jnp.asarray(v) for k, v in constant_tables(slab_rows).items()}
    block_rows = reconstructor.shape[0]
    f32 = jnp.float32
    limit = pltpu.CompilerParams(vmem_limit_bytes=24 << 20)

    ring = list(range(0, n, 2)) + list(range(n - 1, 0, -2))

    owners = tile_owner[..., 0]
    tables_in = [table["mirror"], table["exact"]]
    payload_out = [
        jax.ShapeDtypeStruct((everyone, LG_DEV, LANES), f32),
        jax.ShapeDtypeStruct((LG_DEV, LANES), f32),
    ]

    def exchange(payload):
        return lax.all_to_all(payload, ("tile", "rec"), split_axis=0, concat_axis=0, tiled=True)

    def updates_of(received, copies):
        received = received.reshape(n, rec_count, LG_DEV, LANES)
        return pl.pallas_call(
            update_kernel,
            out_shape=jax.ShapeDtypeStruct((copies, block_rows, LANES), f32),
            in_specs=[smem(), vmem(), vmem()],
            out_specs=vmem(),
            scratch_shapes=[pltpu.VMEM((n * LG_DEV, LANES), f32)],
            compiler_params=limit,
            cost_estimate=microseconds(2),
        )(pattern.T, received, reconstructor)

    wide = (layers, LG_DEV, slab_rows, tile_px)

    def tiles_of(*counts):
        shapes = [jax.ShapeDtypeStruct((c,) + wide, screens.dtype) for c in counts]
        return dict(out_shape=shapes, out_specs=[vmem()] * len(shapes))

    def swap(x, bit):
        return lax.ppermute(x, "tile", [(t, t ^ bit) for t in range(n)])

    def offer(frame, mine):
        (out,) = pl.pallas_call(
            functools.partial(offer_kernel, frame),
            in_specs=[smem(), vmem()],
            compiler_params=limit,
            **tiles_of(n // 2),
        )(tile_slot, mine)
        return out

    def merge(frame, bits, mine, received):
        count = n >> (bits + 1)
        outs = tiles_of(count, count)
        if count == 1:
            outs["out_shape"].append(jax.ShapeDtypeStruct((LG_DEV * layers, LANES), f32))
            outs["out_specs"].append(vmem())
        return pl.pallas_call(
            functools.partial(merge_kernel, frame, bits),
            in_specs=[smem()] * 2 + [vmem()] * 2,
            compiler_params=limit,
            **outs,
        )(owners, tile_slot, mine, received)

    def later(value, after):
        return lax.optimization_barrier((value, after))[0]

    def own_lanes(slopes):
        width = slab_rows // SUBPX * SUB * 2
        return lax.dynamic_slice_in_dim(slopes, my_rec * width, width, 1)

    last = n.bit_length() - 1
    c_own = commands_init.reshape(-1, LANES)
    c_parts = [c_own] + [
        lax.ppermute(c_own, "rec", [(r, r ^ k) for r in range(rec_count)]) for k in range(1, rec_count)
    ]
    wanted = offer(0, screens)
    second = offer(1, later(screens, wanted))
    kept, got = screens, swap(wanted, 1)
    for bits in range(1, last):
        send, kept, *flags = merge(0, bits, kept, got)
        got = swap(send, 1 << bits)
    guide = [(kept, got, *flags)]
    kept, got = later(screens, send), swap(second, 1)
    for bits in range(1, last):
        send, kept, *flags = merge(1, bits, kept, got)
        got = swap(send, 1 << bits)
        if bits == 1:
            guide[0] = (later(guide[0][0], send), *guide[0][1:])
    guide.append((kept, got, *flags))

    gathered = lax.all_gather(later(screens, wanted), "tile", axis_index_groups=[ring])
    gathered = gathered.reshape(n * layers * tiles_here, slab_rows, tile_px)

    def own_items(x):
        return lax.dynamic_slice_in_dim(x, my_tile * ITEMS + LG_DEV, SC_DEV, 2)

    owner = own_items(owners)
    at = jnp.where(owner % 2 == 0, owner // 2, n - 1 - owner // 2) * layers
    places = (at + jnp.arange(layers, dtype=jnp.int32)[None, :, None]) * tiles_here + own_items(tile_slot)
    places = places.reshape(-1)

    payload, slopes_first, c0 = pl.pallas_call(
        first_slopes,
        out_shape=payload_out + [jax.ShapeDtypeStruct((rec_count * block_rows, LANES), f32)],
        in_specs=[vmem()] * (3 + rec_count + len(tables_in)),
        out_specs=[vmem()] * 3,
        scratch_shapes=[pltpu.VMEM((LG_DEV * SUB, LANES), f32)],
        compiler_params=limit,
        cost_estimate=microseconds(3),
    )(*guide[0], *tables_in, *c_parts)
    slopes_first = own_lanes(slopes_first)
    updates = updates_of(later(exchange(payload), send), everyone)
    updates = lax.all_to_all(updates, ("tile", "rec"), split_axis=0, concat_axis=0, tiled=True)
    updates = updates.reshape(n, rec_count, block_rows, LANES)

    payload, slopes_second, c1, mine = pl.pallas_call(
        second_slopes,
        out_shape=payload_out + [jax.ShapeDtypeStruct(r, f32) for r in (c0.shape, c_own.shape)],
        in_specs=[vmem()] * (5 + len(tables_in)),
        out_specs=[vmem()] * 4,
        scratch_shapes=[pltpu.VMEM((LG_DEV * SUB, LANES), f32)],
        compiler_params=limit,
        cost_estimate=microseconds(3),
    )(*guide[1], c0, updates, *tables_in)
    updates = updates_of(exchange(payload), n)
    updates = lax.all_to_all(updates, "tile", split_axis=0, concat_axis=0, tiled=True)
    science = pl.pallas_call(
        science_kernel,
        out_shape=jax.ShapeDtypeStruct((frames, SC_DEV, slab_rows, tile_px), jnp.bfloat16),
        in_specs=[smem()] + [vmem()] * 3 + [pl.BlockSpec(memory_space=pl.ANY)],
        out_specs=vmem(),
        scratch_shapes=[
            pltpu.VMEM((n * layers * tiles_here, slab_rows, tile_px), screens.dtype),
            pltpu.VMEM((frames * PT * SUB, LANES), f32),
            pltpu.SemaphoreType.DMA((n,)),
        ],
        compiler_params=pltpu.CompilerParams(vmem_limit_bytes=60 << 20),
        cost_estimate=pl.CostEstimate(
            flops=8 * frames * SC_DEV * slab_rows * tile_px,
            bytes_accessed=2 * (n * layers * tiles_here + frames * SC_DEV) * slab_rows * tile_px,
            transcendentals=0,
        ),
    )(places, c0, c1, table["mirror"], gathered)
    updates = later(updates, science)
    c2 = mine + loop_gain * jnp.sum(updates, axis=0)
    return jnp.stack([slopes_first, own_lanes(slopes_second)], axis=0), science, c2.reshape(-1)


def per_device(screens, tile_owner, *rest):
    layers, tiles_here, _, _ = screens.shape
    frames, n = tile_owner.shape[0], lax.axis_size("tile")
    capacity = max(2, 3 * ITEMS // (2 * n))
    few = tiles_here <= frames * capacity and n & (n - 1) == 0 and frames == 2 and layers == 2
    return (by_ring if few else by_request)(screens, tile_owner, *rest)


def solution(mesh):
    placed = (
        P(None, "tile", "rec", None),
        P(),
        P(),
        P("rec"),
        P("rec", "tile", None, None),
        P("rec", "tile"),
    )
    return jax.shard_map(
        per_device,
        mesh=mesh,
        in_specs=placed,
        out_specs=(P(None, "tile", "rec"), P(None, "tile", "rec", None), P("rec")),
        check_vma=False,
    )
```

```python
import functools
import math

import jax
import jax.numpy as jnp
import ml_dtypes
import numpy as np
from jax import lax
from jax.experimental import pallas as pl
from jax.experimental.pallas import tpu as pltpu
from jax.sharding import PartitionSpec as P

SUBPX = 16
SPOT = 32
SUB = 8
PT = 64
LG_DEV = 4
SC_DEV = 124
ITEMS = LG_DEV + SC_DEV
LANES = 128
CMD = SUB * SUB

loop_gain = 0.5


def influence(tile_px, sub_px, sub_count):
    pixel = jnp.arange(tile_px, dtype=jnp.float32)[:, None] + 0.5
    centre = (jnp.arange(sub_count, dtype=jnp.float32)[None, :] + 0.5) * sub_px
    return jnp.maximum(0.0, 1.0 - jnp.abs(pixel - centre) / sub_px)


def tables(spot_px, sub_px):
    freq = jnp.arange(spot_px, dtype=jnp.int32)[:, None]
    pixel = jnp.arange(sub_px, dtype=jnp.int32)[None, :]
    turns = (freq * pixel % spot_px).astype(jnp.float32) * (2.0 * math.pi / spot_px)
    return (jnp.cos(turns).astype(jnp.bfloat16), jnp.sin(turns).astype(jnp.bfloat16))


def centred(spot_px):
    index = jnp.arange(spot_px, dtype=jnp.int32)
    return ((index + spot_px // 2) % spot_px - spot_px // 2).astype(jnp.float32) / spot_px


def along_pixels(values, table):
    return jnp.einsum("iaubv,nv->iaubn", values, table, preferred_element_type=jnp.float32)


def along_rows(table, values):
    return jnp.einsum("mu,iaubn->iabmn", table, values, preferred_element_type=jnp.float32)


def spot_slopes(residual):
    item_count, row_px, col_px = residual.shape
    sub_rows = row_px // SUBPX
    sub_cols = col_px // SUBPX
    cos_t, sin_t = tables(SPOT, SUBPX)
    pieces = residual.reshape(item_count, sub_rows, SUBPX, sub_cols, SUBPX)
    real_part = jnp.cos(pieces).astype(jnp.bfloat16)
    imag_part = jnp.sin(pieces).astype(jnp.bfloat16)
    g_re = (along_pixels(real_part, cos_t) + along_pixels(imag_part, sin_t)).astype(jnp.bfloat16)
    g_im = (along_pixels(imag_part, cos_t) - along_pixels(real_part, sin_t)).astype(jnp.bfloat16)
    h_re = along_rows(cos_t, g_re) + along_rows(sin_t, g_im)
    h_im = along_rows(cos_t, g_im) - along_rows(sin_t, g_re)
    spots = h_re * h_re + h_im * h_im
    coords = centred(SPOT)
    totals = jnp.sum(spots, axis=(3, 4))
    slope_x = jnp.sum(spots * coords[None, None, None, None, :], axis=(3, 4)) / totals
    slope_y = jnp.sum(spots * coords[None, None, None, :, None], axis=(3, 4)) / totals
    return jnp.stack([slope_x, slope_y], axis=-1).reshape(item_count, sub_rows * sub_cols * 2)


def pack_tiles(screens, owners, slots, pairs, my_tile, capacity):
    packed = []
    places = jnp.arange(capacity, dtype=jnp.int32)
    for frame, layer_idx in pairs:
        owner_rows = owners[frame, layer_idx]
        slot_rows = slots[frame, layer_idx]
        mine = owner_rows == my_tile
        order = jnp.cumsum(mine.astype(jnp.int32), axis=1) - 1
        picked = mine[:, None, :] & (order[:, None, :] == places[None, :, None])
        wanted = jnp.sum(jnp.where(picked, slot_rows[:, None, :], 0), axis=2)
        packed.append(jnp.take(screens[layer_idx], wanted, axis=0))
    return jnp.stack(packed, axis=1)


def unpack_tiles(received, owners, pairs, my_tile, capacity):
    results = []
    item_count = owners.shape[3]
    later = jnp.arange(item_count, dtype=jnp.int32)
    earlier_mask = later[None, :] < later[:, None]
    for position in range(len(pairs)):
        frame, layer_idx = pairs[position]
        mine = lax.dynamic_index_in_dim(owners[frame, layer_idx], my_tile, 0, keepdims=False)
        same_owner = mine[:, None] == mine[None, :]
        order = jnp.sum((same_owner & earlier_mask).astype(jnp.int32), axis=1)
        flat_index = mine * capacity + order
        layer_tiles = received[:, position].reshape(-1, received.shape[3], received.shape[4])
        results.append(jnp.take(layer_tiles, flat_index, axis=0).astype(jnp.float32))
    return results


def by_request(screens, tile_owner, tile_slot, commands_init, reconstructor, pattern):
    layer_total, tiles_here, slab_rows, tile_px = screens.shape
    frame_total = tile_owner.shape[0]
    tile_count = lax.axis_size("tile")
    rec_count = lax.axis_size("rec")
    my_tile = lax.axis_index("tile")
    my_rec = lax.axis_index("rec")
    capacity = max(2, 3 * ITEMS // (2 * tile_count))
    owners = tile_owner[..., 0].reshape(frame_total, layer_total, tile_count, ITEMS)
    slots = tile_slot.reshape(frame_total, layer_total, tile_count, ITEMS)
    influence_all = influence(tile_px, SUBPX, SUB)
    influence_rows = lax.dynamic_slice_in_dim(influence_all, my_rec * slab_rows, slab_rows, 0)
    lgs_places = (my_tile * LG_DEV + jnp.arange(LG_DEV, dtype=jnp.int32)) % PT
    sci_places = (my_tile * SC_DEV + jnp.arange(SC_DEV, dtype=jnp.int32)) % PT
    item_places = jnp.concatenate([lgs_places, sci_places])
    state = commands_init
    slope_frames = []
    science_frames = []
    for frame in range(frame_total):
        pairs = [(frame, layer_idx) for layer_idx in range(layer_total)]
        sending = pack_tiles(screens, owners, slots, pairs, my_tile, capacity)
        received = lax.all_to_all(sending, "tile", split_axis=0, concat_axis=0, tiled=True)
        pieces = unpack_tiles(received, owners, pairs, my_tile, capacity)
        phase = functools.reduce(jnp.add, pieces)
        full_commands = lax.all_gather(state, "rec", axis=0, tiled=True)
        mirror = full_commands.reshape(PT, SUB, SUB)
        chosen = jnp.take(mirror, item_places, axis=0)
        shapes = jnp.einsum(
            "xa,iab,yb->ixy", influence_rows, chosen, influence_all, precision=lax.Precision.HIGHEST
        )
        residual = phase - shapes
        science_frames.append(residual[LG_DEV:].astype(jnp.bfloat16))
        slopes = spot_slopes(residual[:LG_DEV])
        slope_frames.append(slopes)
        slopes_b = slopes.astype(jnp.bfloat16)
        everyone = lax.all_gather(slopes_b[None], ("tile", "rec"), axis=0, tiled=True)
        everyone = everyone.reshape(tile_count, rec_count, LG_DEV, -1).transpose(0, 2, 1, 3)
        everyone = everyone.reshape(tile_count * LG_DEV, -1)
        needed = jnp.take(everyone, pattern, axis=0)
        partial_rows = jnp.einsum(
            "ibcs,ibs->ic", reconstructor, needed, preferred_element_type=jnp.float32
        ).reshape(-1)
        state = state + loop_gain * lax.psum(partial_rows, "tile")
    return (jnp.stack(slope_frames, axis=0), jnp.stack(science_frames, axis=0), state)


def microseconds(t):
    return pl.CostEstimate(flops=0, bytes_accessed=int(t * 3.69e6), transcendentals=0)


def vmem():
    return pl.BlockSpec(memory_space=pltpu.VMEM)


def smem():
    return pl.BlockSpec(memory_space=pltpu.SMEM)


def constant_tables(slab_rows):
    f32, bf16 = np.float32, ml_dtypes.bfloat16
    turns = (np.arange(SPOT)[:, None] * np.arange(SUBPX)[None, :] % SPOT).astype(f32)
    turns = turns * f32(2.0 * math.pi / SPOT)
    cos_t, sin_t = np.cos(turns).astype(bf16).astype(f32), np.sin(turns).astype(bf16).astype(f32)
    cols = LANES // SUBPX
    eye_c = np.eye(cols, dtype=f32)
    cos_v, sin_v = np.kron(eye_c, cos_t.T), np.kron(eye_c, sin_t.T)
    along_v = np.block([[cos_v, -sin_v], [sin_v, cos_v]])
    rows = LG_DEV * slab_rows // SUBPX
    eye_r = np.eye(rows, dtype=f32)
    cos_u, sin_u = np.kron(eye_r, cos_t), np.kron(eye_r, sin_t)
    along_u = np.block([[cos_u, sin_u], [-sin_u, cos_u]])
    index = np.arange(SPOT)
    coord = (((index + SPOT // 2) % SPOT) - SPOT // 2).astype(f32) / SPOT
    groups = LANES // (2 * cols)
    total_n = np.zeros((cols, SPOT, groups, cols, 2), f32)
    coord_n = np.zeros((cols, SPOT, groups, cols, 2), f32)
    for b in range(cols):
        total_n[b, :, :, b, :] = 1.0
        coord_n[b, :, :, b, 0] = coord[:, None]
    over_n = np.concatenate([t.reshape(cols * SPOT, LANES) for t in (total_n, coord_n)], axis=1)
    sub_rows = slab_rows // SUBPX
    total_m = np.zeros((sub_rows, LG_DEV, LG_DEV, sub_rows, SPOT), f32)
    coord_m = np.zeros((sub_rows, LG_DEV, LG_DEV, sub_rows, SPOT), f32)
    for a in range(sub_rows):
        for i in range(LG_DEV):
            total_m[a, i, i, a, :] = 1.0
            coord_m[a, i, i, a, :] = coord
    over_m = np.concatenate([t.reshape(rows, rows * SPOT) for t in (total_m, coord_m)], axis=0)
    pixel = np.arange(LANES, dtype=f32)[:, None] + f32(0.5)
    centre = (np.arange(SUB, dtype=f32)[None, :] + f32(0.5)) * SUBPX
    infl = np.maximum(f32(0.0), f32(1.0) - np.abs(pixel - centre) / f32(SUBPX))
    per_row = LANES // CMD
    spread = np.tile(infl.T, (per_row * SUB, 1))
    keep = np.kron(np.eye(per_row * SUB, dtype=f32), np.ones((1, SUB), f32))
    half = along_v.shape[1] // 2
    exact = [along_v[:, :half], along_v[:, half:], along_u, over_n, over_m]
    return dict(exact=np.concatenate(exact, axis=0).astype(bf16), mirror=np.concatenate([keep, spread], axis=0))


def unpack_tables(exact, slab_rows):
    e_cols = 2 * LANES
    spots = LG_DEV * slab_rows // SUBPX * SPOT
    edges = [0, e_cols, 2 * e_cols, 2 * e_cols + 2 * spots, 3 * e_cols + 2 * spots, exact.shape[0]]
    v_re, v_im, u, over_n, over_m = [exact.at[pl.ds(a, b - a)] for a, b in zip(edges, edges[1:])]
    return v_re, v_im, u, over_n, over_m


def split_dot(exact, wide, left):
    high = wide.astype(jnp.bfloat16)
    low = (wide - high.astype(jnp.float32)).astype(jnp.bfloat16)
    dot = functools.partial(jnp.dot, preferred_element_type=jnp.float32)
    if left:
        return dot(exact, high) + dot(exact, low)
    return dot(high, exact) + dot(low, exact)


def sincos(x):
    turns = jnp.floor(x * np.float32(2.0 / math.pi) + 0.5)
    r = x - turns * np.float32(1.5703125)
    r = r - turns * np.float32(4.837512969970703125e-4)
    r = r - turns * np.float32(7.54978995489188216e-8)
    z = r * r
    s = ((np.float32(-1.9515295891e-4) * z + np.float32(8.3321608736e-3)) * z - np.float32(1.6666654611e-1)) * z * r + r
    c = ((np.float32(2.443315711809948e-5) * z - np.float32(1.388731625493765e-3)) * z + np.float32(4.166664568298827e-2)) * z * z - np.float32(0.5) * z + 1.0
    q = turns.astype(jnp.int32) & 3
    odd = (q & 1) == 1
    sine = jnp.where(odd, c, s)
    cosine = jnp.where(odd, s, c)
    sine = jnp.where(q >= 2, -sine, sine)
    cosine = jnp.where((q == 1) | (q == 2), -cosine, cosine)
    return sine, cosine


def row_weights(my_rec, slab_rows):
    groups = []
    for k in range(slab_rows // 8):
        g = my_rec * (slab_rows // 8) + k
        first = (g + 1) // 2 - 1
        x = (g * 8 + lax.broadcasted_iota(jnp.int32, (8, LANES), 0)).astype(jnp.float32) + 0.5
        pair = []
        for a in (first, first + 1):
            inside = (a >= 0) & (a < SUB)
            centre = (a.astype(jnp.float32) + 0.5) * SUBPX
            w = jnp.maximum(0.0, 1.0 - jnp.abs(x - centre) / SUBPX)
            pair.append((jnp.clip(a, 0, SUB - 1), jnp.where(inside, w, 0.0)))
        groups.append(pair)
    return groups


def column_profiles(c_rows, mirror):
    at = LANES // CMD * SUB
    keep, spread = mirror[:at], mirror[at:]
    picked = [jnp.broadcast_to(c_rows[i : i + 1], keep.shape) * keep for i in range(c_rows.shape[0])]
    return jnp.dot(
        jnp.concatenate(picked, axis=0), spread, preferred_element_type=jnp.float32, precision=lax.Precision.HIGHEST
    )


def stages(n):
    return [1 << k for k in range(n.bit_length() - 1)]


def destination(me, bits, k):
    return (k << bits) | (me & ((1 << bits) - 1))


def offer_kernel(frame, slots, screens, out):
    partner = lax.axis_index("tile") ^ 1
    for k in range(out.shape[0]):
        d = destination(partner, 1, k)
        for l in range(out.shape[1]):
            for i in range(LG_DEV):
                out[k, l, i] = screens[l, slots[frame, l, d * ITEMS + i]]


def stage_kernel(count, *refs):
    inputs, outs, sem = refs[:count], refs[count + 1 : -1], refs[-1]
    copies = [pltpu.make_async_copy(x, y, sem.at[i]) for i, (x, y) in enumerate(zip(inputs, outs))]
    for copy in copies:
        copy.start()
    for copy in copies:
        copy.wait()


def merge_kernel(frame, bits, owners, slots, mine, received, send, keep, *flags):
    me = lax.axis_index("tile")
    count, layers = send.shape[0], send.shape[1]
    other = 1 << (bits - 1)
    for out, side in ((keep, me), (send, me ^ (1 << bits))):
        for k in range(count):
            d = destination(side, bits + 1, k)
            j = d >> bits
            for l in range(layers):
                for i in range(LG_DEV):
                    g = d * ITEMS + i
                    theirs = ((owners[frame, l, g] ^ me) & other) != 0
                    ours = mine[l, slots[frame, l, g]] if bits == 1 else mine[j, l, i]
                    out[k, l, i] = jnp.where(theirs, received[j, l, i], ours)
    for flag in flags:
        for l in range(layers):
            for i in range(LG_DEV):
                theirs = ((owners[frame, l, me * ITEMS + i] ^ me) >> bits) & 1
                flag[pl.ds(i * layers + l, 1), :] = jnp.full((1, LANES), theirs).astype(jnp.float32)


def last_merge(kept, received, flags):
    layers = kept.shape[1]

    def tile(i, l):
        theirs = flags[pl.ds(i * layers + l, 1), :] > 0.5
        return jnp.where(theirs, received[0, l, i].astype(jnp.float32), kept[0, l, i].astype(jnp.float32))

    return [[tile(i, l) for l in range(layers)] for i in range(LG_DEV)]


def slopes_from(tiles, prof, table, payload, slopes):
    slab_rows = tiles[0][0].shape[0]
    v_re, v_im, along_u, over_n, over_m = unpack_tables(table, slab_rows)
    my_rec = lax.axis_index("rec")
    weights = row_weights(my_rec, slab_rows)
    rows = []
    for i in range(LG_DEV):
        phase = functools.reduce(jnp.add, [tile.astype(jnp.float32) for tile in tiles[i]])
        for k, ((a0, w0), (a1, w1)) in enumerate(weights):
            shape = w0 * prof[pl.ds(i * SUB + a0, 1), :] + w1 * prof[pl.ds(i * SUB + a1, 1), :]
            rows.append(phase[k * 8 : (k + 1) * 8] - shape)
    residual = jnp.concatenate(rows, axis=0)
    sine, cosine = sincos(residual)
    e = jnp.concatenate([cosine.astype(jnp.bfloat16), sine.astype(jnp.bfloat16)], axis=1)
    g = [jnp.dot(e, v[...], preferred_element_type=jnp.float32).astype(jnp.bfloat16) for v in (v_re, v_im)]
    g = jnp.concatenate(g, axis=0)
    h = jnp.dot(along_u[...], g, preferred_element_type=jnp.float32)
    n = h.shape[0] // 2
    h_re, h_im = h[:n], h[n:]
    spot = h_re * h_re + h_im * h_im
    sums = split_dot(over_m[...], split_dot(over_n[...], spot, False), True)
    m = sums.shape[0] // 2
    lane = lax.broadcasted_iota(jnp.int32, (m, LANES), 1)
    row = lax.broadcasted_iota(jnp.int32, (m, LANES), 0)
    top = sums[:m, LANES:] + jnp.where(lane % 2 == 1, sums[m:, :LANES], 0.0)
    ratio = top / sums[:m, :LANES]
    sub_rows = slab_rows // SUBPX
    ratio = jnp.where(lane // SUBPX == my_rec * sub_rows + row // LG_DEV, ratio, 0.0)
    own = ratio[:LG_DEV]
    for a in range(1, sub_rows):
        own = own + ratio[a * LG_DEV : (a + 1) * LG_DEV]
    slopes[...] = own
    payload[...] = jnp.broadcast_to(own.astype(jnp.bfloat16).astype(jnp.float32)[None], payload.shape)


def own_rows(my_tile):
    per_row = LANES // CMD
    need = LG_DEV // per_row
    return lax.rem(my_tile * need, PT // per_row), need


def first_slopes(kept, received, flags, mirror, table, *refs):
    *c_parts, payload, slopes, c, prof = refs
    my_tile, my_rec = lax.axis_index("tile"), lax.axis_index("rec")
    for k, part in enumerate(c_parts):
        c[pl.ds((my_rec ^ k) * part.shape[0], part.shape[0]), :] = part[...]
    base, need = own_rows(my_tile)
    prof[...] = column_profiles(c[pl.ds(base, need), :], mirror)
    tiles = last_merge(kept, received, flags)
    slopes_from(tiles, prof, table, payload, slopes)


def second_slopes(kept, received, flags, c_base, updates, mirror, table, payload, slopes, c_out, c_own, prof):
    my_tile = lax.axis_index("tile")
    c_out[...] = c_base[...] + loop_gain * jnp.sum(updates[...], axis=0).reshape(c_base.shape)
    c_own[...] = c_out[pl.ds(lax.axis_index("rec") * c_own.shape[0], c_own.shape[0]), :]
    base, need = own_rows(my_tile)
    prof[...] = column_profiles(c_out[pl.ds(base, need), :], mirror)
    tiles = last_merge(kept, received, flags)
    slopes_from(tiles, prof, table, payload, slopes)


def update_kernel(pattern, received, blocks, out, slopes):
    slopes[...] = jnp.sum(received[...], axis=1).reshape(slopes.shape)
    rows = []
    for i in range(blocks.shape[0]):
        total = None
        for b in range(blocks.shape[1]):
            vector = slopes[pl.ds(pattern[b, i], 1), :].astype(jnp.bfloat16)
            part = lax.dot_general(
                vector, blocks[i, b], (((1,), (1,)), ((), ())), preferred_element_type=jnp.float32
            )
            total = part if total is None else total + part
        rows.append(total)
    out[...] = jnp.broadcast_to(jnp.concatenate(rows, axis=0)[None], out.shape)


def science_kernel(places, c_first, c_second, mirror, gathered, out, store, ready, prof, sem):
    slab_rows = out.shape[2]
    my_tile, my_rec = lax.axis_index("tile"), lax.axis_index("rec")
    parts = sem.shape[0] - out.shape[0]
    size = store.shape[0] // parts
    copies = [
        pltpu.make_async_copy(gathered.at[pl.ds(i * size, size)], store.at[pl.ds(i * size, size)], sem.at[i])
        for i in range(parts)
    ]
    for copy in copies:
        copy.start()
    weights = row_weights(my_rec, slab_rows)
    profile_rows = PT * SUB
    for f, c in enumerate((c_first, c_second)):
        prof[pl.ds(f * profile_rows, profile_rows)] = column_profiles(c[...], mirror)
    for copy in copies:
        copy.wait()
    layers = places.shape[0] // (out.shape[0] * SC_DEV)
    start = lax.rem(my_tile * SC_DEV, PT)
    written = []
    for f in range(out.shape[0]):

        def some(qs):
            results = []
            for q in qs:
                row = f * profile_rows + lax.rem(start + q, PT) * SUB
                shapes = [
                    w0 * prof[pl.ds(row + a0, 1), :] + w1 * prof[pl.ds(row + a1, 1), :]
                    for (a0, w0), (a1, w1) in weights
                ]
                shape = jnp.concatenate(shapes, axis=0)
                both = not isinstance(q, int) or q + PT < SC_DEV
                for k in (q, q + PT)[: 1 + both]:
                    phase = None
                    for l in range(layers):
                        tile = store[places[(f * layers + l) * SC_DEV + k]].astype(jnp.float32)
                        phase = tile if phase is None else phase + tile
                    results.append((k, (phase - shape).astype(jnp.bfloat16)))
            for k, value in results:
                ready[f, k] = value

        twice = SC_DEV - PT
        together = 6

        @pl.loop(0, twice // together)
        def _(q):
            some([q * together + j for j in range(together)])

        some(range(twice // together * together, PT))
        written.append(pltpu.make_async_copy(ready.at[f], out.at[f], sem.at[parts + f]))
        written[-1].start()
    for copy in written:
        copy.wait()


def by_ring(screens, tile_owner, tile_slot, commands_init, reconstructor, pattern):
    layers, tiles_here, slab_rows, tile_px = screens.shape
    frames = tile_owner.shape[0]
    n = lax.axis_size("tile")
    rec_count = lax.axis_size("rec")
    everyone = n * rec_count
    my_tile, my_rec = lax.axis_index("tile"), lax.axis_index("rec")
    table = {k: jnp.asarray(v) for k, v in constant_tables(slab_rows).items()}
    block_rows = reconstructor.shape[0]
    f32 = jnp.float32
    limit = pltpu.CompilerParams(vmem_limit_bytes=24 << 20)

    ring = list(range(0, n, 2)) + list(range(n - 1, 0, -2))

    owners = tile_owner[..., 0]
    tables_in = [table["mirror"], table["exact"]]
    payload_out = [
        jax.ShapeDtypeStruct((everyone, LG_DEV, LANES), f32),
        jax.ShapeDtypeStruct((LG_DEV, LANES), f32),
    ]

    def exchange(payload):
        return lax.all_to_all(payload, ("tile", "rec"), split_axis=0, concat_axis=0, tiled=True)

    def updates_of(received, copies):
        received = received.reshape(n, rec_count, LG_DEV, LANES)
        return pl.pallas_call(
            update_kernel,
            out_shape=jax.ShapeDtypeStruct((copies, block_rows, LANES), f32),
            in_specs=[smem(), vmem(), vmem()],
            out_specs=vmem(),
            scratch_shapes=[pltpu.VMEM((n * LG_DEV, LANES), f32)],
            compiler_params=limit,
            cost_estimate=microseconds(2),
        )(pattern.T, received, reconstructor)

    wide = (layers, LG_DEV, slab_rows, tile_px)

    def tiles_of(*counts):
        shapes = [jax.ShapeDtypeStruct((c,) + wide, screens.dtype) for c in counts]
        return dict(out_shape=shapes, out_specs=[vmem()] * len(shapes))

    def swap(x, bit):
        return lax.ppermute(x, "tile", [(t, t ^ bit) for t in range(n)])

    def offer(frame, mine):
        (out,) = pl.pallas_call(
            functools.partial(offer_kernel, frame),
            in_specs=[smem(), vmem()],
            compiler_params=limit,
            **tiles_of(n // 2),
        )(tile_slot, mine)
        return out

    def merge(frame, bits, mine, received):
        count = n >> (bits + 1)
        outs = tiles_of(count, count)
        if count == 1:
            outs["out_shape"].append(jax.ShapeDtypeStruct((LG_DEV * layers, LANES), f32))
            outs["out_specs"].append(vmem())
        return pl.pallas_call(
            functools.partial(merge_kernel, frame, bits),
            in_specs=[smem()] * 2 + [vmem()] * 2,
            compiler_params=limit,
            **outs,
        )(owners, tile_slot, mine, received)

    def later(value, after):
        return lax.optimization_barrier((value, after))[0]

    def own_lanes(slopes):
        width = slab_rows // SUBPX * SUB * 2
        return lax.dynamic_slice_in_dim(slopes, my_rec * width, width, 1)

    last = n.bit_length() - 1
    c_own = commands_init.reshape(-1, LANES)
    c_parts = [c_own] + [
        lax.ppermute(c_own, "rec", [(r, r ^ k) for r in range(rec_count)]) for k in range(1, rec_count)
    ]
    wanted = offer(0, screens)
    second = offer(1, later(screens, wanted))
    arrays = tables_in + [c_own, screens]
    staged = pl.pallas_call(
        functools.partial(stage_kernel, len(arrays)),
        out_shape=[jax.ShapeDtypeStruct(x.shape, x.dtype) for x in arrays],
        in_specs=[pl.BlockSpec(memory_space=pl.ANY)] * (len(arrays) + 1),
        out_specs=[vmem()] * len(arrays),
        scratch_shapes=[pltpu.SemaphoreType.DMA((len(arrays),))],
        compiler_params=limit,
    )(*arrays, second)
    tables_in, c_parts[0] = staged[:2], staged[2]
    near = staged[3]
    kept, got = near, later(swap(wanted, 1), staged[0])
    for bits in range(1, last):
        send, kept, *flags = merge(0, bits, kept, got)
        got = swap(send, 1 << bits)
    guide = [(kept, got, *flags)]
    kept, got = near, later(swap(second, 1), send)
    for bits in range(1, last):
        send, kept, *flags = merge(1, bits, kept, got)
        got = swap(send, 1 << bits)
        if bits == 1:
            guide[0] = (later(guide[0][0], send), *guide[0][1:])
    guide.append((kept, got, *flags))

    gathered = lax.all_gather(later(screens, wanted), "tile", axis_index_groups=[ring])
    gathered = gathered.reshape(n * layers * tiles_here, slab_rows, tile_px)

    def own_items(x):
        return lax.dynamic_slice_in_dim(x, my_tile * ITEMS + LG_DEV, SC_DEV, 2)

    owner = own_items(owners)
    at = jnp.where(owner % 2 == 0, owner // 2, n - 1 - owner // 2) * layers
    places = (at + jnp.arange(layers, dtype=jnp.int32)[None, :, None]) * tiles_here + own_items(tile_slot)
    places = places.reshape(-1)

    payload, slopes_first, c0 = pl.pallas_call(
        first_slopes,
        out_shape=payload_out + [jax.ShapeDtypeStruct((rec_count * block_rows, LANES), f32)],
        in_specs=[vmem()] * (3 + rec_count + len(tables_in)),
        out_specs=[vmem()] * 3,
        scratch_shapes=[pltpu.VMEM((LG_DEV * SUB, LANES), f32)],
        compiler_params=limit,
        cost_estimate=microseconds(3),
    )(*guide[0], *tables_in, *c_parts)
    slopes_first = own_lanes(slopes_first)
    updates = updates_of(later(exchange(payload), send), everyone)
    updates = lax.all_to_all(updates, ("tile", "rec"), split_axis=0, concat_axis=0, tiled=True)
    updates = updates.reshape(n, rec_count, block_rows, LANES)

    payload, slopes_second, c1, mine = pl.pallas_call(
        second_slopes,
        out_shape=payload_out + [jax.ShapeDtypeStruct(r, f32) for r in (c0.shape, c_own.shape)],
        in_specs=[vmem()] * (5 + len(tables_in)),
        out_specs=[vmem()] * 4,
        scratch_shapes=[pltpu.VMEM((LG_DEV * SUB, LANES), f32)],
        compiler_params=limit,
        cost_estimate=microseconds(3),
    )(*guide[1], c0, updates, *tables_in)
    updates = updates_of(exchange(payload), n)
    updates = lax.all_to_all(updates, "tile", split_axis=0, concat_axis=0, tiled=True)
    science = pl.pallas_call(
        science_kernel,
        out_shape=jax.ShapeDtypeStruct((frames, SC_DEV, slab_rows, tile_px), jnp.bfloat16),
        in_specs=[smem()] + [vmem()] * 3 + [pl.BlockSpec(memory_space=pl.ANY)],
        out_specs=pl.BlockSpec(memory_space=pl.ANY),
        scratch_shapes=[
            pltpu.VMEM((n * layers * tiles_here, slab_rows, tile_px), screens.dtype),
            pltpu.VMEM((frames, SC_DEV, slab_rows, tile_px), jnp.bfloat16),
            pltpu.VMEM((frames * PT * SUB, LANES), f32),
            pltpu.SemaphoreType.DMA((n + frames,)),
        ],
        compiler_params=pltpu.CompilerParams(vmem_limit_bytes=60 << 20),
        cost_estimate=pl.CostEstimate(
            flops=8 * frames * SC_DEV * slab_rows * tile_px,
            bytes_accessed=2 * (n * layers * tiles_here + frames * SC_DEV) * slab_rows * tile_px,
            transcendentals=0,
        ),
    )(places, c0, c1, table["mirror"], gathered)
    updates = later(updates, science)
    c2 = mine + loop_gain * jnp.sum(updates, axis=0)
    return jnp.stack([slopes_first, own_lanes(slopes_second)], axis=0), science, c2.reshape(-1)


def per_device(screens, tile_owner, *rest):
    layers, tiles_here, _, _ = screens.shape
    frames, n = tile_owner.shape[0], lax.axis_size("tile")
    capacity = max(2, 3 * ITEMS // (2 * n))
    few = tiles_here <= frames * capacity and n & (n - 1) == 0 and frames == 2 and layers == 2
    return (by_ring if few else by_request)(screens, tile_owner, *rest)


def solution(mesh):
    placed = (
        P(None, "tile", "rec", None),
        P(),
        P(),
        P("rec"),
        P("rec", "tile", None, None),
        P("rec", "tile"),
    )
    return jax.shard_map(
        per_device,
        mesh=mesh,
        in_specs=placed,
        out_specs=(P(None, "tile", "rec"), P(None, "tile", "rec", None), P("rec")),
        check_vma=False,
    )
```

```python
import functools
import math

import jax
import jax.numpy as jnp
import ml_dtypes
import numpy as np
from jax import lax
from jax.experimental import pallas as pl
from jax.experimental.pallas import tpu as pltpu
from jax.sharding import PartitionSpec as P

SUBPX = 16
SPOT = 32
SUB = 8
PT = 64
LG_DEV = 4
SC_DEV = 124
ITEMS = LG_DEV + SC_DEV
LANES = 128
CMD = SUB * SUB

loop_gain = 0.5


def influence(tile_px, sub_px, sub_count):
    pixel = jnp.arange(tile_px, dtype=jnp.float32)[:, None] + 0.5
    centre = (jnp.arange(sub_count, dtype=jnp.float32)[None, :] + 0.5) * sub_px
    return jnp.maximum(0.0, 1.0 - jnp.abs(pixel - centre) / sub_px)


def tables(spot_px, sub_px):
    freq = jnp.arange(spot_px, dtype=jnp.int32)[:, None]
    pixel = jnp.arange(sub_px, dtype=jnp.int32)[None, :]
    turns = (freq * pixel % spot_px).astype(jnp.float32) * (2.0 * math.pi / spot_px)
    return (jnp.cos(turns).astype(jnp.bfloat16), jnp.sin(turns).astype(jnp.bfloat16))


def centred(spot_px):
    index = jnp.arange(spot_px, dtype=jnp.int32)
    return ((index + spot_px // 2) % spot_px - spot_px // 2).astype(jnp.float32) / spot_px


def along_pixels(values, table):
    return jnp.einsum("iaubv,nv->iaubn", values, table, preferred_element_type=jnp.float32)


def along_rows(table, values):
    return jnp.einsum("mu,iaubn->iabmn", table, values, preferred_element_type=jnp.float32)


def spot_slopes(residual):
    item_count, row_px, col_px = residual.shape
    sub_rows = row_px // SUBPX
    sub_cols = col_px // SUBPX
    cos_t, sin_t = tables(SPOT, SUBPX)
    pieces = residual.reshape(item_count, sub_rows, SUBPX, sub_cols, SUBPX)
    real_part = jnp.cos(pieces).astype(jnp.bfloat16)
    imag_part = jnp.sin(pieces).astype(jnp.bfloat16)
    g_re = (along_pixels(real_part, cos_t) + along_pixels(imag_part, sin_t)).astype(jnp.bfloat16)
    g_im = (along_pixels(imag_part, cos_t) - along_pixels(real_part, sin_t)).astype(jnp.bfloat16)
    h_re = along_rows(cos_t, g_re) + along_rows(sin_t, g_im)
    h_im = along_rows(cos_t, g_im) - along_rows(sin_t, g_re)
    spots = h_re * h_re + h_im * h_im
    coords = centred(SPOT)
    totals = jnp.sum(spots, axis=(3, 4))
    slope_x = jnp.sum(spots * coords[None, None, None, None, :], axis=(3, 4)) / totals
    slope_y = jnp.sum(spots * coords[None, None, None, :, None], axis=(3, 4)) / totals
    return jnp.stack([slope_x, slope_y], axis=-1).reshape(item_count, sub_rows * sub_cols * 2)


def pack_tiles(screens, owners, slots, pairs, my_tile, capacity):
    packed = []
    places = jnp.arange(capacity, dtype=jnp.int32)
    for frame, layer_idx in pairs:
        owner_rows = owners[frame, layer_idx]
        slot_rows = slots[frame, layer_idx]
        mine = owner_rows == my_tile
        order = jnp.cumsum(mine.astype(jnp.int32), axis=1) - 1
        picked = mine[:, None, :] & (order[:, None, :] == places[None, :, None])
        wanted = jnp.sum(jnp.where(picked, slot_rows[:, None, :], 0), axis=2)
        packed.append(jnp.take(screens[layer_idx], wanted, axis=0))
    return jnp.stack(packed, axis=1)


def unpack_tiles(received, owners, pairs, my_tile, capacity):
    results = []
    item_count = owners.shape[3]
    later = jnp.arange(item_count, dtype=jnp.int32)
    earlier_mask = later[None, :] < later[:, None]
    for position in range(len(pairs)):
        frame, layer_idx = pairs[position]
        mine = lax.dynamic_index_in_dim(owners[frame, layer_idx], my_tile, 0, keepdims=False)
        same_owner = mine[:, None] == mine[None, :]
        order = jnp.sum((same_owner & earlier_mask).astype(jnp.int32), axis=1)
        flat_index = mine * capacity + order
        layer_tiles = received[:, position].reshape(-1, received.shape[3], received.shape[4])
        results.append(jnp.take(layer_tiles, flat_index, axis=0).astype(jnp.float32))
    return results


def by_request(screens, tile_owner, tile_slot, commands_init, reconstructor, pattern):
    layer_total, tiles_here, slab_rows, tile_px = screens.shape
    frame_total = tile_owner.shape[0]
    tile_count = lax.axis_size("tile")
    rec_count = lax.axis_size("rec")
    my_tile = lax.axis_index("tile")
    my_rec = lax.axis_index("rec")
    capacity = max(2, 3 * ITEMS // (2 * tile_count))
    owners = tile_owner[..., 0].reshape(frame_total, layer_total, tile_count, ITEMS)
    slots = tile_slot.reshape(frame_total, layer_total, tile_count, ITEMS)
    influence_all = influence(tile_px, SUBPX, SUB)
    influence_rows = lax.dynamic_slice_in_dim(influence_all, my_rec * slab_rows, slab_rows, 0)
    lgs_places = (my_tile * LG_DEV + jnp.arange(LG_DEV, dtype=jnp.int32)) % PT
    sci_places = (my_tile * SC_DEV + jnp.arange(SC_DEV, dtype=jnp.int32)) % PT
    item_places = jnp.concatenate([lgs_places, sci_places])
    state = commands_init
    slope_frames = []
    science_frames = []
    for frame in range(frame_total):
        pairs = [(frame, layer_idx) for layer_idx in range(layer_total)]
        sending = pack_tiles(screens, owners, slots, pairs, my_tile, capacity)
        received = lax.all_to_all(sending, "tile", split_axis=0, concat_axis=0, tiled=True)
        pieces = unpack_tiles(received, owners, pairs, my_tile, capacity)
        phase = functools.reduce(jnp.add, pieces)
        full_commands = lax.all_gather(state, "rec", axis=0, tiled=True)
        mirror = full_commands.reshape(PT, SUB, SUB)
        chosen = jnp.take(mirror, item_places, axis=0)
        shapes = jnp.einsum(
            "xa,iab,yb->ixy", influence_rows, chosen, influence_all, precision=lax.Precision.HIGHEST
        )
        residual = phase - shapes
        science_frames.append(residual[LG_DEV:].astype(jnp.bfloat16))
        slopes = spot_slopes(residual[:LG_DEV])
        slope_frames.append(slopes)
        slopes_b = slopes.astype(jnp.bfloat16)
        everyone = lax.all_gather(slopes_b[None], ("tile", "rec"), axis=0, tiled=True)
        everyone = everyone.reshape(tile_count, rec_count, LG_DEV, -1).transpose(0, 2, 1, 3)
        everyone = everyone.reshape(tile_count * LG_DEV, -1)
        needed = jnp.take(everyone, pattern, axis=0)
        partial_rows = jnp.einsum(
            "ibcs,ibs->ic", reconstructor, needed, preferred_element_type=jnp.float32
        ).reshape(-1)
        state = state + loop_gain * lax.psum(partial_rows, "tile")
    return (jnp.stack(slope_frames, axis=0), jnp.stack(science_frames, axis=0), state)


def microseconds(t):
    return pl.CostEstimate(flops=0, bytes_accessed=int(t * 3.69e6), transcendentals=0)


def vmem():
    return pl.BlockSpec(memory_space=pltpu.VMEM)


def smem():
    return pl.BlockSpec(memory_space=pltpu.SMEM)


def constant_tables(slab_rows):
    f32, bf16 = np.float32, ml_dtypes.bfloat16
    turns = (np.arange(SPOT)[:, None] * np.arange(SUBPX)[None, :] % SPOT).astype(f32)
    turns = turns * f32(2.0 * math.pi / SPOT)
    cos_t, sin_t = np.cos(turns).astype(bf16).astype(f32), np.sin(turns).astype(bf16).astype(f32)
    cols = LANES // SUBPX
    eye_c = np.eye(cols, dtype=f32)
    cos_v, sin_v = np.kron(eye_c, cos_t.T), np.kron(eye_c, sin_t.T)
    along_v = np.block([[cos_v, -sin_v], [sin_v, cos_v]])
    rows = LG_DEV * slab_rows // SUBPX
    eye_r = np.eye(rows, dtype=f32)
    cos_u, sin_u = np.kron(eye_r, cos_t), np.kron(eye_r, sin_t)
    along_u = np.block([[cos_u, sin_u], [-sin_u, cos_u]])
    index = np.arange(SPOT)
    coord = (((index + SPOT // 2) % SPOT) - SPOT // 2).astype(f32) / SPOT
    groups = LANES // (2 * cols)
    total_n = np.zeros((cols, SPOT, groups, cols, 2), f32)
    coord_n = np.zeros((cols, SPOT, groups, cols, 2), f32)
    for b in range(cols):
        total_n[b, :, :, b, :] = 1.0
        coord_n[b, :, :, b, 0] = coord[:, None]
    over_n = np.concatenate([t.reshape(cols * SPOT, LANES) for t in (total_n, coord_n)], axis=1)
    sub_rows = slab_rows // SUBPX
    total_m = np.zeros((sub_rows, LG_DEV, LG_DEV, sub_rows, SPOT), f32)
    coord_m = np.zeros((sub_rows, LG_DEV, LG_DEV, sub_rows, SPOT), f32)
    for a in range(sub_rows):
        for i in range(LG_DEV):
            total_m[a, i, i, a, :] = 1.0
            coord_m[a, i, i, a, :] = coord
    over_m = np.concatenate([t.reshape(rows, rows * SPOT) for t in (total_m, coord_m)], axis=0)
    pixel = np.arange(LANES, dtype=f32)[:, None] + f32(0.5)
    centre = (np.arange(SUB, dtype=f32)[None, :] + f32(0.5)) * SUBPX
    infl = np.maximum(f32(0.0), f32(1.0) - np.abs(pixel - centre) / f32(SUBPX))
    per_row = LANES // CMD
    spread = np.tile(infl.T, (per_row * SUB, 1))
    keep = np.kron(np.eye(per_row * SUB, dtype=f32), np.ones((1, SUB), f32))
    half = along_v.shape[1] // 2
    exact = [along_v[:, :half], along_v[:, half:], along_u, over_n, over_m]
    return dict(exact=np.concatenate(exact, axis=0).astype(bf16), mirror=np.concatenate([keep, spread], axis=0))


def unpack_tables(exact, slab_rows):
    e_cols = 2 * LANES
    spots = LG_DEV * slab_rows // SUBPX * SPOT
    edges = [0, e_cols, 2 * e_cols, 2 * e_cols + 2 * spots, 3 * e_cols + 2 * spots, exact.shape[0]]
    v_re, v_im, u, over_n, over_m = [exact.at[pl.ds(a, b - a)] for a, b in zip(edges, edges[1:])]
    return v_re, v_im, u, over_n, over_m


def split_dot(exact, wide, left):
    high = wide.astype(jnp.bfloat16)
    low = (wide - high.astype(jnp.float32)).astype(jnp.bfloat16)
    dot = functools.partial(jnp.dot, preferred_element_type=jnp.float32)
    if left:
        return dot(exact, high) + dot(exact, low)
    return dot(high, exact) + dot(low, exact)


def sincos(x):
    turns = jnp.floor(x * np.float32(2.0 / math.pi) + 0.5)
    r = x - turns * np.float32(1.5703125)
    r = r - turns * np.float32(4.837512969970703125e-4)
    r = r - turns * np.float32(7.54978995489188216e-8)
    z = r * r
    s = ((np.float32(-1.9515295891e-4) * z + np.float32(8.3321608736e-3)) * z - np.float32(1.6666654611e-1)) * z * r + r
    c = ((np.float32(2.443315711809948e-5) * z - np.float32(1.388731625493765e-3)) * z + np.float32(4.166664568298827e-2)) * z * z - np.float32(0.5) * z + 1.0
    q = turns.astype(jnp.int32) & 3
    odd = (q & 1) == 1
    sine = jnp.where(odd, c, s)
    cosine = jnp.where(odd, s, c)
    sine = jnp.where(q >= 2, -sine, sine)
    cosine = jnp.where((q == 1) | (q == 2), -cosine, cosine)
    return sine, cosine


def row_weights(my_rec, slab_rows):
    groups = []
    for k in range(slab_rows // 8):
        g = my_rec * (slab_rows // 8) + k
        first = (g + 1) // 2 - 1
        x = (g * 8 + lax.broadcasted_iota(jnp.int32, (8, LANES), 0)).astype(jnp.float32) + 0.5
        pair = []
        for a in (first, first + 1):
            inside = (a >= 0) & (a < SUB)
            centre = (a.astype(jnp.float32) + 0.5) * SUBPX
            w = jnp.maximum(0.0, 1.0 - jnp.abs(x - centre) / SUBPX)
            pair.append((jnp.clip(a, 0, SUB - 1), jnp.where(inside, w, 0.0)))
        groups.append(pair)
    return groups


def column_profiles(c_rows, mirror):
    at = LANES // CMD * SUB
    keep, spread = mirror[:at], mirror[at:]
    picked = [jnp.broadcast_to(c_rows[i : i + 1], keep.shape) * keep for i in range(c_rows.shape[0])]
    return jnp.dot(
        jnp.concatenate(picked, axis=0), spread, preferred_element_type=jnp.float32, precision=lax.Precision.HIGHEST
    )


def stages(n):
    return [1 << k for k in range(n.bit_length() - 1)]


def destination(me, bits, k):
    return (k << bits) | (me & ((1 << bits) - 1))


def offer_kernel(frame, slots, screens, out):
    partner = lax.axis_index("tile") ^ 1
    for k in range(out.shape[0]):
        d = destination(partner, 1, k)
        for l in range(out.shape[1]):
            for i in range(LG_DEV):
                out[k, l, i] = screens[l, slots[frame, l, d * ITEMS + i]]


def stage_kernel(count, *refs):
    inputs, outs, sem = refs[:count], refs[count + 1 : -1], refs[-1]
    copies = [pltpu.make_async_copy(x, y, sem.at[i]) for i, (x, y) in enumerate(zip(inputs, outs))]
    for copy in copies:
        copy.start()
    for copy in copies:
        copy.wait()


def merge_kernel(frame, bits, owners, slots, mine, received, send, keep, *flags):
    me = lax.axis_index("tile")
    count, layers = send.shape[0], send.shape[1]
    other = 1 << (bits - 1)
    for out, side in ((keep, me), (send, me ^ (1 << bits))):
        for k in range(count):
            d = destination(side, bits + 1, k)
            j = d >> bits
            for l in range(layers):
                for i in range(LG_DEV):
                    g = d * ITEMS + i
                    theirs = ((owners[frame, l, g] ^ me) & other) != 0
                    ours = mine[l, slots[frame, l, g]] if bits == 1 else mine[j, l, i]
                    out[k, l, i] = jnp.where(theirs, received[j, l, i], ours)
    for flag in flags:
        for l in range(layers):
            for i in range(LG_DEV):
                theirs = ((owners[frame, l, me * ITEMS + i] ^ me) >> bits) & 1
                flag[pl.ds(i * layers + l, 1), :] = jnp.full((1, LANES), theirs).astype(jnp.float32)


def last_merge(kept, received, flags):
    layers = kept.shape[1]

    def tile(i, l):
        theirs = flags[pl.ds(i * layers + l, 1), :] > 0.5
        return jnp.where(theirs, received[0, l, i].astype(jnp.float32), kept[0, l, i].astype(jnp.float32))

    return [[tile(i, l) for l in range(layers)] for i in range(LG_DEV)]


def slopes_from(tiles, prof, table, payload, slopes):
    slab_rows = tiles[0][0].shape[0]
    v_re, v_im, along_u, over_n, over_m = unpack_tables(table, slab_rows)
    my_rec = lax.axis_index("rec")
    weights = row_weights(my_rec, slab_rows)
    rows = []
    for i in range(LG_DEV):
        phase = functools.reduce(jnp.add, [tile.astype(jnp.float32) for tile in tiles[i]])
        for k, ((a0, w0), (a1, w1)) in enumerate(weights):
            shape = w0 * prof[pl.ds(i * SUB + a0, 1), :] + w1 * prof[pl.ds(i * SUB + a1, 1), :]
            rows.append(phase[k * 8 : (k + 1) * 8] - shape)
    residual = jnp.concatenate(rows, axis=0)
    sine, cosine = sincos(residual)
    e = jnp.concatenate([cosine.astype(jnp.bfloat16), sine.astype(jnp.bfloat16)], axis=1)
    g = [jnp.dot(e, v[...], preferred_element_type=jnp.float32).astype(jnp.bfloat16) for v in (v_re, v_im)]
    g = jnp.concatenate(g, axis=0)
    h = jnp.dot(along_u[...], g, preferred_element_type=jnp.float32)
    n = h.shape[0] // 2
    h_re, h_im = h[:n], h[n:]
    spot = h_re * h_re + h_im * h_im
    sums = split_dot(over_m[...], split_dot(over_n[...], spot, False), True)
    m = sums.shape[0] // 2
    lane = lax.broadcasted_iota(jnp.int32, (m, LANES), 1)
    row = lax.broadcasted_iota(jnp.int32, (m, LANES), 0)
    top = sums[:m, LANES:] + jnp.where(lane % 2 == 1, sums[m:, :LANES], 0.0)
    ratio = top / sums[:m, :LANES]
    sub_rows = slab_rows // SUBPX
    ratio = jnp.where(lane // SUBPX == my_rec * sub_rows + row // LG_DEV, ratio, 0.0)
    own = ratio[:LG_DEV]
    for a in range(1, sub_rows):
        own = own + ratio[a * LG_DEV : (a + 1) * LG_DEV]
    width = slopes.shape[-1]
    slopes[...] = functools.reduce(jnp.add, [own[:, at : at + width] for at in range(0, LANES, width)])
    payload[...] = jnp.broadcast_to(own.astype(jnp.bfloat16).astype(jnp.float32)[None], payload.shape)


def own_rows(my_tile):
    per_row = LANES // CMD
    need = LG_DEV // per_row
    return lax.rem(my_tile * need, PT // per_row), need


def first_slopes(kept, received, flags, mirror, table, *refs):
    *c_parts, payload, slopes, c, prof = refs
    my_tile, my_rec = lax.axis_index("tile"), lax.axis_index("rec")
    for k, part in enumerate(c_parts):
        c[pl.ds((my_rec ^ k) * part.shape[0], part.shape[0]), :] = part[...]
    base, need = own_rows(my_tile)
    prof[...] = column_profiles(c[pl.ds(base, need), :], mirror)
    tiles = last_merge(kept, received, flags)
    slopes_from(tiles, prof, table, payload, slopes)


def second_slopes(kept, received, flags, c_base, updates, earlier, mirror, table, payload, slopes, c_out, c_own, prof):
    my_tile = lax.axis_index("tile")
    c_out[...] = c_base[...] + loop_gain * jnp.sum(updates[...], axis=0).reshape(c_base.shape)
    c_own[...] = c_out[pl.ds(lax.axis_index("rec") * c_own.shape[0], c_own.shape[0]), :]
    base, need = own_rows(my_tile)
    prof[...] = column_profiles(c_out[pl.ds(base, need), :], mirror)
    tiles = last_merge(kept, received, flags)
    slopes[0] = earlier[...]
    slopes_from(tiles, prof, table, payload, slopes.at[1])


def update_kernel(pattern, received, blocks, out, slopes):
    slopes[...] = jnp.sum(received[...], axis=1).reshape(slopes.shape)
    rows = []
    for i in range(blocks.shape[0]):
        total = None
        for b in range(blocks.shape[1]):
            vector = slopes[pl.ds(pattern[b, i], 1), :].astype(jnp.bfloat16)
            part = lax.dot_general(
                vector, blocks[i, b], (((1,), (1,)), ((), ())), preferred_element_type=jnp.float32
            )
            total = part if total is None else total + part
        rows.append(total)
    out[...] = jnp.broadcast_to(jnp.concatenate(rows, axis=0)[None], out.shape)


def science_kernel(places, c_first, c_second, mirror, gathered, out, store, ready, prof, sem):
    slab_rows = out.shape[2]
    my_tile, my_rec = lax.axis_index("tile"), lax.axis_index("rec")
    parts = sem.shape[0] - out.shape[0]
    size = store.shape[0] // parts
    copies = [
        pltpu.make_async_copy(gathered.at[pl.ds(i * size, size)], store.at[pl.ds(i * size, size)], sem.at[i])
        for i in range(parts)
    ]
    for copy in copies:
        copy.start()
    weights = row_weights(my_rec, slab_rows)
    profile_rows = PT * SUB
    for f, c in enumerate((c_first, c_second)):
        prof[pl.ds(f * profile_rows, profile_rows)] = column_profiles(c[...], mirror)
    for copy in copies:
        copy.wait()
    layers = places.shape[0] // (out.shape[0] * SC_DEV)
    start = lax.rem(my_tile * SC_DEV, PT)
    written = []
    for f in range(out.shape[0]):

        def some(qs):
            results = []
            for q in qs:
                row = f * profile_rows + lax.rem(start + q, PT) * SUB
                shapes = [
                    w0 * prof[pl.ds(row + a0, 1), :] + w1 * prof[pl.ds(row + a1, 1), :]
                    for (a0, w0), (a1, w1) in weights
                ]
                shape = jnp.concatenate(shapes, axis=0)
                both = not isinstance(q, int) or q + PT < SC_DEV
                for k in (q, q + PT)[: 1 + both]:
                    phase = None
                    for l in range(layers):
                        tile = store[places[(f * layers + l) * SC_DEV + k]].astype(jnp.float32)
                        phase = tile if phase is None else phase + tile
                    results.append((k, (phase - shape).astype(jnp.bfloat16)))
            for k, value in results:
                ready[f, k] = value

        twice = SC_DEV - PT
        together = 6

        @pl.loop(0, twice // together)
        def _(q):
            some([q * together + j for j in range(together)])

        some(range(twice // together * together, PT))
        written.append(pltpu.make_async_copy(ready.at[f], out.at[f], sem.at[parts + f]))
        written[-1].start()
    for copy in written:
        copy.wait()


def by_ring(screens, tile_owner, tile_slot, commands_init, reconstructor, pattern):
    layers, tiles_here, slab_rows, tile_px = screens.shape
    frames = tile_owner.shape[0]
    n = lax.axis_size("tile")
    rec_count = lax.axis_size("rec")
    everyone = n * rec_count
    my_tile, my_rec = lax.axis_index("tile"), lax.axis_index("rec")
    table = {k: jnp.asarray(v) for k, v in constant_tables(slab_rows).items()}
    block_rows = reconstructor.shape[0]
    f32 = jnp.float32
    limit = pltpu.CompilerParams(vmem_limit_bytes=24 << 20)

    ring = list(range(0, n, 2)) + list(range(n - 1, 0, -2))

    owners = tile_owner[..., 0]
    tables_in = [table["mirror"], table["exact"]]
    width = slab_rows // SUBPX * SUB * 2
    payload_out = [
        jax.ShapeDtypeStruct((everyone, LG_DEV, LANES), f32),
        jax.ShapeDtypeStruct((LG_DEV, width), f32),
    ]

    def exchange(payload):
        return lax.all_to_all(payload, ("tile", "rec"), split_axis=0, concat_axis=0, tiled=True)

    def updates_of(received, copies):
        received = received.reshape(n, rec_count, LG_DEV, LANES)
        return pl.pallas_call(
            update_kernel,
            out_shape=jax.ShapeDtypeStruct((copies, block_rows, LANES), f32),
            in_specs=[smem(), vmem(), vmem()],
            out_specs=vmem(),
            scratch_shapes=[pltpu.VMEM((n * LG_DEV, LANES), f32)],
            compiler_params=limit,
            cost_estimate=microseconds(2),
        )(pattern.T, received, reconstructor)

    wide = (layers, LG_DEV, slab_rows, tile_px)

    def tiles_of(*counts):
        shapes = [jax.ShapeDtypeStruct((c,) + wide, screens.dtype) for c in counts]
        return dict(out_shape=shapes, out_specs=[vmem()] * len(shapes))

    def swap(x, bit):
        return lax.ppermute(x, "tile", [(t, t ^ bit) for t in range(n)])

    def offer(frame, mine):
        (out,) = pl.pallas_call(
            functools.partial(offer_kernel, frame),
            in_specs=[smem(), vmem()],
            compiler_params=limit,
            **tiles_of(n // 2),
        )(tile_slot, mine)
        return out

    def merge(frame, bits, mine, received):
        count = n >> (bits + 1)
        outs = tiles_of(count, count)
        if count == 1:
            outs["out_shape"].append(jax.ShapeDtypeStruct((LG_DEV * layers, LANES), f32))
            outs["out_specs"].append(vmem())
        return pl.pallas_call(
            functools.partial(merge_kernel, frame, bits),
            in_specs=[smem()] * 2 + [vmem()] * 2,
            compiler_params=limit,
            **outs,
        )(owners, tile_slot, mine, received)

    def later(value, after):
        return lax.optimization_barrier((value, after))[0]

    last = n.bit_length() - 1
    c_own = commands_init.reshape(-1, LANES)
    c_parts = [c_own] + [
        lax.ppermute(c_own, "rec", [(r, r ^ k) for r in range(rec_count)]) for k in range(1, rec_count)
    ]
    wanted = offer(0, screens)
    second = offer(1, later(screens, wanted))
    arrays = tables_in + [c_own, screens]
    staged = pl.pallas_call(
        functools.partial(stage_kernel, len(arrays)),
        out_shape=[jax.ShapeDtypeStruct(x.shape, x.dtype) for x in arrays],
        in_specs=[pl.BlockSpec(memory_space=pl.ANY)] * (len(arrays) + 1),
        out_specs=[vmem()] * len(arrays),
        scratch_shapes=[pltpu.SemaphoreType.DMA((len(arrays),))],
        compiler_params=limit,
    )(*arrays, second)
    tables_in, c_parts[0] = staged[:2], staged[2]
    near = staged[3]
    kept, got = near, later(swap(wanted, 1), staged[0])
    for bits in range(1, last):
        send, kept, *flags = merge(0, bits, kept, got)
        got = swap(send, 1 << bits)
    guide = [(kept, got, *flags)]
    kept, got = near, later(swap(second, 1), send)
    for bits in range(1, last):
        send, kept, *flags = merge(1, bits, kept, got)
        got = swap(send, 1 << bits)
        if bits == 1:
            guide[0] = (later(guide[0][0], send), *guide[0][1:])
    guide.append((kept, got, *flags))

    gathered = lax.all_gather(later(screens, wanted), "tile", axis_index_groups=[ring])
    gathered = gathered.reshape(n * layers * tiles_here, slab_rows, tile_px)

    def own_items(x):
        return lax.dynamic_slice_in_dim(x, my_tile * ITEMS + LG_DEV, SC_DEV, 2)

    owner = own_items(owners)
    at = jnp.where(owner % 2 == 0, owner // 2, n - 1 - owner // 2) * layers
    places = (at + jnp.arange(layers, dtype=jnp.int32)[None, :, None]) * tiles_here + own_items(tile_slot)
    places = places.reshape(-1)

    payload, slopes_first, c0 = pl.pallas_call(
        first_slopes,
        out_shape=payload_out + [jax.ShapeDtypeStruct((rec_count * block_rows, LANES), f32)],
        in_specs=[vmem()] * (3 + rec_count + len(tables_in)),
        out_specs=[vmem()] * 3,
        scratch_shapes=[pltpu.VMEM((LG_DEV * SUB, LANES), f32)],
        compiler_params=limit,
        cost_estimate=microseconds(3),
    )(*guide[0], *tables_in, *c_parts)
    updates = updates_of(later(exchange(payload), send), everyone)
    updates = lax.all_to_all(updates, ("tile", "rec"), split_axis=0, concat_axis=0, tiled=True)
    updates = updates.reshape(n, rec_count, block_rows, LANES)

    payload, slopes, c1, mine = pl.pallas_call(
        second_slopes,
        out_shape=payload_out[:1] + [jax.ShapeDtypeStruct(r, f32) for r in ((frames, LG_DEV, width), c0.shape, c_own.shape)],
        in_specs=[vmem()] * (6 + len(tables_in)),
        out_specs=[vmem()] * 4,
        scratch_shapes=[pltpu.VMEM((LG_DEV * SUB, LANES), f32)],
        compiler_params=limit,
        cost_estimate=microseconds(3),
    )(*guide[1], c0, updates, slopes_first, *tables_in)
    updates = updates_of(exchange(payload), n)
    updates = lax.all_to_all(updates, "tile", split_axis=0, concat_axis=0, tiled=True)
    science = pl.pallas_call(
        science_kernel,
        out_shape=jax.ShapeDtypeStruct((frames, SC_DEV, slab_rows, tile_px), jnp.bfloat16),
        in_specs=[smem()] + [vmem()] * 3 + [pl.BlockSpec(memory_space=pl.ANY)],
        out_specs=pl.BlockSpec(memory_space=pl.ANY),
        scratch_shapes=[
            pltpu.VMEM((n * layers * tiles_here, slab_rows, tile_px), screens.dtype),
            pltpu.VMEM((frames, SC_DEV, slab_rows, tile_px), jnp.bfloat16),
            pltpu.VMEM((frames * PT * SUB, LANES), f32),
            pltpu.SemaphoreType.DMA((n + frames,)),
        ],
        compiler_params=pltpu.CompilerParams(vmem_limit_bytes=60 << 20),
        cost_estimate=pl.CostEstimate(
            flops=8 * frames * SC_DEV * slab_rows * tile_px,
            bytes_accessed=2 * (n * layers * tiles_here + frames * SC_DEV) * slab_rows * tile_px,
            transcendentals=0,
        ),
    )(places, c0, c1, table["mirror"], gathered)
    updates = later(updates, science)
    c2 = mine + loop_gain * jnp.sum(updates, axis=0)
    return slopes, science, c2.reshape(-1)


def per_device(screens, tile_owner, *rest):
    layers, tiles_here, _, _ = screens.shape
    frames, n = tile_owner.shape[0], lax.axis_size("tile")
    capacity = max(2, 3 * ITEMS // (2 * n))
    few = tiles_here <= frames * capacity and n & (n - 1) == 0 and frames == 2 and layers == 2
    return (by_ring if few else by_request)(screens, tile_owner, *rest)


def solution(mesh):
    placed = (
        P(None, "tile", "rec", None),
        P(),
        P(),
        P("rec"),
        P("rec", "tile", None, None),
        P("rec", "tile"),
    )
    return jax.shard_map(
        per_device,
        mesh=mesh,
        in_specs=placed,
        out_specs=(P(None, "tile", "rec"), P(None, "tile", "rec", None), P("rec")),
        check_vma=False,
    )
```

```python
import functools
import math

import jax
import jax.numpy as jnp
import ml_dtypes
import numpy as np
from jax import lax
from jax.experimental import pallas as pl
from jax.experimental.pallas import tpu as pltpu
from jax.sharding import PartitionSpec as P

SUBPX = 16
SPOT = 32
SUB = 8
PT = 64
LG_DEV = 4
SC_DEV = 124
ITEMS = LG_DEV + SC_DEV
LANES = 128
CMD = SUB * SUB

loop_gain = 0.5


def influence(tile_px, sub_px, sub_count):
    pixel = jnp.arange(tile_px, dtype=jnp.float32)[:, None] + 0.5
    centre = (jnp.arange(sub_count, dtype=jnp.float32)[None, :] + 0.5) * sub_px
    return jnp.maximum(0.0, 1.0 - jnp.abs(pixel - centre) / sub_px)


def tables(spot_px, sub_px):
    freq = jnp.arange(spot_px, dtype=jnp.int32)[:, None]
    pixel = jnp.arange(sub_px, dtype=jnp.int32)[None, :]
    turns = (freq * pixel % spot_px).astype(jnp.float32) * (2.0 * math.pi / spot_px)
    return (jnp.cos(turns).astype(jnp.bfloat16), jnp.sin(turns).astype(jnp.bfloat16))


def centred(spot_px):
    index = jnp.arange(spot_px, dtype=jnp.int32)
    return ((index + spot_px // 2) % spot_px - spot_px // 2).astype(jnp.float32) / spot_px


def along_pixels(values, table):
    return jnp.einsum("iaubv,nv->iaubn", values, table, preferred_element_type=jnp.float32)


def along_rows(table, values):
    return jnp.einsum("mu,iaubn->iabmn", table, values, preferred_element_type=jnp.float32)


def spot_slopes(residual):
    item_count, row_px, col_px = residual.shape
    sub_rows = row_px // SUBPX
    sub_cols = col_px // SUBPX
    cos_t, sin_t = tables(SPOT, SUBPX)
    pieces = residual.reshape(item_count, sub_rows, SUBPX, sub_cols, SUBPX)
    real_part = jnp.cos(pieces).astype(jnp.bfloat16)
    imag_part = jnp.sin(pieces).astype(jnp.bfloat16)
    g_re = (along_pixels(real_part, cos_t) + along_pixels(imag_part, sin_t)).astype(jnp.bfloat16)
    g_im = (along_pixels(imag_part, cos_t) - along_pixels(real_part, sin_t)).astype(jnp.bfloat16)
    h_re = along_rows(cos_t, g_re) + along_rows(sin_t, g_im)
    h_im = along_rows(cos_t, g_im) - along_rows(sin_t, g_re)
    spots = h_re * h_re + h_im * h_im
    coords = centred(SPOT)
    totals = jnp.sum(spots, axis=(3, 4))
    slope_x = jnp.sum(spots * coords[None, None, None, None, :], axis=(3, 4)) / totals
    slope_y = jnp.sum(spots * coords[None, None, None, :, None], axis=(3, 4)) / totals
    return jnp.stack([slope_x, slope_y], axis=-1).reshape(item_count, sub_rows * sub_cols * 2)


def pack_tiles(screens, owners, slots, pairs, my_tile, capacity):
    packed = []
    places = jnp.arange(capacity, dtype=jnp.int32)
    for frame, layer_idx in pairs:
        owner_rows = owners[frame, layer_idx]
        slot_rows = slots[frame, layer_idx]
        mine = owner_rows == my_tile
        order = jnp.cumsum(mine.astype(jnp.int32), axis=1) - 1
        picked = mine[:, None, :] & (order[:, None, :] == places[None, :, None])
        wanted = jnp.sum(jnp.where(picked, slot_rows[:, None, :], 0), axis=2)
        packed.append(jnp.take(screens[layer_idx], wanted, axis=0))
    return jnp.stack(packed, axis=1)


def unpack_tiles(received, owners, pairs, my_tile, capacity):
    results = []
    item_count = owners.shape[3]
    later = jnp.arange(item_count, dtype=jnp.int32)
    earlier_mask = later[None, :] < later[:, None]
    for position in range(len(pairs)):
        frame, layer_idx = pairs[position]
        mine = lax.dynamic_index_in_dim(owners[frame, layer_idx], my_tile, 0, keepdims=False)
        same_owner = mine[:, None] == mine[None, :]
        order = jnp.sum((same_owner & earlier_mask).astype(jnp.int32), axis=1)
        flat_index = mine * capacity + order
        layer_tiles = received[:, position].reshape(-1, received.shape[3], received.shape[4])
        results.append(jnp.take(layer_tiles, flat_index, axis=0).astype(jnp.float32))
    return results


def by_request(screens, tile_owner, tile_slot, commands_init, reconstructor, pattern):
    layer_total, tiles_here, slab_rows, tile_px = screens.shape
    frame_total = tile_owner.shape[0]
    tile_count = lax.axis_size("tile")
    rec_count = lax.axis_size("rec")
    my_tile = lax.axis_index("tile")
    my_rec = lax.axis_index("rec")
    capacity = max(2, 3 * ITEMS // (2 * tile_count))
    owners = tile_owner[..., 0].reshape(frame_total, layer_total, tile_count, ITEMS)
    slots = tile_slot.reshape(frame_total, layer_total, tile_count, ITEMS)
    influence_all = influence(tile_px, SUBPX, SUB)
    influence_rows = lax.dynamic_slice_in_dim(influence_all, my_rec * slab_rows, slab_rows, 0)
    lgs_places = (my_tile * LG_DEV + jnp.arange(LG_DEV, dtype=jnp.int32)) % PT
    sci_places = (my_tile * SC_DEV + jnp.arange(SC_DEV, dtype=jnp.int32)) % PT
    item_places = jnp.concatenate([lgs_places, sci_places])
    state = commands_init
    slope_frames = []
    science_frames = []
    for frame in range(frame_total):
        pairs = [(frame, layer_idx) for layer_idx in range(layer_total)]
        sending = pack_tiles(screens, owners, slots, pairs, my_tile, capacity)
        received = lax.all_to_all(sending, "tile", split_axis=0, concat_axis=0, tiled=True)
        pieces = unpack_tiles(received, owners, pairs, my_tile, capacity)
        phase = functools.reduce(jnp.add, pieces)
        full_commands = lax.all_gather(state, "rec", axis=0, tiled=True)
        mirror = full_commands.reshape(PT, SUB, SUB)
        chosen = jnp.take(mirror, item_places, axis=0)
        shapes = jnp.einsum(
            "xa,iab,yb->ixy", influence_rows, chosen, influence_all, precision=lax.Precision.HIGHEST
        )
        residual = phase - shapes
        science_frames.append(residual[LG_DEV:].astype(jnp.bfloat16))
        slopes = spot_slopes(residual[:LG_DEV])
        slope_frames.append(slopes)
        slopes_b = slopes.astype(jnp.bfloat16)
        everyone = lax.all_gather(slopes_b[None], ("tile", "rec"), axis=0, tiled=True)
        everyone = everyone.reshape(tile_count, rec_count, LG_DEV, -1).transpose(0, 2, 1, 3)
        everyone = everyone.reshape(tile_count * LG_DEV, -1)
        needed = jnp.take(everyone, pattern, axis=0)
        partial_rows = jnp.einsum(
            "ibcs,ibs->ic", reconstructor, needed, preferred_element_type=jnp.float32
        ).reshape(-1)
        state = state + loop_gain * lax.psum(partial_rows, "tile")
    return (jnp.stack(slope_frames, axis=0), jnp.stack(science_frames, axis=0), state)


def microseconds(t):
    return pl.CostEstimate(flops=0, bytes_accessed=int(t * 3.69e6), transcendentals=0)


def vmem():
    return pl.BlockSpec(memory_space=pltpu.VMEM)


def smem():
    return pl.BlockSpec(memory_space=pltpu.SMEM)


def constant_tables(slab_rows):
    f32, bf16 = np.float32, ml_dtypes.bfloat16
    turns = (np.arange(SPOT)[:, None] * np.arange(SUBPX)[None, :] % SPOT).astype(f32)
    turns = turns * f32(2.0 * math.pi / SPOT)
    cos_t, sin_t = np.cos(turns).astype(bf16).astype(f32), np.sin(turns).astype(bf16).astype(f32)
    cols = LANES // SUBPX
    eye_c = np.eye(cols, dtype=f32)
    cos_v, sin_v = np.kron(eye_c, cos_t.T), np.kron(eye_c, sin_t.T)
    along_v = np.block([[cos_v, -sin_v], [sin_v, cos_v]])
    rows = LG_DEV * slab_rows // SUBPX
    eye_r = np.eye(rows, dtype=f32)
    cos_u, sin_u = np.kron(eye_r, cos_t), np.kron(eye_r, sin_t)
    along_u = np.block([[cos_u, sin_u], [-sin_u, cos_u]])
    index = np.arange(SPOT)
    coord = (((index + SPOT // 2) % SPOT) - SPOT // 2).astype(f32) / SPOT
    groups = LANES // (2 * cols)
    total_n = np.zeros((cols, SPOT, groups, cols, 2), f32)
    coord_n = np.zeros((cols, SPOT, groups, cols, 2), f32)
    for b in range(cols):
        total_n[b, :, :, b, :] = 1.0
        coord_n[b, :, :, b, 0] = coord[:, None]
    over_n = np.concatenate([t.reshape(cols * SPOT, LANES) for t in (total_n, coord_n)], axis=1)
    sub_rows = slab_rows // SUBPX
    total_m = np.zeros((sub_rows, LG_DEV, LG_DEV, sub_rows, SPOT), f32)
    coord_m = np.zeros((sub_rows, LG_DEV, LG_DEV, sub_rows, SPOT), f32)
    for a in range(sub_rows):
        for i in range(LG_DEV):
            total_m[a, i, i, a, :] = 1.0
            coord_m[a, i, i, a, :] = coord
    over_m = np.concatenate([t.reshape(rows, rows * SPOT) for t in (total_m, coord_m)], axis=0)
    pixel = np.arange(LANES, dtype=f32)[:, None] + f32(0.5)
    centre = (np.arange(SUB, dtype=f32)[None, :] + f32(0.5)) * SUBPX
    infl = np.maximum(f32(0.0), f32(1.0) - np.abs(pixel - centre) / f32(SUBPX))
    per_row = LANES // CMD
    spread = np.tile(infl.T, (per_row * SUB, 1))
    keep = np.kron(np.eye(per_row * SUB, dtype=f32), np.ones((1, SUB), f32))
    half = along_v.shape[1] // 2
    exact = [along_v[:, :half], along_v[:, half:], along_u, over_n, over_m]
    return dict(exact=np.concatenate(exact, axis=0).astype(bf16), mirror=np.concatenate([keep, spread], axis=0))


def unpack_tables(exact, slab_rows):
    e_cols = 2 * LANES
    spots = LG_DEV * slab_rows // SUBPX * SPOT
    edges = [0, e_cols, 2 * e_cols, 2 * e_cols + 2 * spots, 3 * e_cols + 2 * spots, exact.shape[0]]
    v_re, v_im, u, over_n, over_m = [exact.at[pl.ds(a, b - a)] for a, b in zip(edges, edges[1:])]
    return v_re, v_im, u, over_n, over_m


def split_dot(exact, wide, left):
    high = wide.astype(jnp.bfloat16)
    low = (wide - high.astype(jnp.float32)).astype(jnp.bfloat16)
    dot = functools.partial(jnp.dot, preferred_element_type=jnp.float32)
    if left:
        return dot(exact, high) + dot(exact, low)
    return dot(high, exact) + dot(low, exact)


def sincos(x):
    turns = jnp.floor(x * np.float32(2.0 / math.pi) + 0.5)
    r = x - turns * np.float32(1.5703125)
    r = r - turns * np.float32(4.837512969970703125e-4)
    r = r - turns * np.float32(7.54978995489188216e-8)
    z = r * r
    s = ((np.float32(-1.9515295891e-4) * z + np.float32(8.3321608736e-3)) * z - np.float32(1.6666654611e-1)) * z * r + r
    c = ((np.float32(2.443315711809948e-5) * z - np.float32(1.388731625493765e-3)) * z + np.float32(4.166664568298827e-2)) * z * z - np.float32(0.5) * z + 1.0
    q = turns.astype(jnp.int32) & 3
    odd = (q & 1) == 1
    sine = jnp.where(odd, c, s)
    cosine = jnp.where(odd, s, c)
    sine = jnp.where(q >= 2, -sine, sine)
    cosine = jnp.where((q == 1) | (q == 2), -cosine, cosine)
    return sine, cosine


def row_weights(my_rec, slab_rows):
    groups = []
    for k in range(slab_rows // 8):
        g = my_rec * (slab_rows // 8) + k
        first = (g + 1) // 2 - 1
        x = (g * 8 + lax.broadcasted_iota(jnp.int32, (8, LANES), 0)).astype(jnp.float32) + 0.5
        pair = []
        for a in (first, first + 1):
            inside = (a >= 0) & (a < SUB)
            centre = (a.astype(jnp.float32) + 0.5) * SUBPX
            w = jnp.maximum(0.0, 1.0 - jnp.abs(x - centre) / SUBPX)
            pair.append((jnp.clip(a, 0, SUB - 1), jnp.where(inside, w, 0.0)))
        groups.append(pair)
    return groups


def column_profiles(c_rows, mirror):
    at = LANES // CMD * SUB
    keep, spread = mirror[:at], mirror[at:]
    picked = [jnp.broadcast_to(c_rows[i : i + 1], keep.shape) * keep for i in range(c_rows.shape[0])]
    return jnp.dot(
        jnp.concatenate(picked, axis=0), spread, preferred_element_type=jnp.float32, precision=lax.Precision.HIGHEST
    )


def stages(n):
    return [1 << k for k in range(n.bit_length() - 1)]


def destination(me, bits, k):
    return (k << bits) | (me & ((1 << bits) - 1))


def offer_kernel(frame, slots, screens, out):
    partner = lax.axis_index("tile") ^ 1
    for k in range(out.shape[0]):
        d = destination(partner, 1, k)
        for l in range(out.shape[1]):
            for i in range(LG_DEV):
                out[k, l, i] = screens[l, slots[frame, l, d * ITEMS + i]]


def stage_kernel(count, *refs):
    inputs, outs, sem = refs[:count], refs[count + 1 : -1], refs[-1]
    copies = [pltpu.make_async_copy(x, y, sem.at[i]) for i, (x, y) in enumerate(zip(inputs, outs))]
    for copy in copies:
        copy.start()
    for copy in copies:
        copy.wait()


def merge_kernel(frame, bits, owners, slots, mine, received, send, keep, *flags):
    me = lax.axis_index("tile")
    count, layers = send.shape[0], send.shape[1]
    other = 1 << (bits - 1)
    for out, side in ((keep, me), (send, me ^ (1 << bits))):
        for k in range(count):
            d = destination(side, bits + 1, k)
            j = d >> bits
            for l in range(layers):
                for i in range(LG_DEV):
                    g = d * ITEMS + i
                    theirs = ((owners[frame, l, g] ^ me) & other) != 0
                    ours = mine[l, slots[frame, l, g]] if bits == 1 else mine[j, l, i]
                    out[k, l, i] = jnp.where(theirs, received[j, l, i], ours)
    for flag in flags:
        for l in range(layers):
            for i in range(LG_DEV):
                theirs = ((owners[frame, l, me * ITEMS + i] ^ me) >> bits) & 1
                flag[pl.ds(i * layers + l, 1), :] = jnp.full((1, LANES), theirs).astype(jnp.float32)


def last_merge(kept, received, flags):
    layers = kept.shape[1]

    def tile(i, l):
        theirs = flags[pl.ds(i * layers + l, 1), :] > 0.5
        return jnp.where(theirs, received[0, l, i].astype(jnp.float32), kept[0, l, i].astype(jnp.float32))

    return [[tile(i, l) for l in range(layers)] for i in range(LG_DEV)]


def slopes_from(tiles, prof, table, payload, slopes):
    slab_rows = tiles[0][0].shape[0]
    v_re, v_im, along_u, over_n, over_m = unpack_tables(table, slab_rows)
    my_rec = lax.axis_index("rec")
    weights = row_weights(my_rec, slab_rows)
    rows = []
    for i in range(LG_DEV):
        phase = functools.reduce(jnp.add, [tile.astype(jnp.float32) for tile in tiles[i]])
        for k, ((a0, w0), (a1, w1)) in enumerate(weights):
            shape = w0 * prof[pl.ds(i * SUB + a0, 1), :] + w1 * prof[pl.ds(i * SUB + a1, 1), :]
            rows.append(phase[k * 8 : (k + 1) * 8] - shape)
    residual = jnp.concatenate(rows, axis=0)
    sine, cosine = sincos(residual)
    e = jnp.concatenate([cosine.astype(jnp.bfloat16), sine.astype(jnp.bfloat16)], axis=1)
    g = [jnp.dot(e, v[...], preferred_element_type=jnp.float32).astype(jnp.bfloat16) for v in (v_re, v_im)]
    g = jnp.concatenate(g, axis=0)
    h = jnp.dot(along_u[...], g, preferred_element_type=jnp.float32)
    n = h.shape[0] // 2
    h_re, h_im = h[:n], h[n:]
    spot = h_re * h_re + h_im * h_im
    sums = split_dot(over_m[...], split_dot(over_n[...], spot, False), True)
    m = sums.shape[0] // 2
    lane = lax.broadcasted_iota(jnp.int32, (m, LANES), 1)
    row = lax.broadcasted_iota(jnp.int32, (m, LANES), 0)
    top = sums[:m, LANES:] + jnp.where(lane % 2 == 1, sums[m:, :LANES], 0.0)
    ratio = top / sums[:m, :LANES]
    sub_rows = slab_rows // SUBPX
    ratio = jnp.where(lane // SUBPX == my_rec * sub_rows + row // LG_DEV, ratio, 0.0)
    own = ratio[:LG_DEV]
    for a in range(1, sub_rows):
        own = own + ratio[a * LG_DEV : (a + 1) * LG_DEV]
    width = slopes.shape[-1]
    slopes[...] = functools.reduce(jnp.add, [own[:, at : at + width] for at in range(0, LANES, width)])
    payload[...] = jnp.broadcast_to(own.astype(jnp.bfloat16).astype(jnp.float32)[None], payload.shape)


def own_rows(my_tile):
    per_row = LANES // CMD
    need = LG_DEV // per_row
    return lax.rem(my_tile * need, PT // per_row), need


def first_slopes(kept, received, flags, mirror, table, *refs):
    *c_parts, payload, slopes, c, prof = refs
    my_tile, my_rec = lax.axis_index("tile"), lax.axis_index("rec")
    for k, part in enumerate(c_parts):
        c[pl.ds((my_rec ^ k) * part.shape[0], part.shape[0]), :] = part[...]
    base, need = own_rows(my_tile)
    prof[...] = column_profiles(c[pl.ds(base, need), :], mirror)
    tiles = last_merge(kept, received, flags)
    slopes_from(tiles, prof, table, payload, slopes)


def second_slopes(kept, received, flags, c_base, updates, earlier, mirror, table, payload, slopes, c_out, c_own, prof):
    my_tile = lax.axis_index("tile")
    c_out[...] = c_base[...] + loop_gain * jnp.sum(updates[...], axis=0).reshape(c_base.shape)
    c_own[...] = c_out[pl.ds(lax.axis_index("rec") * c_own.shape[0], c_own.shape[0]), :]
    base, need = own_rows(my_tile)
    prof[...] = column_profiles(c_out[pl.ds(base, need), :], mirror)
    tiles = last_merge(kept, received, flags)
    slopes[0] = earlier[...]
    slopes_from(tiles, prof, table, payload, slopes.at[1])


def update_kernel(pattern, received, blocks, out, slopes):
    slopes[...] = jnp.sum(received[...], axis=1).reshape(slopes.shape)
    rows = []
    for i in range(blocks.shape[0]):
        total = None
        for b in range(blocks.shape[1]):
            vector = slopes[pl.ds(pattern[b, i], 1), :].astype(jnp.bfloat16)
            part = lax.dot_general(
                vector, blocks[i, b], (((1,), (1,)), ((), ())), preferred_element_type=jnp.float32
            )
            total = part if total is None else total + part
        rows.append(total)
    out[...] = jnp.broadcast_to(jnp.concatenate(rows, axis=0)[None], out.shape)


def science_kernel(places, c_first, c_second, mirror, gathered, out, store, part, ready, prof, sem):
    slab_rows = out.shape[2]
    my_tile, my_rec = lax.axis_index("tile"), lax.axis_index("rec")
    layers = places.shape[0] // (out.shape[0] * SC_DEV)
    parts = sem.shape[0] - out.shape[0]
    size = store.shape[0] // parts
    copies = []
    for i in range(parts):
        at = (i % (parts // layers) * layers + i // (parts // layers)) * size
        copies.append(pltpu.make_async_copy(gathered.at[pl.ds(at, size)], store.at[pl.ds(at, size)], sem.at[i]))
    for copy in copies:
        copy.start()
    weights = row_weights(my_rec, slab_rows)
    profile_rows = PT * SUB
    for f, c in enumerate((c_first, c_second)):
        prof[pl.ds(f * profile_rows, profile_rows)] = column_profiles(c[...], mirror)
    start = lax.rem(my_tile * SC_DEV, PT)
    twice = SC_DEV - PT
    together = 6

    def tile(f, l, k):
        return store[places[(f * layers + l) * SC_DEV + k]].astype(jnp.float32)

    for copy in copies[: parts // layers]:
        copy.wait()
    for f in range(out.shape[0]):

        def some(qs):
            results = []
            for q in qs:
                row = f * profile_rows + lax.rem(start + q, PT) * SUB
                shapes = [
                    w0 * prof[pl.ds(row + a0, 1), :] + w1 * prof[pl.ds(row + a1, 1), :]
                    for (a0, w0), (a1, w1) in weights
                ]
                shape = jnp.concatenate(shapes, axis=0)
                both = not isinstance(q, int) or q + PT < SC_DEV
                results += [(k, tile(f, 0, k) - shape) for k in (q, q + PT)[: 1 + both]]
            for k, value in results:
                part[f, k] = value

        @pl.loop(0, twice // together)
        def _(q):
            some([q * together + j for j in range(together)])

        some(range(twice // together * together, PT))
    for copy in copies[parts // layers :]:
        copy.wait()
    written = []
    for f in range(out.shape[0]):

        def rest(ks):
            results = [(k, part[f, k] + functools.reduce(jnp.add, [tile(f, l, k) for l in range(1, layers)])) for k in ks]
            for k, value in results:
                ready[f, k] = value.astype(jnp.bfloat16)

        @pl.loop(0, SC_DEV // 10)
        def _(q):
            rest([q * 10 + j for j in range(10)])

        rest(range(SC_DEV // 10 * 10, SC_DEV))
        written.append(pltpu.make_async_copy(ready.at[f], out.at[f], sem.at[parts + f]))
        written[-1].start()
    for copy in written:
        copy.wait()


def by_ring(screens, tile_owner, tile_slot, commands_init, reconstructor, pattern):
    layers, tiles_here, slab_rows, tile_px = screens.shape
    frames = tile_owner.shape[0]
    n = lax.axis_size("tile")
    rec_count = lax.axis_size("rec")
    everyone = n * rec_count
    my_tile, my_rec = lax.axis_index("tile"), lax.axis_index("rec")
    table = {k: jnp.asarray(v) for k, v in constant_tables(slab_rows).items()}
    block_rows = reconstructor.shape[0]
    f32 = jnp.float32
    limit = pltpu.CompilerParams(vmem_limit_bytes=24 << 20)

    ring = list(range(0, n, 2)) + list(range(n - 1, 0, -2))

    owners = tile_owner[..., 0]
    tables_in = [table["mirror"], table["exact"]]
    width = slab_rows // SUBPX * SUB * 2
    payload_out = [
        jax.ShapeDtypeStruct((everyone, LG_DEV, LANES), f32),
        jax.ShapeDtypeStruct((LG_DEV, width), f32),
    ]

    def exchange(payload):
        return lax.all_to_all(payload, ("tile", "rec"), split_axis=0, concat_axis=0, tiled=True)

    def updates_of(received, copies):
        received = received.reshape(n, rec_count, LG_DEV, LANES)
        return pl.pallas_call(
            update_kernel,
            out_shape=jax.ShapeDtypeStruct((copies, block_rows, LANES), f32),
            in_specs=[smem(), vmem(), vmem()],
            out_specs=vmem(),
            scratch_shapes=[pltpu.VMEM((n * LG_DEV, LANES), f32)],
            compiler_params=limit,
            cost_estimate=microseconds(2),
        )(pattern.T, received, reconstructor)

    wide = (layers, LG_DEV, slab_rows, tile_px)

    def tiles_of(*counts):
        shapes = [jax.ShapeDtypeStruct((c,) + wide, screens.dtype) for c in counts]
        return dict(out_shape=shapes, out_specs=[vmem()] * len(shapes))

    def swap(x, bit):
        return lax.ppermute(x, "tile", [(t, t ^ bit) for t in range(n)])

    def offer(frame, mine):
        (out,) = pl.pallas_call(
            functools.partial(offer_kernel, frame),
            in_specs=[smem(), vmem()],
            compiler_params=limit,
            **tiles_of(n // 2),
        )(tile_slot, mine)
        return out

    def merge(frame, bits, mine, received):
        count = n >> (bits + 1)
        outs = tiles_of(count, count)
        if count == 1:
            outs["out_shape"].append(jax.ShapeDtypeStruct((LG_DEV * layers, LANES), f32))
            outs["out_specs"].append(vmem())
        return pl.pallas_call(
            functools.partial(merge_kernel, frame, bits),
            in_specs=[smem()] * 2 + [vmem()] * 2,
            compiler_params=limit,
            **outs,
        )(owners, tile_slot, mine, received)

    def later(value, after):
        return lax.optimization_barrier((value, after))[0]

    last = n.bit_length() - 1
    c_own = commands_init.reshape(-1, LANES)
    c_parts = [c_own] + [
        lax.ppermute(c_own, "rec", [(r, r ^ k) for r in range(rec_count)]) for k in range(1, rec_count)
    ]
    wanted = offer(0, screens)
    second = offer(1, later(screens, wanted))
    arrays = tables_in + [c_own, screens]
    staged = pl.pallas_call(
        functools.partial(stage_kernel, len(arrays)),
        out_shape=[jax.ShapeDtypeStruct(x.shape, x.dtype) for x in arrays],
        in_specs=[pl.BlockSpec(memory_space=pl.ANY)] * (len(arrays) + 1),
        out_specs=[vmem()] * len(arrays),
        scratch_shapes=[pltpu.SemaphoreType.DMA((len(arrays),))],
        compiler_params=limit,
    )(*arrays, second)
    tables_in, c_parts[0] = staged[:2], staged[2]
    near = staged[3]
    kept, got = near, later(swap(wanted, 1), staged[0])
    for bits in range(1, last):
        send, kept, *flags = merge(0, bits, kept, got)
        got = swap(send, 1 << bits)
    guide = [(kept, got, *flags)]
    kept, got = near, later(swap(second, 1), send)
    for bits in range(1, last):
        send, kept, *flags = merge(1, bits, kept, got)
        got = swap(send, 1 << bits)
        if bits == 1:
            guide[0] = (later(guide[0][0], send), *guide[0][1:])
    guide.append((kept, got, *flags))

    gathered = lax.all_gather(later(screens, wanted), "tile", axis_index_groups=[ring])
    gathered = gathered.reshape(n * layers * tiles_here, slab_rows, tile_px)

    def own_items(x):
        return lax.dynamic_slice_in_dim(x, my_tile * ITEMS + LG_DEV, SC_DEV, 2)

    owner = own_items(owners)
    at = jnp.where(owner % 2 == 0, owner // 2, n - 1 - owner // 2) * layers
    places = (at + jnp.arange(layers, dtype=jnp.int32)[None, :, None]) * tiles_here + own_items(tile_slot)
    places = places.reshape(-1)

    payload, slopes_first, c0 = pl.pallas_call(
        first_slopes,
        out_shape=payload_out + [jax.ShapeDtypeStruct((rec_count * block_rows, LANES), f32)],
        in_specs=[vmem()] * (3 + rec_count + len(tables_in)),
        out_specs=[vmem()] * 3,
        scratch_shapes=[pltpu.VMEM((LG_DEV * SUB, LANES), f32)],
        compiler_params=limit,
        cost_estimate=microseconds(3),
    )(*guide[0], *tables_in, *c_parts)
    updates = updates_of(later(exchange(payload), send), everyone)
    updates = lax.all_to_all(updates, ("tile", "rec"), split_axis=0, concat_axis=0, tiled=True)
    updates = updates.reshape(n, rec_count, block_rows, LANES)

    payload, slopes, c1, mine = pl.pallas_call(
        second_slopes,
        out_shape=payload_out[:1] + [jax.ShapeDtypeStruct(r, f32) for r in ((frames, LG_DEV, width), c0.shape, c_own.shape)],
        in_specs=[vmem()] * (6 + len(tables_in)),
        out_specs=[vmem()] * 4,
        scratch_shapes=[pltpu.VMEM((LG_DEV * SUB, LANES), f32)],
        compiler_params=limit,
        cost_estimate=microseconds(3),
    )(*guide[1], c0, updates, slopes_first, *tables_in)
    updates = updates_of(exchange(payload), n)
    updates = lax.all_to_all(updates, "tile", split_axis=0, concat_axis=0, tiled=True)
    science = pl.pallas_call(
        science_kernel,
        out_shape=jax.ShapeDtypeStruct((frames, SC_DEV, slab_rows, tile_px), jnp.bfloat16),
        in_specs=[smem()] + [vmem()] * 3 + [pl.BlockSpec(memory_space=pl.ANY)],
        out_specs=pl.BlockSpec(memory_space=pl.ANY),
        scratch_shapes=[
            pltpu.VMEM((n * layers * tiles_here, slab_rows, tile_px), screens.dtype),
            pltpu.VMEM((frames, SC_DEV, slab_rows, tile_px), f32),
            pltpu.VMEM((frames, SC_DEV, slab_rows, tile_px), jnp.bfloat16),
            pltpu.VMEM((frames * PT * SUB, LANES), f32),
            pltpu.SemaphoreType.DMA((n * layers + frames,)),
        ],
        compiler_params=pltpu.CompilerParams(vmem_limit_bytes=60 << 20),
        cost_estimate=pl.CostEstimate(
            flops=8 * frames * SC_DEV * slab_rows * tile_px,
            bytes_accessed=2 * (n * layers * tiles_here + frames * SC_DEV) * slab_rows * tile_px,
            transcendentals=0,
        ),
    )(places, c0, c1, table["mirror"], gathered)
    updates = later(updates, science)
    c2 = mine + loop_gain * jnp.sum(updates, axis=0)
    return slopes, science, c2.reshape(-1)


def per_device(screens, tile_owner, *rest):
    layers, tiles_here, _, _ = screens.shape
    frames, n = tile_owner.shape[0], lax.axis_size("tile")
    capacity = max(2, 3 * ITEMS // (2 * n))
    few = tiles_here <= frames * capacity and n & (n - 1) == 0 and frames == 2 and layers == 2
    return (by_ring if few else by_request)(screens, tile_owner, *rest)


def solution(mesh):
    placed = (
        P(None, "tile", "rec", None),
        P(),
        P(),
        P("rec"),
        P("rec", "tile", None, None),
        P("rec", "tile"),
    )
    return jax.shard_map(
        per_device,
        mesh=mesh,
        in_specs=placed,
        out_specs=(P(None, "tile", "rec"), P(None, "tile", "rec", None), P("rec")),
        check_vma=False,
    )
```

```python
import functools
import math

import jax
import jax.numpy as jnp
import ml_dtypes
import numpy as np
from jax import lax
from jax.experimental import pallas as pl
from jax.experimental.pallas import tpu as pltpu
from jax.sharding import PartitionSpec as P

SUBPX = 16
SPOT = 32
SUB = 8
PT = 64
LG_DEV = 4
SC_DEV = 124
ITEMS = LG_DEV + SC_DEV
LANES = 128
CMD = SUB * SUB

loop_gain = 0.5


def influence(tile_px, sub_px, sub_count):
    pixel = jnp.arange(tile_px, dtype=jnp.float32)[:, None] + 0.5
    centre = (jnp.arange(sub_count, dtype=jnp.float32)[None, :] + 0.5) * sub_px
    return jnp.maximum(0.0, 1.0 - jnp.abs(pixel - centre) / sub_px)


def tables(spot_px, sub_px):
    freq = jnp.arange(spot_px, dtype=jnp.int32)[:, None]
    pixel = jnp.arange(sub_px, dtype=jnp.int32)[None, :]
    turns = (freq * pixel % spot_px).astype(jnp.float32) * (2.0 * math.pi / spot_px)
    return (jnp.cos(turns).astype(jnp.bfloat16), jnp.sin(turns).astype(jnp.bfloat16))


def centred(spot_px):
    index = jnp.arange(spot_px, dtype=jnp.int32)
    return ((index + spot_px // 2) % spot_px - spot_px // 2).astype(jnp.float32) / spot_px


def along_pixels(values, table):
    return jnp.einsum("iaubv,nv->iaubn", values, table, preferred_element_type=jnp.float32)


def along_rows(table, values):
    return jnp.einsum("mu,iaubn->iabmn", table, values, preferred_element_type=jnp.float32)


def spot_slopes(residual):
    item_count, row_px, col_px = residual.shape
    sub_rows = row_px // SUBPX
    sub_cols = col_px // SUBPX
    cos_t, sin_t = tables(SPOT, SUBPX)
    pieces = residual.reshape(item_count, sub_rows, SUBPX, sub_cols, SUBPX)
    real_part = jnp.cos(pieces).astype(jnp.bfloat16)
    imag_part = jnp.sin(pieces).astype(jnp.bfloat16)
    g_re = (along_pixels(real_part, cos_t) + along_pixels(imag_part, sin_t)).astype(jnp.bfloat16)
    g_im = (along_pixels(imag_part, cos_t) - along_pixels(real_part, sin_t)).astype(jnp.bfloat16)
    h_re = along_rows(cos_t, g_re) + along_rows(sin_t, g_im)
    h_im = along_rows(cos_t, g_im) - along_rows(sin_t, g_re)
    spots = h_re * h_re + h_im * h_im
    coords = centred(SPOT)
    totals = jnp.sum(spots, axis=(3, 4))
    slope_x = jnp.sum(spots * coords[None, None, None, None, :], axis=(3, 4)) / totals
    slope_y = jnp.sum(spots * coords[None, None, None, :, None], axis=(3, 4)) / totals
    return jnp.stack([slope_x, slope_y], axis=-1).reshape(item_count, sub_rows * sub_cols * 2)


def pack_tiles(screens, owners, slots, pairs, my_tile, capacity):
    packed = []
    places = jnp.arange(capacity, dtype=jnp.int32)
    for frame, layer_idx in pairs:
        owner_rows = owners[frame, layer_idx]
        slot_rows = slots[frame, layer_idx]
        mine = owner_rows == my_tile
        order = jnp.cumsum(mine.astype(jnp.int32), axis=1) - 1
        picked = mine[:, None, :] & (order[:, None, :] == places[None, :, None])
        wanted = jnp.sum(jnp.where(picked, slot_rows[:, None, :], 0), axis=2)
        packed.append(jnp.take(screens[layer_idx], wanted, axis=0))
    return jnp.stack(packed, axis=1)


def unpack_tiles(received, owners, pairs, my_tile, capacity):
    results = []
    item_count = owners.shape[3]
    later = jnp.arange(item_count, dtype=jnp.int32)
    earlier_mask = later[None, :] < later[:, None]
    for position in range(len(pairs)):
        frame, layer_idx = pairs[position]
        mine = lax.dynamic_index_in_dim(owners[frame, layer_idx], my_tile, 0, keepdims=False)
        same_owner = mine[:, None] == mine[None, :]
        order = jnp.sum((same_owner & earlier_mask).astype(jnp.int32), axis=1)
        flat_index = mine * capacity + order
        layer_tiles = received[:, position].reshape(-1, received.shape[3], received.shape[4])
        results.append(jnp.take(layer_tiles, flat_index, axis=0).astype(jnp.float32))
    return results


def by_request(screens, tile_owner, tile_slot, commands_init, reconstructor, pattern):
    layer_total, tiles_here, slab_rows, tile_px = screens.shape
    frame_total = tile_owner.shape[0]
    tile_count = lax.axis_size("tile")
    rec_count = lax.axis_size("rec")
    my_tile = lax.axis_index("tile")
    my_rec = lax.axis_index("rec")
    capacity = max(2, 3 * ITEMS // (2 * tile_count))
    owners = tile_owner[..., 0].reshape(frame_total, layer_total, tile_count, ITEMS)
    slots = tile_slot.reshape(frame_total, layer_total, tile_count, ITEMS)
    influence_all = influence(tile_px, SUBPX, SUB)
    influence_rows = lax.dynamic_slice_in_dim(influence_all, my_rec * slab_rows, slab_rows, 0)
    lgs_places = (my_tile * LG_DEV + jnp.arange(LG_DEV, dtype=jnp.int32)) % PT
    sci_places = (my_tile * SC_DEV + jnp.arange(SC_DEV, dtype=jnp.int32)) % PT
    item_places = jnp.concatenate([lgs_places, sci_places])
    state = commands_init
    slope_frames = []
    science_frames = []
    for frame in range(frame_total):
        pairs = [(frame, layer_idx) for layer_idx in range(layer_total)]
        sending = pack_tiles(screens, owners, slots, pairs, my_tile, capacity)
        received = lax.all_to_all(sending, "tile", split_axis=0, concat_axis=0, tiled=True)
        pieces = unpack_tiles(received, owners, pairs, my_tile, capacity)
        phase = functools.reduce(jnp.add, pieces)
        full_commands = lax.all_gather(state, "rec", axis=0, tiled=True)
        mirror = full_commands.reshape(PT, SUB, SUB)
        chosen = jnp.take(mirror, item_places, axis=0)
        shapes = jnp.einsum(
            "xa,iab,yb->ixy", influence_rows, chosen, influence_all, precision=lax.Precision.HIGHEST
        )
        residual = phase - shapes
        science_frames.append(residual[LG_DEV:].astype(jnp.bfloat16))
        slopes = spot_slopes(residual[:LG_DEV])
        slope_frames.append(slopes)
        slopes_b = slopes.astype(jnp.bfloat16)
        everyone = lax.all_gather(slopes_b[None], ("tile", "rec"), axis=0, tiled=True)
        everyone = everyone.reshape(tile_count, rec_count, LG_DEV, -1).transpose(0, 2, 1, 3)
        everyone = everyone.reshape(tile_count * LG_DEV, -1)
        needed = jnp.take(everyone, pattern, axis=0)
        partial_rows = jnp.einsum(
            "ibcs,ibs->ic", reconstructor, needed, preferred_element_type=jnp.float32
        ).reshape(-1)
        state = state + loop_gain * lax.psum(partial_rows, "tile")
    return (jnp.stack(slope_frames, axis=0), jnp.stack(science_frames, axis=0), state)


def microseconds(t):
    return pl.CostEstimate(flops=0, bytes_accessed=int(t * 3.69e6), transcendentals=0)


def vmem():
    return pl.BlockSpec(memory_space=pltpu.VMEM)


def smem():
    return pl.BlockSpec(memory_space=pltpu.SMEM)


def constant_tables(slab_rows):
    f32, bf16 = np.float32, ml_dtypes.bfloat16
    turns = (np.arange(SPOT)[:, None] * np.arange(SUBPX)[None, :] % SPOT).astype(f32)
    turns = turns * f32(2.0 * math.pi / SPOT)
    cos_t, sin_t = np.cos(turns).astype(bf16).astype(f32), np.sin(turns).astype(bf16).astype(f32)
    cols = LANES // SUBPX
    eye_c = np.eye(cols, dtype=f32)
    cos_v, sin_v = np.kron(eye_c, cos_t.T), np.kron(eye_c, sin_t.T)
    along_v = np.block([[cos_v, -sin_v], [sin_v, cos_v]])
    rows = LG_DEV * slab_rows // SUBPX
    eye_r = np.eye(rows, dtype=f32)
    cos_u, sin_u = np.kron(eye_r, cos_t), np.kron(eye_r, sin_t)
    along_u = np.block([[cos_u, sin_u], [-sin_u, cos_u]])
    index = np.arange(SPOT)
    coord = (((index + SPOT // 2) % SPOT) - SPOT // 2).astype(f32) / SPOT
    groups = LANES // (2 * cols)
    total_n = np.zeros((cols, SPOT, groups, cols, 2), f32)
    coord_n = np.zeros((cols, SPOT, groups, cols, 2), f32)
    for b in range(cols):
        total_n[b, :, :, b, :] = 1.0
        coord_n[b, :, :, b, 0] = coord[:, None]
    over_n = np.concatenate([t.reshape(cols * SPOT, LANES) for t in (total_n, coord_n)], axis=1)
    sub_rows = slab_rows // SUBPX
    total_m = np.zeros((sub_rows, LG_DEV, LG_DEV, sub_rows, SPOT), f32)
    coord_m = np.zeros((sub_rows, LG_DEV, LG_DEV, sub_rows, SPOT), f32)
    for a in range(sub_rows):
        for i in range(LG_DEV):
            total_m[a, i, i, a, :] = 1.0
            coord_m[a, i, i, a, :] = coord
    over_m = np.concatenate([t.reshape(rows, rows * SPOT) for t in (total_m, coord_m)], axis=0)
    pixel = np.arange(LANES, dtype=f32)[:, None] + f32(0.5)
    centre = (np.arange(SUB, dtype=f32)[None, :] + f32(0.5)) * SUBPX
    infl = np.maximum(f32(0.0), f32(1.0) - np.abs(pixel - centre) / f32(SUBPX))
    per_row = LANES // CMD
    spread = np.tile(infl.T, (per_row * SUB, 1))
    keep = np.kron(np.eye(per_row * SUB, dtype=f32), np.ones((1, SUB), f32))
    half = along_v.shape[1] // 2
    exact = [along_v[:, :half], along_v[:, half:], along_u, over_n, over_m]
    return dict(exact=np.concatenate(exact, axis=0).astype(bf16), mirror=np.concatenate([keep, spread], axis=0))


def unpack_tables(exact, slab_rows):
    e_cols = 2 * LANES
    spots = LG_DEV * slab_rows // SUBPX * SPOT
    edges = [0, e_cols, 2 * e_cols, 2 * e_cols + 2 * spots, 3 * e_cols + 2 * spots, exact.shape[0]]
    v_re, v_im, u, over_n, over_m = [exact.at[pl.ds(a, b - a)] for a, b in zip(edges, edges[1:])]
    return v_re, v_im, u, over_n, over_m


def split_dot(exact, wide, left):
    high = wide.astype(jnp.bfloat16)
    low = (wide - high.astype(jnp.float32)).astype(jnp.bfloat16)
    dot = functools.partial(jnp.dot, preferred_element_type=jnp.float32)
    if left:
        return dot(exact, high) + dot(exact, low)
    return dot(high, exact) + dot(low, exact)


def sincos(x):
    turns = jnp.floor(x * np.float32(2.0 / math.pi) + 0.5)
    r = x - turns * np.float32(1.5703125)
    r = r - turns * np.float32(4.837512969970703125e-4)
    r = r - turns * np.float32(7.54978995489188216e-8)
    z = r * r
    s = ((np.float32(-1.9515295891e-4) * z + np.float32(8.3321608736e-3)) * z - np.float32(1.6666654611e-1)) * z * r + r
    c = ((np.float32(2.443315711809948e-5) * z - np.float32(1.388731625493765e-3)) * z + np.float32(4.166664568298827e-2)) * z * z - np.float32(0.5) * z + 1.0
    q = turns.astype(jnp.int32) & 3
    odd = (q & 1) == 1
    sine = jnp.where(odd, c, s)
    cosine = jnp.where(odd, s, c)
    sine = jnp.where(q >= 2, -sine, sine)
    cosine = jnp.where((q == 1) | (q == 2), -cosine, cosine)
    return sine, cosine


def row_weights(my_rec, slab_rows):
    groups = []
    for k in range(slab_rows // 8):
        g = my_rec * (slab_rows // 8) + k
        first = (g + 1) // 2 - 1
        x = (g * 8 + lax.broadcasted_iota(jnp.int32, (8, LANES), 0)).astype(jnp.float32) + 0.5
        pair = []
        for a in (first, first + 1):
            inside = (a >= 0) & (a < SUB)
            centre = (a.astype(jnp.float32) + 0.5) * SUBPX
            w = jnp.maximum(0.0, 1.0 - jnp.abs(x - centre) / SUBPX)
            pair.append((jnp.clip(a, 0, SUB - 1), jnp.where(inside, w, 0.0)))
        groups.append(pair)
    return groups


def column_profiles(c_rows, mirror):
    at = LANES // CMD * SUB
    keep, spread = mirror[:at], mirror[at:]
    picked = [jnp.broadcast_to(c_rows[i : i + 1], keep.shape) * keep for i in range(c_rows.shape[0])]
    return jnp.dot(
        jnp.concatenate(picked, axis=0), spread, preferred_element_type=jnp.float32, precision=lax.Precision.HIGHEST
    )


def stages(n):
    return [1 << k for k in range(n.bit_length() - 1)]


def destination(me, bits, k):
    return (k << bits) | (me & ((1 << bits) - 1))


def offer_kernel(frame, slots, screens, out):
    partner = lax.axis_index("tile") ^ 1
    for k in range(out.shape[0]):
        d = destination(partner, 1, k)
        for l in range(out.shape[1]):
            for i in range(LG_DEV):
                out[k, l, i] = screens[l, slots[frame, l, d * ITEMS + i]]


def stage_kernel(count, *refs):
    inputs, outs, sem = refs[:count], refs[count + 1 : -1], refs[-1]
    copies = [pltpu.make_async_copy(x, y, sem.at[i]) for i, (x, y) in enumerate(zip(inputs, outs))]
    for copy in copies:
        copy.start()
    for copy in copies:
        copy.wait()


def merge_kernel(frame, bits, owners, slots, mine, received, send, keep, *flags):
    me = lax.axis_index("tile")
    count, layers = send.shape[0], send.shape[1]
    other = 1 << (bits - 1)
    for out, side in ((keep, me), (send, me ^ (1 << bits))):
        for k in range(count):
            d = destination(side, bits + 1, k)
            j = d >> bits
            for l in range(layers):
                for i in range(LG_DEV):
                    g = d * ITEMS + i
                    theirs = ((owners[frame, l, g] ^ me) & other) != 0
                    ours = mine[l, slots[frame, l, g]] if bits == 1 else mine[j, l, i]
                    out[k, l, i] = jnp.where(theirs, received[j, l, i], ours)
    for flag in flags:
        for l in range(layers):
            for i in range(LG_DEV):
                theirs = ((owners[frame, l, me * ITEMS + i] ^ me) >> bits) & 1
                flag[pl.ds(i * layers + l, 1), :] = jnp.full((1, LANES), theirs).astype(jnp.float32)


def last_merge(kept, received, flags):
    layers = kept.shape[1]

    def tile(i, l):
        theirs = flags[pl.ds(i * layers + l, 1), :] > 0.5
        return jnp.where(theirs, received[0, l, i].astype(jnp.float32), kept[0, l, i].astype(jnp.float32))

    return [[tile(i, l) for l in range(layers)] for i in range(LG_DEV)]


def slopes_from(tiles, prof, table, payload, slopes):
    slab_rows = tiles[0][0].shape[0]
    v_re, v_im, along_u, over_n, over_m = unpack_tables(table, slab_rows)
    my_rec = lax.axis_index("rec")
    weights = row_weights(my_rec, slab_rows)
    rows = []
    for i in range(LG_DEV):
        phase = functools.reduce(jnp.add, [tile.astype(jnp.float32) for tile in tiles[i]])
        for k, ((a0, w0), (a1, w1)) in enumerate(weights):
            shape = w0 * prof[pl.ds(i * SUB + a0, 1), :] + w1 * prof[pl.ds(i * SUB + a1, 1), :]
            rows.append(phase[k * 8 : (k + 1) * 8] - shape)
    residual = jnp.concatenate(rows, axis=0)
    sine, cosine = sincos(residual)
    e = jnp.concatenate([cosine.astype(jnp.bfloat16), sine.astype(jnp.bfloat16)], axis=1)
    g = [jnp.dot(e, v[...], preferred_element_type=jnp.float32).astype(jnp.bfloat16) for v in (v_re, v_im)]
    g = jnp.concatenate(g, axis=0)
    h = jnp.dot(along_u[...], g, preferred_element_type=jnp.float32)
    n = h.shape[0] // 2
    h_re, h_im = h[:n], h[n:]
    spot = h_re * h_re + h_im * h_im
    sums = split_dot(over_m[...], split_dot(over_n[...], spot, False), True)
    m = sums.shape[0] // 2
    lane = lax.broadcasted_iota(jnp.int32, (m, LANES), 1)
    row = lax.broadcasted_iota(jnp.int32, (m, LANES), 0)
    top = sums[:m, LANES:] + jnp.where(lane % 2 == 1, sums[m:, :LANES], 0.0)
    ratio = top / sums[:m, :LANES]
    sub_rows = slab_rows // SUBPX
    ratio = jnp.where(lane // SUBPX == my_rec * sub_rows + row // LG_DEV, ratio, 0.0)
    own = ratio[:LG_DEV]
    for a in range(1, sub_rows):
        own = own + ratio[a * LG_DEV : (a + 1) * LG_DEV]
    width = slopes.shape[-1]
    slopes[...] = functools.reduce(jnp.add, [own[:, at : at + width] for at in range(0, LANES, width)])
    payload[...] = jnp.broadcast_to(own.astype(jnp.bfloat16).astype(jnp.float32)[None], payload.shape)


def own_rows(my_tile):
    per_row = LANES // CMD
    need = LG_DEV // per_row
    return lax.rem(my_tile * need, PT // per_row), need


def first_slopes(kept, received, flags, mirror, table, *refs):
    *c_parts, payload, slopes, c, prof = refs
    my_tile, my_rec = lax.axis_index("tile"), lax.axis_index("rec")
    for k, part in enumerate(c_parts):
        c[pl.ds((my_rec ^ k) * part.shape[0], part.shape[0]), :] = part[...]
    base, need = own_rows(my_tile)
    prof[...] = column_profiles(c[pl.ds(base, need), :], mirror)
    tiles = last_merge(kept, received, flags)
    slopes_from(tiles, prof, table, payload, slopes)


def second_slopes(kept, received, flags, c_base, updates, earlier, mirror, table, payload, slopes, c_out, c_own, prof):
    my_tile = lax.axis_index("tile")
    c_out[...] = c_base[...] + loop_gain * jnp.sum(updates[...], axis=0).reshape(c_base.shape)
    c_own[...] = c_out[pl.ds(lax.axis_index("rec") * c_own.shape[0], c_own.shape[0]), :]
    base, need = own_rows(my_tile)
    prof[...] = column_profiles(c_out[pl.ds(base, need), :], mirror)
    tiles = last_merge(kept, received, flags)
    slopes[0] = earlier[...]
    slopes_from(tiles, prof, table, payload, slopes.at[1])


def update_kernel(pattern, received, blocks, out, slopes):
    slopes[...] = jnp.sum(received[...], axis=1).reshape(slopes.shape)
    rows = []
    for i in range(blocks.shape[0]):
        total = None
        for b in range(blocks.shape[1]):
            vector = slopes[pl.ds(pattern[b, i], 1), :].astype(jnp.bfloat16)
            part = lax.dot_general(
                vector, blocks[i, b], (((1,), (1,)), ((), ())), preferred_element_type=jnp.float32
            )
            total = part if total is None else total + part
        rows.append(total)
    out[...] = jnp.broadcast_to(jnp.concatenate(rows, axis=0)[None], out.shape)


def science_kernel(places, c_first, c_second, mirror, gathered, out, store, part, ready, prof, sem):
    slab_rows = out.shape[2]
    my_tile, my_rec = lax.axis_index("tile"), lax.axis_index("rec")
    layers = places.shape[0] // (out.shape[0] * SC_DEV)
    parts = sem.shape[0] - out.shape[0]
    size = store.shape[0] // parts
    copies = []
    for i in range(parts):
        at = (i % (parts // layers) * layers + i // (parts // layers)) * size
        copies.append(pltpu.make_async_copy(gathered.at[pl.ds(at, size)], store.at[pl.ds(at, size)], sem.at[i]))
    for copy in copies:
        copy.start()
    weights = row_weights(my_rec, slab_rows)
    profile_rows = PT * SUB
    for f, c in enumerate((c_first, c_second)):
        prof[pl.ds(f * profile_rows, profile_rows)] = column_profiles(c[...], mirror)
    start = lax.rem(my_tile * SC_DEV, PT)
    twice = SC_DEV - PT
    together = 6

    def tile(f, l, k):
        return store[places[(f * layers + l) * SC_DEV + k]].astype(jnp.float32)

    for copy in copies[: parts // layers]:
        copy.wait()
    for f in range(out.shape[0]):

        def some(qs):
            results = []
            for q in qs:
                row = f * profile_rows + lax.rem(start + q, PT) * SUB
                shapes = [
                    w0 * prof[pl.ds(row + a0, 1), :] + w1 * prof[pl.ds(row + a1, 1), :]
                    for (a0, w0), (a1, w1) in weights
                ]
                shape = jnp.concatenate(shapes, axis=0)
                both = not isinstance(q, int) or q + PT < SC_DEV
                results += [(k, tile(f, 0, k) - shape) for k in (q, q + PT)[: 1 + both]]
            for k, value in results:
                part[f, k] = value

        @pl.loop(0, twice // together)
        def _(q):
            some([q * together + j for j in range(together)])

        some(range(twice // together * together, PT))
    for copy in copies[parts // layers :]:
        copy.wait()
    written = []
    for f in range(out.shape[0]):

        def rest(ks):
            results = [(k, part[f, k] + functools.reduce(jnp.add, [tile(f, l, k) for l in range(1, layers)])) for k in ks]
            for k, value in results:
                ready[f, k] = value.astype(jnp.bfloat16)

        @pl.loop(0, SC_DEV // 10)
        def _(q):
            rest([q * 10 + j for j in range(10)])

        rest(range(SC_DEV // 10 * 10, SC_DEV))
        written.append(pltpu.make_async_copy(ready.at[f], out.at[f], sem.at[parts + f]))
        written[-1].start()
    for copy in written:
        copy.wait()


def by_ring(screens, tile_owner, tile_slot, commands_init, reconstructor, pattern):
    layers, tiles_here, slab_rows, tile_px = screens.shape
    frames = tile_owner.shape[0]
    n = lax.axis_size("tile")
    rec_count = lax.axis_size("rec")
    everyone = n * rec_count
    my_tile, my_rec = lax.axis_index("tile"), lax.axis_index("rec")
    table = {k: jnp.asarray(v) for k, v in constant_tables(slab_rows).items()}
    block_rows = reconstructor.shape[0]
    f32 = jnp.float32
    limit = pltpu.CompilerParams(vmem_limit_bytes=24 << 20)

    ring = list(range(0, n, 2)) + list(range(n - 1, 0, -2))

    owners = tile_owner[..., 0]
    tables_in = [table["mirror"], table["exact"]]
    width = slab_rows // SUBPX * SUB * 2
    payload_out = [
        jax.ShapeDtypeStruct((everyone, LG_DEV, LANES), f32),
        jax.ShapeDtypeStruct((LG_DEV, width), f32),
    ]

    def exchange(payload):
        return lax.all_to_all(payload, ("tile", "rec"), split_axis=0, concat_axis=0, tiled=True)

    def updates_of(received, copies):
        received = received.reshape(n, rec_count, LG_DEV, LANES)
        return pl.pallas_call(
            update_kernel,
            out_shape=jax.ShapeDtypeStruct((copies, block_rows, LANES), f32),
            in_specs=[smem(), vmem(), vmem()],
            out_specs=vmem(),
            scratch_shapes=[pltpu.VMEM((n * LG_DEV, LANES), f32)],
            compiler_params=limit,
            cost_estimate=microseconds(2),
        )(pattern.T, received, reconstructor)

    wide = (layers, LG_DEV, slab_rows, tile_px)

    def tiles_of(*counts):
        shapes = [jax.ShapeDtypeStruct((c,) + wide, screens.dtype) for c in counts]
        return dict(out_shape=shapes, out_specs=[vmem()] * len(shapes))

    def swap(x, bit):
        return lax.ppermute(x, "tile", [(t, t ^ bit) for t in range(n)])

    def offer(frame, mine):
        (out,) = pl.pallas_call(
            functools.partial(offer_kernel, frame),
            in_specs=[smem(), vmem()],
            compiler_params=limit,
            **tiles_of(n // 2),
        )(tile_slot, mine)
        return out

    def merge(frame, bits, mine, received):
        count = n >> (bits + 1)
        outs = tiles_of(count, count)
        if count == 1:
            outs["out_shape"].append(jax.ShapeDtypeStruct((LG_DEV * layers, LANES), f32))
            outs["out_specs"].append(vmem())
        return pl.pallas_call(
            functools.partial(merge_kernel, frame, bits),
            in_specs=[smem()] * 2 + [vmem()] * 2,
            compiler_params=limit,
            **outs,
        )(owners, tile_slot, mine, received)

    def later(value, after):
        return lax.optimization_barrier((value, after))[0]

    last = n.bit_length() - 1
    c_own = commands_init.reshape(-1, LANES)
    c_parts = [c_own] + [
        lax.ppermute(c_own, "rec", [(r, r ^ k) for r in range(rec_count)]) for k in range(1, rec_count)
    ]
    wanted = offer(0, screens)
    second = offer(1, later(screens, wanted))
    arrays = tables_in + [c_own, screens]
    staged = pl.pallas_call(
        functools.partial(stage_kernel, len(arrays)),
        out_shape=[jax.ShapeDtypeStruct(x.shape, x.dtype) for x in arrays],
        in_specs=[pl.BlockSpec(memory_space=pl.ANY)] * (len(arrays) + 1),
        out_specs=[vmem()] * len(arrays),
        scratch_shapes=[pltpu.SemaphoreType.DMA((len(arrays),))],
        compiler_params=limit,
    )(*arrays, second)
    tables_in, c_parts[0] = staged[:2], staged[2]
    near = staged[3]
    kept, got = near, later(swap(wanted, 1), staged[0])
    for bits in range(1, last):
        send, kept, *flags = merge(0, bits, kept, got)
        got = swap(send, 1 << bits)
    guide = [(kept, got, *flags)]
    kept, got = near, later(swap(second, 1), send)
    for bits in range(1, last):
        send, kept, *flags = merge(1, bits, kept, got)
        got = swap(send, 1 << bits)
        if bits == 1:
            guide[0] = (later(guide[0][0], send), *guide[0][1:])
    guide.append((kept, got, *flags))

    gathered = lax.all_gather(later(screens, wanted), "tile", axis_index_groups=[ring])
    gathered = gathered.reshape(n * layers * tiles_here, slab_rows, tile_px)

    def own_items(x):
        return lax.dynamic_slice_in_dim(x, my_tile * ITEMS + LG_DEV, SC_DEV, 2)

    owner = own_items(owners)
    at = jnp.where(owner % 2 == 0, owner // 2, n - 1 - owner // 2) * layers
    places = (at + jnp.arange(layers, dtype=jnp.int32)[None, :, None]) * tiles_here + own_items(tile_slot)
    places = places.reshape(-1)

    payload, slopes_first, c0 = pl.pallas_call(
        first_slopes,
        out_shape=payload_out + [jax.ShapeDtypeStruct((rec_count * block_rows, LANES), f32)],
        in_specs=[vmem()] * (3 + rec_count + len(tables_in)),
        out_specs=[vmem()] * 3,
        scratch_shapes=[pltpu.VMEM((LG_DEV * SUB, LANES), f32)],
        compiler_params=limit,
        cost_estimate=microseconds(3),
    )(*guide[0], *tables_in, *c_parts)
    updates = updates_of(later(exchange(payload), send), everyone)
    updates = lax.all_to_all(updates, ("tile", "rec"), split_axis=0, concat_axis=0, tiled=True)
    updates = updates.reshape(n, rec_count, block_rows, LANES)

    payload, slopes, c1, mine = pl.pallas_call(
        second_slopes,
        out_shape=payload_out[:1] + [jax.ShapeDtypeStruct(r, f32) for r in ((frames, LG_DEV, width), c0.shape, c_own.shape)],
        in_specs=[vmem()] * (6 + len(tables_in)),
        out_specs=[vmem()] * 4,
        scratch_shapes=[pltpu.VMEM((LG_DEV * SUB, LANES), f32)],
        compiler_params=limit,
        cost_estimate=microseconds(3),
    )(*guide[1], c0, updates, slopes_first, *tables_in)
    updates = updates_of(exchange(payload), n)
    updates = lax.all_to_all(updates, "tile", split_axis=0, concat_axis=0, tiled=True)
    science = pl.pallas_call(
        science_kernel,
        out_shape=jax.ShapeDtypeStruct((frames, SC_DEV, slab_rows, tile_px), jnp.bfloat16),
        in_specs=[smem()] + [vmem()] * 3 + [pl.BlockSpec(memory_space=pl.ANY)],
        out_specs=pl.BlockSpec(memory_space=pl.ANY),
        scratch_shapes=[
            pltpu.VMEM((n * layers * tiles_here, slab_rows, tile_px), screens.dtype),
            pltpu.VMEM((frames, SC_DEV, slab_rows, tile_px), f32),
            pltpu.VMEM((frames, SC_DEV, slab_rows, tile_px), jnp.bfloat16),
            pltpu.VMEM((frames * PT * SUB, LANES), f32),
            pltpu.SemaphoreType.DMA((n * layers + frames,)),
        ],
        compiler_params=pltpu.CompilerParams(vmem_limit_bytes=50 << 20),
        cost_estimate=pl.CostEstimate(
            flops=8 * frames * SC_DEV * slab_rows * tile_px,
            bytes_accessed=2 * (n * layers * tiles_here + frames * SC_DEV) * slab_rows * tile_px,
            transcendentals=0,
        ),
    )(places, c0, c1, table["mirror"], gathered)
    updates = later(updates, science)
    c2 = mine + loop_gain * jnp.sum(updates, axis=0)
    return slopes, science, c2.reshape(-1)


def per_device(screens, tile_owner, *rest):
    layers, tiles_here, _, _ = screens.shape
    frames, n = tile_owner.shape[0], lax.axis_size("tile")
    capacity = max(2, 3 * ITEMS // (2 * n))
    few = tiles_here <= frames * capacity and n & (n - 1) == 0 and frames == 2 and layers == 2
    return (by_ring if few else by_request)(screens, tile_owner, *rest)


def solution(mesh):
    placed = (
        P(None, "tile", "rec", None),
        P(),
        P(),
        P("rec"),
        P("rec", "tile", None, None),
        P("rec", "tile"),
    )
    return jax.shard_map(
        per_device,
        mesh=mesh,
        in_specs=placed,
        out_specs=(P(None, "tile", "rec"), P(None, "tile", "rec", None), P("rec")),
        check_vma=False,
    )
```

```python
import functools
import math

import jax
import jax.numpy as jnp
import ml_dtypes
import numpy as np
from jax import lax
from jax.experimental import pallas as pl
from jax.experimental.pallas import tpu as pltpu
from jax.sharding import PartitionSpec as P

SUBPX = 16
SPOT = 32
SUB = 8
PT = 64
LG_DEV = 4
SC_DEV = 124
ITEMS = LG_DEV + SC_DEV
LANES = 128
CMD = SUB * SUB

loop_gain = 0.5


def influence(tile_px, sub_px, sub_count):
    pixel = jnp.arange(tile_px, dtype=jnp.float32)[:, None] + 0.5
    centre = (jnp.arange(sub_count, dtype=jnp.float32)[None, :] + 0.5) * sub_px
    return jnp.maximum(0.0, 1.0 - jnp.abs(pixel - centre) / sub_px)


def tables(spot_px, sub_px):
    freq = jnp.arange(spot_px, dtype=jnp.int32)[:, None]
    pixel = jnp.arange(sub_px, dtype=jnp.int32)[None, :]
    turns = (freq * pixel % spot_px).astype(jnp.float32) * (2.0 * math.pi / spot_px)
    return (jnp.cos(turns).astype(jnp.bfloat16), jnp.sin(turns).astype(jnp.bfloat16))


def centred(spot_px):
    index = jnp.arange(spot_px, dtype=jnp.int32)
    return ((index + spot_px // 2) % spot_px - spot_px // 2).astype(jnp.float32) / spot_px


def along_pixels(values, table):
    return jnp.einsum("iaubv,nv->iaubn", values, table, preferred_element_type=jnp.float32)


def along_rows(table, values):
    return jnp.einsum("mu,iaubn->iabmn", table, values, preferred_element_type=jnp.float32)


def spot_slopes(residual):
    item_count, row_px, col_px = residual.shape
    sub_rows = row_px // SUBPX
    sub_cols = col_px // SUBPX
    cos_t, sin_t = tables(SPOT, SUBPX)
    pieces = residual.reshape(item_count, sub_rows, SUBPX, sub_cols, SUBPX)
    real_part = jnp.cos(pieces).astype(jnp.bfloat16)
    imag_part = jnp.sin(pieces).astype(jnp.bfloat16)
    g_re = (along_pixels(real_part, cos_t) + along_pixels(imag_part, sin_t)).astype(jnp.bfloat16)
    g_im = (along_pixels(imag_part, cos_t) - along_pixels(real_part, sin_t)).astype(jnp.bfloat16)
    h_re = along_rows(cos_t, g_re) + along_rows(sin_t, g_im)
    h_im = along_rows(cos_t, g_im) - along_rows(sin_t, g_re)
    spots = h_re * h_re + h_im * h_im
    coords = centred(SPOT)
    totals = jnp.sum(spots, axis=(3, 4))
    slope_x = jnp.sum(spots * coords[None, None, None, None, :], axis=(3, 4)) / totals
    slope_y = jnp.sum(spots * coords[None, None, None, :, None], axis=(3, 4)) / totals
    return jnp.stack([slope_x, slope_y], axis=-1).reshape(item_count, sub_rows * sub_cols * 2)


def pack_tiles(screens, owners, slots, pairs, my_tile, capacity):
    packed = []
    places = jnp.arange(capacity, dtype=jnp.int32)
    for frame, layer_idx in pairs:
        owner_rows = owners[frame, layer_idx]
        slot_rows = slots[frame, layer_idx]
        mine = owner_rows == my_tile
        order = jnp.cumsum(mine.astype(jnp.int32), axis=1) - 1
        picked = mine[:, None, :] & (order[:, None, :] == places[None, :, None])
        wanted = jnp.sum(jnp.where(picked, slot_rows[:, None, :], 0), axis=2)
        packed.append(jnp.take(screens[layer_idx], wanted, axis=0))
    return jnp.stack(packed, axis=1)


def unpack_tiles(received, owners, pairs, my_tile, capacity):
    results = []
    item_count = owners.shape[3]
    later = jnp.arange(item_count, dtype=jnp.int32)
    earlier_mask = later[None, :] < later[:, None]
    for position in range(len(pairs)):
        frame, layer_idx = pairs[position]
        mine = lax.dynamic_index_in_dim(owners[frame, layer_idx], my_tile, 0, keepdims=False)
        same_owner = mine[:, None] == mine[None, :]
        order = jnp.sum((same_owner & earlier_mask).astype(jnp.int32), axis=1)
        flat_index = mine * capacity + order
        layer_tiles = received[:, position].reshape(-1, received.shape[3], received.shape[4])
        results.append(jnp.take(layer_tiles, flat_index, axis=0).astype(jnp.float32))
    return results


def by_request(screens, tile_owner, tile_slot, commands_init, reconstructor, pattern):
    layer_total, tiles_here, slab_rows, tile_px = screens.shape
    frame_total = tile_owner.shape[0]
    tile_count = lax.axis_size("tile")
    rec_count = lax.axis_size("rec")
    my_tile = lax.axis_index("tile")
    my_rec = lax.axis_index("rec")
    capacity = max(2, 3 * ITEMS // (2 * tile_count))
    owners = tile_owner[..., 0].reshape(frame_total, layer_total, tile_count, ITEMS)
    slots = tile_slot.reshape(frame_total, layer_total, tile_count, ITEMS)
    influence_all = influence(tile_px, SUBPX, SUB)
    influence_rows = lax.dynamic_slice_in_dim(influence_all, my_rec * slab_rows, slab_rows, 0)
    lgs_places = (my_tile * LG_DEV + jnp.arange(LG_DEV, dtype=jnp.int32)) % PT
    sci_places = (my_tile * SC_DEV + jnp.arange(SC_DEV, dtype=jnp.int32)) % PT
    item_places = jnp.concatenate([lgs_places, sci_places])
    state = commands_init
    slope_frames = []
    science_frames = []
    for frame in range(frame_total):
        pairs = [(frame, layer_idx) for layer_idx in range(layer_total)]
        sending = pack_tiles(screens, owners, slots, pairs, my_tile, capacity)
        received = lax.all_to_all(sending, "tile", split_axis=0, concat_axis=0, tiled=True)
        pieces = unpack_tiles(received, owners, pairs, my_tile, capacity)
        phase = functools.reduce(jnp.add, pieces)
        full_commands = lax.all_gather(state, "rec", axis=0, tiled=True)
        mirror = full_commands.reshape(PT, SUB, SUB)
        chosen = jnp.take(mirror, item_places, axis=0)
        shapes = jnp.einsum(
            "xa,iab,yb->ixy", influence_rows, chosen, influence_all, precision=lax.Precision.HIGHEST
        )
        residual = phase - shapes
        science_frames.append(residual[LG_DEV:].astype(jnp.bfloat16))
        slopes = spot_slopes(residual[:LG_DEV])
        slope_frames.append(slopes)
        slopes_b = slopes.astype(jnp.bfloat16)
        everyone = lax.all_gather(slopes_b[None], ("tile", "rec"), axis=0, tiled=True)
        everyone = everyone.reshape(tile_count, rec_count, LG_DEV, -1).transpose(0, 2, 1, 3)
        everyone = everyone.reshape(tile_count * LG_DEV, -1)
        needed = jnp.take(everyone, pattern, axis=0)
        partial_rows = jnp.einsum(
            "ibcs,ibs->ic", reconstructor, needed, preferred_element_type=jnp.float32
        ).reshape(-1)
        state = state + loop_gain * lax.psum(partial_rows, "tile")
    return (jnp.stack(slope_frames, axis=0), jnp.stack(science_frames, axis=0), state)


def microseconds(t):
    return pl.CostEstimate(flops=0, bytes_accessed=int(t * 3.69e6), transcendentals=0)


def vmem():
    return pl.BlockSpec(memory_space=pltpu.VMEM)


def smem():
    return pl.BlockSpec(memory_space=pltpu.SMEM)


def constant_tables(slab_rows):
    f32, bf16 = np.float32, ml_dtypes.bfloat16
    turns = (np.arange(SPOT)[:, None] * np.arange(SUBPX)[None, :] % SPOT).astype(f32)
    turns = turns * f32(2.0 * math.pi / SPOT)
    cos_t, sin_t = np.cos(turns).astype(bf16).astype(f32), np.sin(turns).astype(bf16).astype(f32)
    cols = LANES // SUBPX
    eye_c = np.eye(cols, dtype=f32)
    cos_v, sin_v = np.kron(eye_c, cos_t.T), np.kron(eye_c, sin_t.T)
    along_v = np.block([[cos_v, -sin_v], [sin_v, cos_v]])
    rows = LG_DEV * slab_rows // SUBPX
    eye_r = np.eye(rows, dtype=f32)
    cos_u, sin_u = np.kron(eye_r, cos_t), np.kron(eye_r, sin_t)
    along_u = np.block([[cos_u, sin_u], [-sin_u, cos_u]])
    index = np.arange(SPOT)
    coord = (((index + SPOT // 2) % SPOT) - SPOT // 2).astype(f32) / SPOT
    groups = LANES // (2 * cols)
    total_n = np.zeros((cols, SPOT, groups, cols, 2), f32)
    coord_n = np.zeros((cols, SPOT, groups, cols, 2), f32)
    for b in range(cols):
        total_n[b, :, :, b, :] = 1.0
        coord_n[b, :, :, b, 0] = coord[:, None]
    over_n = np.concatenate([t.reshape(cols * SPOT, LANES) for t in (total_n, coord_n)], axis=1)
    sub_rows = slab_rows // SUBPX
    total_m = np.zeros((sub_rows, LG_DEV, LG_DEV, sub_rows, SPOT), f32)
    coord_m = np.zeros((sub_rows, LG_DEV, LG_DEV, sub_rows, SPOT), f32)
    for a in range(sub_rows):
        for i in range(LG_DEV):
            total_m[a, i, i, a, :] = 1.0
            coord_m[a, i, i, a, :] = coord
    over_m = np.concatenate([t.reshape(rows, rows * SPOT) for t in (total_m, coord_m)], axis=0)
    pixel = np.arange(LANES, dtype=f32)[:, None] + f32(0.5)
    centre = (np.arange(SUB, dtype=f32)[None, :] + f32(0.5)) * SUBPX
    infl = np.maximum(f32(0.0), f32(1.0) - np.abs(pixel - centre) / f32(SUBPX))
    per_row = LANES // CMD
    spread = np.tile(infl.T, (per_row * SUB, 1))
    keep = np.kron(np.eye(per_row * SUB, dtype=f32), np.ones((1, SUB), f32))
    half = along_v.shape[1] // 2
    exact = [along_v[:, :half], along_v[:, half:], along_u, over_n, over_m]
    return dict(exact=np.concatenate(exact, axis=0).astype(bf16), mirror=np.concatenate([keep, spread], axis=0))


def unpack_tables(exact, slab_rows):
    e_cols = 2 * LANES
    spots = LG_DEV * slab_rows // SUBPX * SPOT
    edges = [0, e_cols, 2 * e_cols, 2 * e_cols + 2 * spots, 3 * e_cols + 2 * spots, exact.shape[0]]
    v_re, v_im, u, over_n, over_m = [exact.at[pl.ds(a, b - a)] for a, b in zip(edges, edges[1:])]
    return v_re, v_im, u, over_n, over_m


def split_dot(exact, wide, left):
    high = wide.astype(jnp.bfloat16)
    low = (wide - high.astype(jnp.float32)).astype(jnp.bfloat16)
    dot = functools.partial(jnp.dot, preferred_element_type=jnp.float32)
    if left:
        return dot(exact, high) + dot(exact, low)
    return dot(high, exact) + dot(low, exact)


def sincos(x):
    turns = jnp.floor(x * np.float32(2.0 / math.pi) + 0.5)
    r = x - turns * np.float32(1.5703125)
    r = r - turns * np.float32(4.837512969970703125e-4)
    r = r - turns * np.float32(7.54978995489188216e-8)
    z = r * r
    s = ((np.float32(-1.9515295891e-4) * z + np.float32(8.3321608736e-3)) * z - np.float32(1.6666654611e-1)) * z * r + r
    c = ((np.float32(2.443315711809948e-5) * z - np.float32(1.388731625493765e-3)) * z + np.float32(4.166664568298827e-2)) * z * z - np.float32(0.5) * z + 1.0
    q = turns.astype(jnp.int32) & 3
    odd = (q & 1) == 1
    sine = jnp.where(odd, c, s)
    cosine = jnp.where(odd, s, c)
    sine = jnp.where(q >= 2, -sine, sine)
    cosine = jnp.where((q == 1) | (q == 2), -cosine, cosine)
    return sine, cosine


def row_weights(my_rec, slab_rows):
    groups = []
    for k in range(slab_rows // 8):
        g = my_rec * (slab_rows // 8) + k
        first = (g + 1) // 2 - 1
        x = (g * 8 + lax.broadcasted_iota(jnp.int32, (8, LANES), 0)).astype(jnp.float32) + 0.5
        pair = []
        for a in (first, first + 1):
            inside = (a >= 0) & (a < SUB)
            centre = (a.astype(jnp.float32) + 0.5) * SUBPX
            w = jnp.maximum(0.0, 1.0 - jnp.abs(x - centre) / SUBPX)
            pair.append((jnp.clip(a, 0, SUB - 1), jnp.where(inside, w, 0.0)))
        groups.append(pair)
    return groups


def column_profiles(c_rows, mirror):
    at = LANES // CMD * SUB
    keep, spread = mirror[:at], mirror[at:]
    picked = [jnp.broadcast_to(c_rows[i : i + 1], keep.shape) * keep for i in range(c_rows.shape[0])]
    return jnp.dot(
        jnp.concatenate(picked, axis=0), spread, preferred_element_type=jnp.float32, precision=lax.Precision.HIGHEST
    )


def stages(n):
    return [1 << k for k in range(n.bit_length() - 1)]


def destination(me, bits, k):
    return (k << bits) | (me & ((1 << bits) - 1))


def offer_kernel(frame, slots, screens, out):
    partner = lax.axis_index("tile") ^ 1
    for k in range(out.shape[0]):
        d = destination(partner, 1, k)
        for l in range(out.shape[1]):
            for i in range(LG_DEV):
                out[k, l, i] = screens[l, slots[frame, l, d * ITEMS + i]]


def stage_kernel(count, *refs):
    inputs, outs, sem = refs[:count], refs[count + 1 : -1], refs[-1]
    copies = [pltpu.make_async_copy(x, y, sem.at[i]) for i, (x, y) in enumerate(zip(inputs, outs))]
    for copy in copies:
        copy.start()
    for copy in copies:
        copy.wait()


def merge_kernel(frame, bits, owners, slots, mine, received, send, keep, *flags):
    me = lax.axis_index("tile")
    count, layers = send.shape[0], send.shape[1]
    other = 1 << (bits - 1)
    for out, side in ((keep, me), (send, me ^ (1 << bits))):
        for k in range(count):
            d = destination(side, bits + 1, k)
            j = d >> bits
            for l in range(layers):
                for i in range(LG_DEV):
                    g = d * ITEMS + i
                    theirs = ((owners[frame, l, g] ^ me) & other) != 0
                    ours = mine[l, slots[frame, l, g]] if bits == 1 else mine[j, l, i]
                    out[k, l, i] = jnp.where(theirs, received[j, l, i], ours)
    for flag in flags:
        for l in range(layers):
            for i in range(LG_DEV):
                theirs = ((owners[frame, l, me * ITEMS + i] ^ me) >> bits) & 1
                flag[pl.ds(i * layers + l, 1), :] = jnp.full((1, LANES), theirs).astype(jnp.float32)


def last_merge(kept, received, flags):
    layers = kept.shape[1]

    def tile(i, l):
        theirs = flags[pl.ds(i * layers + l, 1), :] > 0.5
        return jnp.where(theirs, received[0, l, i].astype(jnp.float32), kept[0, l, i].astype(jnp.float32))

    return [[tile(i, l) for l in range(layers)] for i in range(LG_DEV)]


def slopes_from(tiles, prof, table, payload, slopes):
    slab_rows = tiles[0][0].shape[0]
    v_re, v_im, along_u, over_n, over_m = unpack_tables(table, slab_rows)
    my_rec = lax.axis_index("rec")
    weights = row_weights(my_rec, slab_rows)
    rows = []
    for i in range(LG_DEV):
        phase = functools.reduce(jnp.add, [tile.astype(jnp.float32) for tile in tiles[i]])
        for k, ((a0, w0), (a1, w1)) in enumerate(weights):
            shape = w0 * prof[pl.ds(i * SUB + a0, 1), :] + w1 * prof[pl.ds(i * SUB + a1, 1), :]
            rows.append(phase[k * 8 : (k + 1) * 8] - shape)
    residual = jnp.concatenate(rows, axis=0)
    sine, cosine = sincos(residual)
    e = jnp.concatenate([cosine.astype(jnp.bfloat16), sine.astype(jnp.bfloat16)], axis=1)
    g = [jnp.dot(e, v[...], preferred_element_type=jnp.float32).astype(jnp.bfloat16) for v in (v_re, v_im)]
    g = jnp.concatenate(g, axis=0)
    h = jnp.dot(along_u[...], g, preferred_element_type=jnp.float32)
    n = h.shape[0] // 2
    h_re, h_im = h[:n], h[n:]
    spot = h_re * h_re + h_im * h_im
    sums = split_dot(over_m[...], split_dot(over_n[...], spot, False), True)
    m = sums.shape[0] // 2
    lane = lax.broadcasted_iota(jnp.int32, (m, LANES), 1)
    row = lax.broadcasted_iota(jnp.int32, (m, LANES), 0)
    top = sums[:m, LANES:] + jnp.where(lane % 2 == 1, sums[m:, :LANES], 0.0)
    ratio = top / sums[:m, :LANES]
    sub_rows = slab_rows // SUBPX
    ratio = jnp.where(lane // SUBPX == my_rec * sub_rows + row // LG_DEV, ratio, 0.0)
    own = ratio[:LG_DEV]
    for a in range(1, sub_rows):
        own = own + ratio[a * LG_DEV : (a + 1) * LG_DEV]
    width = slopes.shape[-1]
    slopes[...] = functools.reduce(jnp.add, [own[:, at : at + width] for at in range(0, LANES, width)])
    payload[...] = jnp.broadcast_to(own.astype(jnp.bfloat16).astype(jnp.float32)[None], payload.shape)


def own_rows(my_tile):
    per_row = LANES // CMD
    need = LG_DEV // per_row
    return lax.rem(my_tile * need, PT // per_row), need


def first_slopes(kept, received, flags, mirror, table, *refs):
    *c_parts, payload, slopes, c, prof = refs
    my_tile, my_rec = lax.axis_index("tile"), lax.axis_index("rec")
    for k, part in enumerate(c_parts):
        c[pl.ds((my_rec ^ k) * part.shape[0], part.shape[0]), :] = part[...]
    base, need = own_rows(my_tile)
    prof[...] = column_profiles(c[pl.ds(base, need), :], mirror)
    tiles = last_merge(kept, received, flags)
    slopes_from(tiles, prof, table, payload, slopes)


def second_slopes(kept, received, flags, c_base, updates, earlier, mirror, table, payload, slopes, c_out, c_own, prof):
    my_tile = lax.axis_index("tile")
    c_out[...] = c_base[...] + loop_gain * jnp.sum(updates[...], axis=0).reshape(c_base.shape)
    c_own[...] = c_out[pl.ds(lax.axis_index("rec") * c_own.shape[0], c_own.shape[0]), :]
    base, need = own_rows(my_tile)
    prof[...] = column_profiles(c_out[pl.ds(base, need), :], mirror)
    tiles = last_merge(kept, received, flags)
    slopes[0] = earlier[...]
    slopes_from(tiles, prof, table, payload, slopes.at[1])


def update_kernel(pattern, received, blocks, out, slopes):
    slopes[...] = jnp.sum(received[...], axis=1).reshape(slopes.shape)
    rows = []
    for i in range(blocks.shape[0]):
        total = None
        for b in range(blocks.shape[1]):
            vector = slopes[pl.ds(pattern[b, i], 1), :].astype(jnp.bfloat16)
            part = lax.dot_general(
                vector, blocks[i, b], (((1,), (1,)), ((), ())), preferred_element_type=jnp.float32
            )
            total = part if total is None else total + part
        rows.append(total)
    out[...] = jnp.broadcast_to(jnp.concatenate(rows, axis=0)[None], out.shape)


def science_kernel(places, c_first, c_second, mirror, gathered, out, store, part, ready, prof, sem):
    slab_rows = out.shape[2]
    my_tile, my_rec = lax.axis_index("tile"), lax.axis_index("rec")
    layers = places.shape[0] // (out.shape[0] * SC_DEV)
    parts = sem.shape[0] - out.shape[0]
    size = store.shape[0] // parts
    copies = []
    for i in range(parts):
        at = (i % (parts // layers) * layers + i // (parts // layers)) * size
        copies.append(pltpu.make_async_copy(gathered.at[pl.ds(at, size)], store.at[pl.ds(at, size)], sem.at[i]))
    for copy in copies:
        copy.start()
    weights = row_weights(my_rec, slab_rows)
    profile_rows = PT * SUB
    for f, c in enumerate((c_first, c_second)):
        prof[pl.ds(f * profile_rows, profile_rows)] = column_profiles(c[...], mirror)
    start = lax.rem(my_tile * SC_DEV, PT)
    twice = SC_DEV - PT
    together = 10

    def tile(f, l, k):
        return store[places[(f * layers + l) * SC_DEV + k]].astype(jnp.float32)

    for copy in copies[: parts // layers]:
        copy.wait()
    for f in range(out.shape[0]):

        def some(qs):
            results = []
            for q in qs:
                row = f * profile_rows + lax.rem(start + q, PT) * SUB
                shapes = [
                    w0 * prof[pl.ds(row + a0, 1), :] + w1 * prof[pl.ds(row + a1, 1), :]
                    for (a0, w0), (a1, w1) in weights
                ]
                shape = jnp.concatenate(shapes, axis=0)
                both = not isinstance(q, int) or q + PT < SC_DEV
                results += [(k, tile(f, 0, k) - shape) for k in (q, q + PT)[: 1 + both]]
            for k, value in results:
                part[f, k] = value

        @pl.loop(0, twice // together)
        def _(q):
            some([q * together + j for j in range(together)])

        some(range(twice // together * together, PT))
    for copy in copies[parts // layers :]:
        copy.wait()
    written = []
    for f in range(out.shape[0]):

        def rest(ks):
            results = [(k, part[f, k] + functools.reduce(jnp.add, [tile(f, l, k) for l in range(1, layers)])) for k in ks]
            for k, value in results:
                ready[f, k] = value.astype(jnp.bfloat16)

        @pl.loop(0, SC_DEV // 10)
        def _(q):
            rest([q * 10 + j for j in range(10)])

        rest(range(SC_DEV // 10 * 10, SC_DEV))
        written.append(pltpu.make_async_copy(ready.at[f], out.at[f], sem.at[parts + f]))
        written[-1].start()
    for copy in written:
        copy.wait()


def by_ring(screens, tile_owner, tile_slot, commands_init, reconstructor, pattern):
    layers, tiles_here, slab_rows, tile_px = screens.shape
    frames = tile_owner.shape[0]
    n = lax.axis_size("tile")
    rec_count = lax.axis_size("rec")
    everyone = n * rec_count
    my_tile, my_rec = lax.axis_index("tile"), lax.axis_index("rec")
    table = {k: jnp.asarray(v) for k, v in constant_tables(slab_rows).items()}
    block_rows = reconstructor.shape[0]
    f32 = jnp.float32
    limit = pltpu.CompilerParams(vmem_limit_bytes=24 << 20)

    ring = list(range(0, n, 2)) + list(range(n - 1, 0, -2))

    owners = tile_owner[..., 0]
    tables_in = [table["mirror"], table["exact"]]
    width = slab_rows // SUBPX * SUB * 2
    payload_out = [
        jax.ShapeDtypeStruct((everyone, LG_DEV, LANES), f32),
        jax.ShapeDtypeStruct((LG_DEV, width), f32),
    ]

    def exchange(payload):
        return lax.all_to_all(payload, ("tile", "rec"), split_axis=0, concat_axis=0, tiled=True)

    def updates_of(received, copies):
        received = received.reshape(n, rec_count, LG_DEV, LANES)
        return pl.pallas_call(
            update_kernel,
            out_shape=jax.ShapeDtypeStruct((copies, block_rows, LANES), f32),
            in_specs=[smem(), vmem(), vmem()],
            out_specs=vmem(),
            scratch_shapes=[pltpu.VMEM((n * LG_DEV, LANES), f32)],
            compiler_params=limit,
            cost_estimate=microseconds(2),
        )(pattern.T, received, reconstructor)

    wide = (layers, LG_DEV, slab_rows, tile_px)

    def tiles_of(*counts):
        shapes = [jax.ShapeDtypeStruct((c,) + wide, screens.dtype) for c in counts]
        return dict(out_shape=shapes, out_specs=[vmem()] * len(shapes))

    def swap(x, bit):
        return lax.ppermute(x, "tile", [(t, t ^ bit) for t in range(n)])

    def offer(frame, mine):
        (out,) = pl.pallas_call(
            functools.partial(offer_kernel, frame),
            in_specs=[smem(), vmem()],
            compiler_params=limit,
            **tiles_of(n // 2),
        )(tile_slot, mine)
        return out

    def merge(frame, bits, mine, received):
        count = n >> (bits + 1)
        outs = tiles_of(count, count)
        if count == 1:
            outs["out_shape"].append(jax.ShapeDtypeStruct((LG_DEV * layers, LANES), f32))
            outs["out_specs"].append(vmem())
        return pl.pallas_call(
            functools.partial(merge_kernel, frame, bits),
            in_specs=[smem()] * 2 + [vmem()] * 2,
            compiler_params=limit,
            **outs,
        )(owners, tile_slot, mine, received)

    def later(value, after):
        return lax.optimization_barrier((value, after))[0]

    last = n.bit_length() - 1
    c_own = commands_init.reshape(-1, LANES)
    c_parts = [c_own] + [
        lax.ppermute(c_own, "rec", [(r, r ^ k) for r in range(rec_count)]) for k in range(1, rec_count)
    ]
    wanted = offer(0, screens)
    second = offer(1, later(screens, wanted))
    arrays = tables_in + [c_own, screens]
    staged = pl.pallas_call(
        functools.partial(stage_kernel, len(arrays)),
        out_shape=[jax.ShapeDtypeStruct(x.shape, x.dtype) for x in arrays],
        in_specs=[pl.BlockSpec(memory_space=pl.ANY)] * (len(arrays) + 1),
        out_specs=[vmem()] * len(arrays),
        scratch_shapes=[pltpu.SemaphoreType.DMA((len(arrays),))],
        compiler_params=limit,
    )(*arrays, second)
    tables_in, c_parts[0] = staged[:2], staged[2]
    near = staged[3]
    kept, got = near, later(swap(wanted, 1), staged[0])
    for bits in range(1, last):
        send, kept, *flags = merge(0, bits, kept, got)
        got = swap(send, 1 << bits)
    guide = [(kept, got, *flags)]
    kept, got = near, later(swap(second, 1), send)
    for bits in range(1, last):
        send, kept, *flags = merge(1, bits, kept, got)
        got = swap(send, 1 << bits)
        if bits == 1:
            guide[0] = (later(guide[0][0], send), *guide[0][1:])
    guide.append((kept, got, *flags))

    gathered = lax.all_gather(later(screens, wanted), "tile", axis_index_groups=[ring])
    gathered = gathered.reshape(n * layers * tiles_here, slab_rows, tile_px)

    def own_items(x):
        return lax.dynamic_slice_in_dim(x, my_tile * ITEMS + LG_DEV, SC_DEV, 2)

    owner = own_items(owners)
    at = jnp.where(owner % 2 == 0, owner // 2, n - 1 - owner // 2) * layers
    places = (at + jnp.arange(layers, dtype=jnp.int32)[None, :, None]) * tiles_here + own_items(tile_slot)
    places = places.reshape(-1)

    payload, slopes_first, c0 = pl.pallas_call(
        first_slopes,
        out_shape=payload_out + [jax.ShapeDtypeStruct((rec_count * block_rows, LANES), f32)],
        in_specs=[vmem()] * (3 + rec_count + len(tables_in)),
        out_specs=[vmem()] * 3,
        scratch_shapes=[pltpu.VMEM((LG_DEV * SUB, LANES), f32)],
        compiler_params=limit,
        cost_estimate=microseconds(3),
    )(*guide[0], *tables_in, *c_parts)
    updates = updates_of(later(exchange(payload), send), everyone)
    updates = lax.all_to_all(updates, ("tile", "rec"), split_axis=0, concat_axis=0, tiled=True)
    updates = updates.reshape(n, rec_count, block_rows, LANES)

    payload, slopes, c1, mine = pl.pallas_call(
        second_slopes,
        out_shape=payload_out[:1] + [jax.ShapeDtypeStruct(r, f32) for r in ((frames, LG_DEV, width), c0.shape, c_own.shape)],
        in_specs=[vmem()] * (6 + len(tables_in)),
        out_specs=[vmem()] * 4,
        scratch_shapes=[pltpu.VMEM((LG_DEV * SUB, LANES), f32)],
        compiler_params=limit,
        cost_estimate=microseconds(3),
    )(*guide[1], c0, updates, slopes_first, *tables_in)
    updates = updates_of(exchange(payload), n)
    updates = lax.all_to_all(updates, "tile", split_axis=0, concat_axis=0, tiled=True)
    science = pl.pallas_call(
        science_kernel,
        out_shape=jax.ShapeDtypeStruct((frames, SC_DEV, slab_rows, tile_px), jnp.bfloat16),
        in_specs=[smem()] + [vmem()] * 3 + [pl.BlockSpec(memory_space=pl.ANY)],
        out_specs=pl.BlockSpec(memory_space=pl.ANY),
        scratch_shapes=[
            pltpu.VMEM((n * layers * tiles_here, slab_rows, tile_px), screens.dtype),
            pltpu.VMEM((frames, SC_DEV, slab_rows, tile_px), f32),
            pltpu.VMEM((frames, SC_DEV, slab_rows, tile_px), jnp.bfloat16),
            pltpu.VMEM((frames * PT * SUB, LANES), f32),
            pltpu.SemaphoreType.DMA((n * layers + frames,)),
        ],
        compiler_params=pltpu.CompilerParams(vmem_limit_bytes=50 << 20),
        cost_estimate=pl.CostEstimate(
            flops=8 * frames * SC_DEV * slab_rows * tile_px,
            bytes_accessed=2 * (n * layers * tiles_here + frames * SC_DEV) * slab_rows * tile_px,
            transcendentals=0,
        ),
    )(places, c0, c1, table["mirror"], gathered)
    updates = later(updates, science)
    c2 = mine + loop_gain * jnp.sum(updates, axis=0)
    return slopes, science, c2.reshape(-1)


def per_device(screens, tile_owner, *rest):
    layers, tiles_here, _, _ = screens.shape
    frames, n = tile_owner.shape[0], lax.axis_size("tile")
    capacity = max(2, 3 * ITEMS // (2 * n))
    few = tiles_here <= frames * capacity and n & (n - 1) == 0 and frames == 2 and layers == 2
    return (by_ring if few else by_request)(screens, tile_owner, *rest)


def solution(mesh):
    placed = (
        P(None, "tile", "rec", None),
        P(),
        P(),
        P("rec"),
        P("rec", "tile", None, None),
        P("rec", "tile"),
    )
    return jax.shard_map(
        per_device,
        mesh=mesh,
        in_specs=placed,
        out_specs=(P(None, "tile", "rec"), P(None, "tile", "rec", None), P("rec")),
        check_vma=False,
    )
```
